1024 devices in a mesh: lat: 32 (over x, z_lo), lon: 32 (over z_hi, y, core).
Axes of the slice: x: 4, y: 4, z: 32 (z_hi: 4, z_lo: 8; z = z_hi * 8 + z_lo), core: 2. Of those that a mesh axis runs over, the one named last changes fastest.
Arguments:
- u_vel: float32 [4, 1024, 4096], P(None, 'lat', 'lon'), may hold values from -3 to 3
- v_vel: float32 [4, 1024, 4096], P(None, 'lat', 'lon'), may hold values from -3 to 3
- temp: float32 [4, 1024, 4096], P(None, 'lat', 'lon'), may hold values from -6 to 6
- salt: float32 [4, 1024, 4096], P(None, 'lat', 'lon'), may hold values from -6 to 6
- eta: float32 [1024, 4096], P('lat', 'lon'), may hold values from -5 to 5
- wet_levels: int32 [3, 1024, 4096], P(None, 'lat', 'lon'), may hold values from 0 to 4, as said below
Outputs:
- u_new: float32 [4, 1024, 4096], P(None, 'lat', 'lon')
- v_new: float32 [4, 1024, 4096], P(None, 'lat', 'lon')
- temp_new: float32 [4, 1024, 4096], P(None, 'lat', 'lon')
- salt_new: float32 [4, 1024, 4096], P(None, 'lat', 'lon')
- eta_new: float32 [1024, 4096], P('lat', 'lon')
The draws below stay inside these ranges and needn't reach their ends.
Inputs may be any that keep to these rules, and one draw needn't show every extreme that they name: `wet_levels`: entry 0 of a column is its number of wet levels, 0 on land; entry 1 is the smaller of entry 0 of the column and of its eastern neighbour (periodic in longitude); entry 2 the smaller of entry 0 of the column and of its northern neighbour, 0 on the last row.
All inputs are finite; a program needn't handle non-finite values.
Results may differ from the reference program's by a relative error of at most 0.0003.
Values sent between devices are 32-bit elements; how exact they have to be, the bound alone decides.
A program may use at most 32 MiB of HBM per device.

```python
import jax
import jax.numpy as jnp
from jax import lax

LEVELS = 4
SUB = 8
NX = 4096
NY = 1024


def draw_wet_levels(key, part):
    ocean_key = jax.random.fold_in(key, 11)
    floor_key = jax.random.fold_in(key, 23)
    ocean_cell = jax.random.randint(ocean_key, (NY, NX), 0, 5) > 0
    bottom = jax.random.randint(floor_key, (NY, NX), 1, LEVELS + 1)
    column = jnp.where(ocean_cell, bottom, 0).astype(jnp.int32)
    eastern = jnp.minimum(column, jnp.roll(column, -1, 1))
    northern = jnp.minimum(column, jnp.concatenate([column[1:], jnp.zeros_like(column[:1])], 0))
    return jnp.stack([column, eastern, northern]).astype(jnp.int32)


def block_levels(key, shape, cuts, smallest, largest):
    def one(dim, blocks):
        draws = jax.random.uniform(jax.random.fold_in(jax.random.fold_in(key, 6), dim), (blocks,), jnp.float32, smallest / len(cuts), largest / len(cuts))
        return jnp.repeat(jnp.exp(draws), shape[dim] // blocks).reshape((-1,) + (1,) * (len(shape) - dim - 1))

    loudness = one(*cuts[0])
    for cut in cuts[1:]:
        loudness = loudness * one(*cut)
    return loudness


def centred(rng, dims, width, limit, cuts=(), kind=jnp.bfloat16):
    values = width * jax.random.normal(rng, dims, jnp.float32)
    if cuts:
        values = values * block_levels(rng, dims, cuts, -0.22, 0.18)
    return jnp.clip(values, -limit, limit).astype(kind)


def setup_inputs(seed: int = 0) -> dict:
    streams_of = jax.random.split(jax.random.key(seed), 7)
    u_vel = centred(streams_of[0], (LEVELS, NY, NX), 0.5, 3.0, ((1, 32), (2, 32)), jnp.float32)
    v_vel = centred(streams_of[1], (LEVELS, NY, NX), 0.5, 3.0, ((1, 32), (2, 32)), jnp.float32)
    temp = centred(streams_of[2], (LEVELS, NY, NX), 1.0, 6.0, ((1, 32), (2, 32)), jnp.float32)
    salt = centred(streams_of[3], (LEVELS, NY, NX), 1.0, 6.0, ((1, 32), (2, 32)), jnp.float32)
    eta = centred(streams_of[4], (NY, NX), 1.0, 5.0, ((0, 32), (1, 32)), jnp.float32)
    wet_levels = draw_wet_levels(jax.random.fold_in(streams_of[6], 71), 0)
    return {"u_vel": u_vel, "v_vel": v_vel, "temp": temp, "salt": salt, "eta": eta, "wet_levels": wet_levels}


time_step = 0.4
epsilon = 1e-6
wave_share = 0.45


def weno_value(minus_two, minus_one, centre, plus_one, plus_two):
    first = (2.0 * minus_two - 7.0 * minus_one + 11.0 * centre) / 6.0
    second = (-minus_one + 5.0 * centre + 2.0 * plus_one) / 6.0
    third = (2.0 * centre + 5.0 * plus_one - plus_two) / 6.0
    rough_a = 13.0 / 12.0 * (minus_two - 2.0 * minus_one + centre) ** 2 + 0.25 * (minus_two - 4.0 * minus_one + 3.0 * centre) ** 2
    rough_b = 13.0 / 12.0 * (minus_one - 2.0 * centre + plus_one) ** 2 + 0.25 * (minus_one - plus_one) ** 2
    rough_c = 13.0 / 12.0 * (centre - 2.0 * plus_one + plus_two) ** 2 + 0.25 * (3.0 * centre - 4.0 * plus_one + plus_two) ** 2
    weight_a = 0.1 / (epsilon + rough_a) ** 2
    weight_b = 0.6 / (epsilon + rough_b) ** 2
    weight_c = 0.3 / (epsilon + rough_c) ** 2
    return (weight_a * first + weight_b * second + weight_c * third) / (weight_a + weight_b + weight_c)


def face_values(cells, flow, axis):
    axis = axis % cells.ndim
    count = cells.shape[axis] - 5
    pieces = [lax.slice_in_dim(cells, start, start + count, axis=axis) for start in range(6)]
    upwind = weno_value(pieces[0], pieces[1], pieces[2], pieces[3], pieces[4])
    downwind = weno_value(pieces[5], pieces[4], pieces[3], pieces[2], pieces[1])
    return jnp.where(flow >= 0.0, upwind, downwind)


def advect(fields, east, north):
    rows_y = fields.shape[-2] - 6
    cols_x = fields.shape[-1] - 6
    flow_x = east[..., 3:3 + rows_y, 2:3 + cols_x]
    flux_x = flow_x * face_values(fields[..., 3:3 + rows_y, :], flow_x, -1)
    flow_y = north[..., 2:3 + rows_y, 3:3 + cols_x]
    flux_y = flow_y * face_values(fields[..., :, 3:3 + cols_x], flow_y, -2)
    return -((flux_x[..., 1:] - flux_x[..., :-1]) + (flux_y[..., 1:, :] - flux_y[..., :-1, :]))


def toward(values, axis, offset, cycle):
    if cycle:
        return jnp.roll(values, offset, axis)
    length = values.shape[axis]
    blank = jnp.zeros_like(lax.slice_in_dim(values, 0, 1, axis=axis))
    if offset == 1:
        return jnp.concatenate([blank, lax.slice_in_dim(values, 0, length - 1, axis=axis)], axis)
    return jnp.concatenate([lax.slice_in_dim(values, 1, length, axis=axis), blank], axis)


def surface_run(state, statics, count, wave, cycle):
    height, trans_x, trans_y = state[0], state[1], state[2]
    force_x, force_y, depth_x, depth_y = statics[0], statics[1], statics[2], statics[3]
    for repeat in range(count):
        height = height - (trans_x - toward(trans_x, 1, 1, cycle) + trans_y - toward(trans_y, 0, 1, False))
        trans_x = trans_x - wave * depth_x * (toward(height, 1, -1, cycle) - height) + force_x
        trans_y = trans_y - wave * depth_y * (toward(height, 0, -1, False) - height) + force_y
    return jnp.stack([height, trans_x, trans_y])


def pad_three(values):
    values = jnp.concatenate([values[..., -3:], values, values[..., :3]], -1)
    widths = [(0, 0)] * (values.ndim - 2) + [(3, 3), (0, 0)]
    return jnp.pad(values, widths)


def reference(u_vel, v_vel, temp, salt, eta, wet_levels):
    levels = wet_levels.astype(jnp.float32)
    level_c, level_x, level_y = levels[0], levels[1], levels[2]

    def momentum(carry, inputs):
        u_level, v_level, depth = inputs
        wet_x = (depth < level_x).astype(jnp.float32)
        wet_y = (depth < level_y).astype(jnp.float32)
        east_flow = u_level * wet_x
        north_flow = v_level * wet_y
        padded = pad_three(jnp.stack([east_flow, north_flow]))
        tendency = advect(padded, padded[0], padded[1])
        new_u = (east_flow + time_step * tendency[0]) * wet_x
        new_v = (north_flow + time_step * tendency[1]) * wet_y
        terms = (east_flow, north_flow, tendency[0] * wet_x, tendency[1] * wet_y, new_u, new_v)
        carry = tuple(total + term for total, term in zip(carry, terms))
        return carry, (new_u, new_v)

    blank = jnp.zeros(eta.shape, jnp.float32)
    depths = jnp.arange(LEVELS, dtype=jnp.float32)
    sums, (step_u, step_v) = lax.scan(momentum, (blank, blank, blank, blank, blank, blank), (u_vel, v_vel, depths))
    trans_x, trans_y, push_x, push_y, total_u, total_v = sums
    scale = time_step / SUB
    statics = jnp.stack([scale * push_x, scale * push_y, level_x, level_y])
    surface = surface_run(jnp.stack([eta, trans_x, trans_y]), statics, SUB, wave_share / LEVELS, True)
    safe_x = jnp.maximum(level_x, 1.0)
    safe_y = jnp.maximum(level_y, 1.0)

    def finish(inputs):
        u_level, v_level, t_level, s_level, depth = inputs
        wet_c = (depth < level_c).astype(jnp.float32)
        wet_x = (depth < level_x).astype(jnp.float32)
        wet_y = (depth < level_y).astype(jnp.float32)
        new_u = (u_level - total_u / safe_x + surface[1] / safe_x) * wet_x
        new_v = (v_level - total_v / safe_y + surface[2] / safe_y) * wet_y
        tracer = jnp.stack([t_level * wet_c, s_level * wet_c])
        tendency = advect(pad_three(tracer), pad_three(new_u), pad_three(new_v))
        new_tracer = (tracer + time_step * tendency) * wet_c
        return new_u, new_v, new_tracer[0], new_tracer[1]

    u_new, v_new, temp_new, salt_new = lax.map(finish, (step_u, step_v, temp, salt, depths))
    return u_new, v_new, temp_new, salt_new, surface[0]
```

```python
import jax
import jax.numpy as jnp
from jax import lax
from jax.experimental import pallas as pl
from jax.experimental.pallas import tpu as pltpu
from jax.sharding import PartitionSpec as P

MESH = pl.DeviceIdType.MESH
F32 = jnp.float32
LEVELS = 4
SUB = 8
STEP = 0.4
WAVE = 0.45 / 4
EPS = 1e-6 * 12.0 / 13.0
ROWS = 32
COLS = 128
PAD = 16
EXT = ROWS + 2 * PAD
LO = 8
SPAN = 48

U_MAIN, V_MAIN, U_SW, U_SE, V_SW, V_SE = 0, 4, 8, 9, 10, 11


def lanes(x, shift):
    shift = shift % COLS
    return x if shift == 0 else pltpu.roll(x, shift, 1)


def rows(x, shift):
    return pltpu.roll(x, shift % x.shape[0], 0)


def correction(d0, d1, d2, d3):
    x0 = d1 - d0
    x1 = d2 - d1
    x2 = d3 - d2
    m1 = d1 + d1
    m2 = d2 + d2
    y0 = x0 + m1
    y1 = d1 + d2
    y2 = x2 - m2
    e0 = x0 * x0 + (y0 * y0) * (3.0 / 13.0) + EPS
    e1 = x1 * x1 + (y1 * y1) * (3.0 / 13.0) + EPS
    e2 = x2 * x2 + (y2 * y2) * (3.0 / 13.0) + EPS
    a0 = e1 * e2
    a1 = e0 * e2
    a2 = e0 * e1
    w0 = a0 * a0
    w1 = (a1 * a1) * 6.0
    w2 = (a2 * a2) * 3.0
    top = w0 * (5.0 * d1 - 2.0 * d0) + w1 * (d1 + m2) + w2 * (4.0 * d2 - d3)
    return top / ((w0 + w1 + w2) * 6.0)


def upwind_value(flow, q0, q1, gm2, gm1, g0, g1, g2):
    ahead = flow >= 0.0
    fix = correction(jnp.where(ahead, gm2, g2), jnp.where(ahead, gm1, g1), g0, jnp.where(ahead, g1, gm1))
    return jnp.where(ahead, q0 + fix, q1 - fix)


def x_parts(q):
    q1 = lanes(q, -1)
    g = q1 - q
    return q, q1, lanes(g, 2), lanes(g, 1), g, lanes(g, -1), lanes(g, -2)


def y_parts(ref, k, r0, n):
    q = [ref[k, pl.ds(r0 + s, n), :] for s in range(-2, 4)]
    g = [q[i + 1] - q[i] for i in range(5)]
    return q[2], q[3], g[0], g[1], g[2], g[3], g[4]


def ring(parts):
    lane = lax.broadcasted_iota(jnp.int32, parts[0].shape, 1)
    out = lanes(parts[0], 16)
    for k in range(1, LEVELS):
        out = jnp.where(lane >= 32 * k, lanes(parts[k], 32 * k + 16), out)
    return out


def level_sum(x):
    y = x + lanes(x, 64)
    return y + lanes(y, 32)


def spread(x, start):
    lane = lax.broadcasted_iota(jnp.int32, x.shape, 1)
    return level_sum(jnp.where((lane >= start) & (lane < start + 32), x, 0.0))


def kernel(n_lat, n_lon, u_hbm, v_hbm, t_hbm, s_hbm, e_hbm, w_hbm,
           u_out, v_out, t_out, s_out, e_out,
           raw, raw2, wet, UV, TS, WE, PK, TE, TW, RW, RE, RTW, RTE,
           TEND, FY, XU, XD, YU, YD, NV, NU, XS,
           in_sem, send_sem, recv_sem):
    lat = lax.axis_index("lat")
    lon = lax.axis_index("lon")
    north = (lax.rem(lat + 1, n_lat), lon)
    south = (lax.rem(lat + n_lat - 1, n_lat), lon)
    east = (lat, lax.rem(lon + 1, n_lon))
    west = (lat, lax.rem(lon + n_lon - 1, n_lon))

    barrier = pltpu.get_barrier_semaphore()
    for peer in (north, south, east, west):
        pl.semaphore_signal(barrier, inc=1, device_id=peer, device_id_type=MESH)

    loads = [
        pltpu.make_async_copy(w_hbm, wet, in_sem.at[0]),
        pltpu.make_async_copy(u_hbm, raw.at[pl.ds(0, 4)], in_sem.at[1]),
        pltpu.make_async_copy(v_hbm, raw.at[pl.ds(4, 4)], in_sem.at[2]),
        pltpu.make_async_copy(t_hbm, raw.at[pl.ds(8, 4)], in_sem.at[3]),
        pltpu.make_async_copy(s_hbm, raw.at[pl.ds(12, 4)], in_sem.at[4]),
        pltpu.make_async_copy(e_hbm, raw2, in_sem.at[5]),
    ]
    for load in loads:
        load.start()
    for load in loads:
        load.wait()

    OWN = pl.ds(PAD, ROWS)
    for k in range(LEVELS):
        UV[U_MAIN + k, OWN, :] = jnp.where(wet[1] > k, raw[k], 0.0)
        UV[V_MAIN + k, OWN, :] = jnp.where(wet[2] > k, raw[4 + k], 0.0)
        TS[k, OWN, :] = jnp.where(wet[0] > k, raw[8 + k], 0.0)
        TS[4 + k, OWN, :] = jnp.where(wet[0] > k, raw[12 + k], 0.0)
    WE[0, OWN, :] = wet[0].astype(F32)
    WE[1, OWN, :] = raw2[...]

    lane32 = lax.broadcasted_iota(jnp.int32, (ROWS, COLS), 1)
    half32 = lax.rem(lane32, 32) < 16
    ring_u = ring([UV[U_MAIN + k, OWN, :] for k in range(LEVELS)])
    ring_v = ring([UV[V_MAIN + k, OWN, :] for k in range(LEVELS)])
    PK[0, OWN, :] = jnp.where(half32, ring_u, lanes(ring_v, 16))
    PK[1, OWN, :] = jnp.where(lane32 < 32, lanes(raw2[...], 16), lanes(wet[0].astype(F32), 48))
    PK[2, OWN, :] = jnp.where(half32, lanes(ring_u, -16), ring_v)
    ring_t = ring([TS[k, OWN, :] for k in range(LEVELS)])
    ring_s = ring([TS[4 + k, OWN, :] for k in range(LEVELS)])
    TE[...] = jnp.where(half32, ring_t, lanes(ring_s, 16))
    TW[...] = jnp.where(half32, lanes(ring_t, -16), ring_s)

    pl.semaphore_wait(barrier, 4)

    def send(slot, src, dst, peer):
        copy = pltpu.make_async_remote_copy(
            src_ref=src, dst_ref=dst, send_sem=send_sem.at[slot], recv_sem=recv_sem.at[slot],
            device_id=peer, device_id_type=MESH)
        copy.start()
        return copy

    top, bottom = pl.ds(32, 16), pl.ds(16, 16)
    under, over = pl.ds(0, 16), pl.ds(48, 16)
    every = pl.ds(0, 8)
    corner_n = send(0, PK.at[:, top, :], PK.at[:, under, :], north)
    corner_s = send(1, PK.at[:, bottom, :], PK.at[:, over, :], south)
    bulk = [
        send(2, UV.at[every, top, :], UV.at[every, under, :], north),
        send(3, UV.at[every, bottom, :], UV.at[every, over, :], south),
        send(4, WE.at[:, top, :], WE.at[:, under, :], north),
        send(5, WE.at[:, bottom, :], WE.at[:, over, :], south),
        send(6, TS.at[:, pl.ds(40, 8), :], TS.at[:, pl.ds(8, 8), :], north),
        send(7, TS.at[:, pl.ds(16, 8), :], TS.at[:, pl.ds(48, 8), :], south),
    ]
    sides = [
        send(8, PK.at[pl.ds(0, 2), OWN, :], RW.at[:, OWN, :], east),
        send(9, PK.at[pl.ds(1, 2), OWN, :], RE.at[:, OWN, :], west),
        send(10, TE, RTW, east),
        send(11, TW, RTE, west),
    ]
    corner_n.wait_recv()
    relays = [
        send(12, PK.at[pl.ds(0, 2), under, :], RW.at[:, under, :], east),
        send(13, PK.at[pl.ds(1, 2), under, :], RE.at[:, under, :], west),
    ]
    corner_s.wait_recv()
    relays += [
        send(14, PK.at[pl.ds(0, 2), over, :], RW.at[:, over, :], east),
        send(15, PK.at[pl.ds(1, 2), over, :], RE.at[:, over, :], west),
    ]

    def tracer_x(k, carry):
        for r0 in range(0, ROWS, 16):
            q0, q1, gm2, gm1, g0, g1, g2 = x_parts(TS[k, pl.ds(PAD + r0, 16), :])
            XU[k, pl.ds(r0, 16), :] = q0 + correction(gm2, gm1, g0, g1)
            XD[k, pl.ds(r0, 16), :] = q1 - correction(g2, g1, g0, gm1)
        return carry

    lax.fori_loop(0, 8, tracer_x, 0)

    for copy in bulk:
        copy.wait_recv()

    zero16 = jnp.zeros((16, COLS), F32)
    FY[pl.ds(SPAN, 8), :] = jnp.zeros((8, COLS), F32)

    @pl.when(lat == 0)
    def _():
        for k in range(8):
            UV[k, under, :] = zero16
            TS[k, under, :] = zero16
        WE[0, under, :] = zero16
        WE[1, under, :] = zero16

    @pl.when(lat == n_lat - 1)
    def _():
        for k in range(8):
            UV[k, over, :] = zero16
            TS[k, over, :] = zero16
        WE[0, over, :] = zero16
        WE[1, over, :] = zero16

    def tendency(q_plane, u_plane, v_plane, out):
        for r0 in range(0, SPAN, 8):
            base = LO - 1 + r0
            FY[pl.ds(r0, 8), :] = UV[v_plane, pl.ds(base, 8), :] * upwind_value(
                UV[v_plane, pl.ds(base, 8), :], *y_parts(UV, q_plane, base, 8))
        for r0 in range(0, SPAN, 16):
            flow = UV[u_plane, pl.ds(LO + r0, 16), :]
            flux = flow * upwind_value(flow, *x_parts(UV[q_plane, pl.ds(LO + r0, 16), :]))
            TEND[out, pl.ds(r0, 16), :] = -(flux - lanes(flux, 1) + (
                FY[pl.ds(r0 + 1, 16), :] - FY[pl.ds(r0, 16), :]))

    def momentum(k, carry):
        tendency(k, k, V_MAIN + k, k)
        tendency(V_MAIN + k, k, V_MAIN + k, V_MAIN + k)
        return carry

    lax.fori_loop(0, LEVELS, momentum, 0)

    def tracer_y(k, carry):
        for r0 in range(0, 40, 8):
            q0, q1, gm2, gm1, g0, g1, g2 = y_parts(TS, k, PAD - 1 + r0, 8)
            YU[k, pl.ds(r0, 8), :] = q0 + correction(gm2, gm1, g0, g1)
            YD[k, pl.ds(r0, 8), :] = q1 - correction(g2, g1, g0, gm1)
        return carry

    lax.fori_loop(0, 8, tracer_y, 0)

    for copy in sides + relays:
        copy.wait_recv()

    @pl.when(lat == 0)
    def _():
        for i in range(2):
            RW[i, under, :] = zero16
            RE[i, under, :] = zero16

    @pl.when(lat == n_lat - 1)
    def _():
        for i in range(2):
            RW[i, over, :] = zero16
            RE[i, over, :] = zero16

    lane64 = lax.broadcasted_iota(jnp.int32, (EXT, COLS), 1)
    half = lax.rem(lane64, 32) < 16
    ring_u = ring([UV[U_MAIN + k] for k in range(LEVELS)])
    ring_v = ring([UV[V_MAIN + k] for k in range(LEVELS)])
    UV[U_SW] = jnp.where(half, RW[0], ring_u)
    UV[V_SW] = jnp.where(half, lanes(RW[0], -16), ring_v)
    UV[U_SE] = jnp.where(half, ring_u, lanes(RE[1], 16))
    UV[V_SE] = jnp.where(half, ring_v, RE[1])

    def strips(i, carry):
        tendency(U_SW + i, U_SW + i, V_SW + i, U_SW + i)
        tendency(V_SW + i, U_SW + i, V_SW + i, V_SW + i)
        return carry

    lax.fori_loop(0, 2, strips, 0)

    own_2d = jnp.where(lane64 < 32, lanes(WE[1], 16), lanes(WE[0], 48))
    west_2d = jnp.where(half, RW[1], own_2d)
    east_2d = jnp.where(half, own_2d, RE[0])
    lane = lax.broadcasted_iota(jnp.int32, (SPAN, COLS), 1)
    level = (lane // 32).astype(F32)
    BAND = pl.ds(LO, SPAN)

    def band(x):
        return x[LO:LO + SPAN]

    def joined(sw, main, se):
        return jnp.where(lane < 24, sw, jnp.where(lane < 64, lanes(main, 16), jnp.where(lane < 104, lanes(main, -16), se)))

    def shifted_up(x):
        return rows(x, -1)

    wet_sw = spread(west_2d, 32)
    wet_se = spread(east_2d, 32)
    wet_main = WE[0]
    eta_main = WE[1, BAND, :]
    eta_side = joined(spread(band(west_2d), 0), eta_main, spread(band(east_2d), 0))

    def faces(w):
        here = band(w)
        return jnp.minimum(here, lanes(here, -1)), jnp.minimum(here, band(shifted_up(w)))

    wx_main, wy_main = faces(wet_main)
    wx_sw, wy_sw = faces(wet_sw)
    wx_se, wy_se = faces(wet_se)
    wx_side = joined(wx_sw, wx_main, wx_se)
    wy_side = joined(wy_sw, wy_main, wy_se)

    def main_sum(ref, first, where_rows, limit=None):
        total = None
        for k in range(LEVELS):
            term = ref[first + k, where_rows, :]
            if limit is not None:
                term = jnp.where(limit > k, term, 0.0)
            total = term if total is None else total + term
        return total

    def side_sum(ref, plane, where_rows, limit=None):
        term = ref[plane, where_rows, :]
        if limit is not None:
            term = jnp.where(limit > level, term, 0.0)
        return level_sum(term)

    ALL = pl.ds(0, SPAN)
    scale = STEP / SUB
    push_x = main_sum(TEND, U_MAIN, ALL, wx_main)
    push_y = main_sum(TEND, V_MAIN, ALL, wy_main)
    push_x_sw = side_sum(TEND, U_SW, ALL, wx_sw)
    push_x_se = side_sum(TEND, U_SE, ALL, wx_se)
    push_y_sw = side_sum(TEND, V_SW, ALL, wy_sw)
    push_y_se = side_sum(TEND, V_SE, ALL, wy_se)
    tx0 = main_sum(UV, U_MAIN, BAND)
    ty0 = main_sum(UV, V_MAIN, BAND)
    tx0_sw, tx0_se = side_sum(UV, U_SW, BAND), side_sum(UV, U_SE, BAND)
    ty0_sw, ty0_se = side_sum(UV, V_SW, BAND), side_sum(UV, V_SE, BAND)
    LOWER = pl.ds(LO - 1, SPAN)
    tym_main = main_sum(UV, V_MAIN, LOWER)
    tym_side = joined(side_sum(UV, V_SW, LOWER), tym_main, side_sum(UV, V_SE, LOWER))

    def substeps(height, tx, ty, tym, fx, fy, cx, cy):
        for n in range(SUB):
            below = tym if n == 0 else rows(ty, 1)
            height = height - (tx - lanes(tx, 1) + ty - below)
            tx = tx - cx * (lanes(height, -1) - height) + fx
            ty = ty - cy * (rows(height, -1) - height) + fy
        return height, tx, ty

    h_main, tx_main, ty_main = substeps(
        eta_main, tx0, ty0, tym_main, scale * push_x, scale * push_y, WAVE * wx_main, WAVE * wy_main)
    h_side, tx_side, ty_side = substeps(
        eta_side, joined(tx0_sw, tx0, tx0_se), joined(ty0_sw, ty0, ty0_se), tym_side,
        scale * joined(push_x_sw, push_x, push_x_se), scale * joined(push_y_sw, push_y, push_y_se),
        WAVE * wx_side, WAVE * wy_side)

    own = slice(PAD - LO, PAD - LO + ROWS)
    e_out[...] = jnp.where(lane < 16, lanes(h_side, -16), jnp.where(lane >= 112, lanes(h_side, 16), h_main))[own]

    def fresh_side(flow_plane, tend_plane, total, depth, trans):
        safe = jnp.maximum(depth, 1.0)
        step = UV[flow_plane, BAND, :] + STEP * TEND[tend_plane, ALL, :]
        return jnp.where(depth > level, step + (trans - total) / safe, 0.0)

    def total_of(trans0, push):
        return trans0 + STEP * push

    u_sw = fresh_side(U_SW, U_SW, total_of(tx0_sw, push_x_sw), wx_sw, spread(tx_side, 0))
    u_se = fresh_side(U_SE, U_SE, total_of(tx0_se, push_x_se), wx_se, spread(tx_side, 96))
    v_sw = fresh_side(V_SW, V_SW, total_of(ty0_sw, push_y_sw), wy_sw, spread(ty_side, 0))
    v_se = fresh_side(V_SE, V_SE, total_of(ty0_se, push_y_se), wy_se, spread(ty_side, 96))

    gain_x = (tx_main - total_of(tx0, push_x)) / jnp.maximum(wx_main, 1.0)
    gain_y = (ty_main - total_of(ty0, push_y)) / jnp.maximum(wy_main, 1.0)
    for k in range(LEVELS):
        fresh = jnp.where(wx_main > k, UV[U_MAIN + k, BAND, :] + STEP * TEND[U_MAIN + k, ALL, :] + gain_x, 0.0)
        fresh = jnp.where(lane < 12, lanes(u_sw, -(32 * k + 16)), jnp.where(lane >= 116, lanes(u_se, 112 - 32 * k), fresh))
        NU[k] = fresh[own]
        u_out[k] = fresh[own]
        fresh = jnp.where(wy_main > k, UV[V_MAIN + k, BAND, :] + STEP * TEND[V_MAIN + k, ALL, :] + gain_y, 0.0)
        fresh = jnp.where(lane < 12, lanes(v_sw, -(32 * k + 16)), jnp.where(lane >= 116, lanes(v_se, 112 - 32 * k), fresh))
        NV[k] = fresh
        v_out[k] = fresh[own]

    ring_t = ring([TS[k, OWN, :] for k in range(LEVELS)])
    ring_s = ring([TS[4 + k, OWN, :] for k in range(LEVELS)])

    def side_flux(cells, flow):
        flux = flow * upwind_value(flow, *x_parts(cells))
        return flux - lanes(flux, 1)

    XS[0] = side_flux(jnp.where(half32, RTW[...], ring_t), u_sw[own])
    XS[1] = side_flux(jnp.where(half32, ring_t, lanes(RTE[...], 16)), u_se[own])
    XS[2] = side_flux(jnp.where(half32, lanes(RTW[...], -16), ring_s), u_sw[own])
    XS[3] = side_flux(jnp.where(half32, ring_s, RTE[...]), u_se[own])

    for field in range(2):
        out = (t_out, s_out)[field]
        for k in range(LEVELS):
            p = 4 * field + k
            flow = NU[k]
            flux = flow * jnp.where(flow >= 0.0, XU[p], XD[p])
            div_x = flux - lanes(flux, 1)
            div_x = jnp.where(lane32 < 8, lanes(XS[2 * field], -(32 * k + 16)),
                              jnp.where(lane32 >= 120, lanes(XS[2 * field + 1], 112 - 32 * k), div_x))
            up = NV[k, pl.ds(8, ROWS), :]
            down = NV[k, pl.ds(7, ROWS), :]
            flux_up = up * jnp.where(up >= 0.0, YU[p, pl.ds(1, ROWS), :], YD[p, pl.ds(1, ROWS), :])
            flux_down = down * jnp.where(down >= 0.0, YU[p, pl.ds(0, ROWS), :], YD[p, pl.ds(0, ROWS), :])
            cells = TS[p, OWN, :]
            fresh = cells - STEP * (div_x + (flux_up - flux_down))
            out[k] = jnp.where(wet[0] > k, fresh, 0.0)

    corner_n.wait_send()
    corner_s.wait_send()
    for copy in bulk + sides + relays:
        copy.wait_send()


def solution(mesh):
    n_lat, n_lon = mesh.shape["lat"], mesh.shape["lon"]

    def step(u_vel, v_vel, temp, salt, eta, wet_levels):
        levels = jax.ShapeDtypeStruct((LEVELS, ROWS, COLS), F32)
        plane = jax.ShapeDtypeStruct((ROWS, COLS), F32)
        hbm = pl.BlockSpec(memory_space=pl.ANY)
        vmem = pl.BlockSpec(memory_space=pltpu.VMEM)

        def body(*refs):
            kernel(n_lat, n_lon, *refs)

        return pl.pallas_call(
            body,
            out_shape=(levels, levels, levels, levels, plane),
            in_specs=[hbm] * 6,
            out_specs=(vmem,) * 5,
            scratch_shapes=[
                pltpu.VMEM((16, ROWS, COLS), F32),
                pltpu.VMEM((ROWS, COLS), F32),
                pltpu.VMEM((3, ROWS, COLS), jnp.int32),
                pltpu.VMEM((12, EXT, COLS), F32),
                pltpu.VMEM((8, EXT, COLS), F32),
                pltpu.VMEM((2, EXT, COLS), F32),
                pltpu.VMEM((3, EXT, COLS), F32),
                pltpu.VMEM((ROWS, COLS), F32),
                pltpu.VMEM((ROWS, COLS), F32),
                pltpu.VMEM((2, EXT, COLS), F32),
                pltpu.VMEM((2, EXT, COLS), F32),
                pltpu.VMEM((ROWS, COLS), F32),
                pltpu.VMEM((ROWS, COLS), F32),
                pltpu.VMEM((12, SPAN, COLS), F32),
                pltpu.VMEM((SPAN + 8, COLS), F32),
                pltpu.VMEM((8, ROWS, COLS), F32),
                pltpu.VMEM((8, ROWS, COLS), F32),
                pltpu.VMEM((8, 40, COLS), F32),
                pltpu.VMEM((8, 40, COLS), F32),
                pltpu.VMEM((4, SPAN, COLS), F32),
                pltpu.VMEM((4, ROWS, COLS), F32),
                pltpu.VMEM((4, ROWS, COLS), F32),
                pltpu.SemaphoreType.DMA((6,)),
                pltpu.SemaphoreType.DMA((16,)),
                pltpu.SemaphoreType.DMA((16,)),
            ],
            compiler_params=pltpu.CompilerParams(collective_id=0, has_side_effects=True),
        )(u_vel, v_vel, temp, salt, eta, wet_levels)

    tile, flat = P(None, "lat", "lon"), P("lat", "lon")
    return jax.shard_map(
        step, mesh=mesh, in_specs=(tile, tile, tile, tile, flat, tile),
        out_specs=(tile, tile, tile, tile, flat), check_vma=False)
```

```python
import jax
import jax.numpy as jnp
from jax import lax
from jax.experimental import pallas as pl
from jax.experimental.pallas import tpu as pltpu
from jax.sharding import PartitionSpec as P

MESH = pl.DeviceIdType.MESH
F32 = jnp.float32
LEVELS = 4
SUB = 8
STEP = 0.4
WAVE = 0.45 / 4
EPS = 1e-6 * 12.0 / 13.0
ROWS = 32
COLS = 128
PAD = 16
EXT = ROWS + 2 * PAD
LO = 8
SPAN = 48

U_MAIN, V_MAIN, U_SW, U_SE, V_SW, V_SE = 0, 4, 8, 9, 10, 11


def lanes(x, shift):
    shift = shift % COLS
    return x if shift == 0 else pltpu.roll(x, shift, 1)


def rows(x, shift):
    return pltpu.roll(x, shift % x.shape[0], 0)


def correction(d0, d1, d2, d3):
    x0 = d1 - d0
    x1 = d2 - d1
    x2 = d3 - d2
    m1 = d1 + d1
    m2 = d2 + d2
    y0 = x0 + m1
    y1 = d1 + d2
    y2 = x2 - m2
    e0 = x0 * x0 + (y0 * y0) * (3.0 / 13.0) + EPS
    e1 = x1 * x1 + (y1 * y1) * (3.0 / 13.0) + EPS
    e2 = x2 * x2 + (y2 * y2) * (3.0 / 13.0) + EPS
    a0 = e1 * e2
    a1 = e0 * e2
    a2 = e0 * e1
    w0 = a0 * a0
    w1 = (a1 * a1) * 6.0
    w2 = (a2 * a2) * 3.0
    top = w0 * (5.0 * d1 - 2.0 * d0) + w1 * (d1 + m2) + w2 * (4.0 * d2 - d3)
    return top / ((w0 + w1 + w2) * 6.0)


def upwind_value(flow, q0, q1, gm2, gm1, g0, g1, g2):
    ahead = flow >= 0.0
    fix = correction(jnp.where(ahead, gm2, g2), jnp.where(ahead, gm1, g1), g0, jnp.where(ahead, g1, gm1))
    return jnp.where(ahead, q0 + fix, q1 - fix)


def x_parts(q):
    q1 = lanes(q, -1)
    g = q1 - q
    return q, q1, lanes(g, 2), lanes(g, 1), g, lanes(g, -1), lanes(g, -2)


def y_parts(ref, k, r0, n):
    q = [ref[k, pl.ds(r0 + s, n), :] for s in range(-2, 4)]
    g = [q[i + 1] - q[i] for i in range(5)]
    return q[2], q[3], g[0], g[1], g[2], g[3], g[4]


def ring(parts):
    lane = lax.broadcasted_iota(jnp.int32, parts[0].shape, 1)
    out = lanes(parts[0], 16)
    for k in range(1, LEVELS):
        out = jnp.where(lane >= 32 * k, lanes(parts[k], 32 * k + 16), out)
    return out


def level_sum(x):
    y = x + lanes(x, 64)
    return y + lanes(y, 32)


def spread(x, start):
    lane = lax.broadcasted_iota(jnp.int32, x.shape, 1)
    return level_sum(jnp.where((lane >= start) & (lane < start + 32), x, 0.0))


DIRS = ((1, 0), (-1, 0), (0, 1), (0, -1), (1, 1), (-1, 1), (1, -1), (-1, -1))
NORTH, SOUTH, EAST, WEST, NE, SE, NW, SW = range(8)


def kernel(n_lat, n_lon, u_hbm, v_hbm, t_hbm, s_hbm, e_hbm, w_hbm,
           result,
           raw, raw2, wet, UV, TS, WE, PE, PW, RW, RE,
           TEND, FY, XU, XD, YU, YD, NV, NU, XS,
           in_sem, ready, send_sem, recv_sem):
    lat = lax.axis_index("lat")
    lon = lax.axis_index("lon")

    def start_rank(i, j):
        return ((j // 8) * 8 + lax.rem(i, 8)) * (n_lat * n_lon) + i * n_lon + j

    peers = [(lax.rem(lat + n_lat + di, n_lat), lax.rem(lon + n_lon + dj, n_lon)) for di, dj in DIRS]
    here = start_rank(lat, lon)
    earlier = [start_rank(*peer) < here for peer in peers]

    barrier = pltpu.get_barrier_semaphore()
    expected = 0
    for d in range(8):
        expected = expected + jnp.where(earlier[d], 1, 0)

        @pl.when(jnp.logical_not(earlier[d]))
        def _():
            pl.semaphore_signal(barrier, inc=1, device_id=peers[d], device_id_type=MESH)

    loads = [
        pltpu.make_async_copy(w_hbm, wet, in_sem.at[0]),
        pltpu.make_async_copy(u_hbm, raw.at[pl.ds(0, 4)], in_sem.at[1]),
        pltpu.make_async_copy(v_hbm, raw.at[pl.ds(4, 4)], in_sem.at[2]),
        pltpu.make_async_copy(t_hbm, raw.at[pl.ds(8, 4)], in_sem.at[3]),
        pltpu.make_async_copy(s_hbm, raw.at[pl.ds(12, 4)], in_sem.at[4]),
        pltpu.make_async_copy(e_hbm, raw2, in_sem.at[5]),
    ]
    for load in loads:
        load.start()
    for load in loads:
        load.wait()

    OWN = pl.ds(PAD, ROWS)
    for k in range(LEVELS):
        UV[U_MAIN + k, OWN, :] = jnp.where(wet[1] > k, raw[k], 0.0)
        UV[V_MAIN + k, OWN, :] = jnp.where(wet[2] > k, raw[4 + k], 0.0)
        TS[k, OWN, :] = jnp.where(wet[0] > k, raw[8 + k], 0.0)
        TS[4 + k, OWN, :] = jnp.where(wet[0] > k, raw[12 + k], 0.0)
    WE[0, OWN, :] = wet[0].astype(F32)
    WE[1, OWN, :] = raw2[...]

    lane32 = lax.broadcasted_iota(jnp.int32, (ROWS, COLS), 1)
    half32 = lax.rem(lane32, 32) < 16
    ring_u = ring([UV[U_MAIN + k, OWN, :] for k in range(LEVELS)])
    ring_v = ring([UV[V_MAIN + k, OWN, :] for k in range(LEVELS)])
    ring_t = ring([TS[k, OWN, :] for k in range(LEVELS)])
    ring_s = ring([TS[4 + k, OWN, :] for k in range(LEVELS)])
    eta8, wet24 = lanes(raw2[...], 8), lanes(wet[0].astype(F32), 24)
    PE[0, OWN, :] = jnp.where(half32, ring_u, lanes(ring_v, 16))
    PW[0, OWN, :] = jnp.where(half32, lanes(ring_u, -16), ring_v)
    PE[1, OWN, :] = jnp.where(lane32 < 8, eta8, jnp.where(
        (lane32 >= 16) & (lane32 < 24), wet24, jnp.where(half32, ring_t, lanes(ring_s, 16))))
    PW[1, OWN, :] = jnp.where((lane32 >= 8) & (lane32 < 16), eta8, jnp.where(
        (lane32 >= 24) & (lane32 < 32), wet24, jnp.where(half32, lanes(ring_t, -16), ring_s)))

    top, bottom = pl.ds(32, 16), pl.ds(16, 16)
    under, over = pl.ds(0, 16), pl.ds(48, 16)
    every = pl.ds(0, 8)
    parcels = {
        NORTH: [(UV.at[every, top, :], UV.at[every, under, :]),
                (WE.at[:, top, :], WE.at[:, under, :]),
                (TS.at[:, pl.ds(40, 8), :], TS.at[:, pl.ds(8, 8), :])],
        SOUTH: [(UV.at[every, bottom, :], UV.at[every, over, :]),
                (WE.at[:, bottom, :], WE.at[:, over, :]),
                (TS.at[:, pl.ds(16, 8), :], TS.at[:, pl.ds(48, 8), :])],
        EAST: [(PE.at[:, OWN, :], RW.at[:, OWN, :])],
        WEST: [(PW.at[:, OWN, :], RE.at[:, OWN, :])],
        NE: [(PE.at[:, top, :], RW.at[:, under, :])],
        SE: [(PE.at[:, bottom, :], RW.at[:, over, :])],
        NW: [(PW.at[:, top, :], RE.at[:, under, :])],
        SW: [(PW.at[:, bottom, :], RE.at[:, over, :])],
    }
    first_slot, slots = {}, 0
    for d in range(8):
        first_slot[d] = slots
        slots += len(parcels[d])

    def copies(d):
        return [
            pltpu.make_async_remote_copy(
                src_ref=src, dst_ref=dst, send_sem=send_sem.at[first_slot[d] + i], recv_sem=recv_sem.at[first_slot[d] + i],
                device_id=peers[d], device_id_type=MESH)
            for i, (src, dst) in enumerate(parcels[d])]

    def send_to_earlier(d):
        @pl.when(earlier[d])
        def _():
            for copy in copies(d):
                copy.start()

    def send_to_later(d):
        @pl.when(jnp.logical_not(earlier[d]))
        def _():
            pl.semaphore_wait(ready.at[d], 1)
            for copy in copies(d):
                copy.start()

    def wait_from(d):
        for copy in copies(d):
            copy.wait_recv()

    @pl.when(expected > 0)
    def _():
        pl.semaphore_wait(barrier, expected)

    for d in (EAST, NE, SE, WEST, NW, SW):
        send_to_earlier(d)
    for d in range(8):
        @pl.when(earlier[d])
        def _():
            pl.semaphore_signal(ready.at[DIRS.index((-DIRS[d][0], -DIRS[d][1]))], inc=1, device_id=peers[d], device_id_type=MESH)

    def tracer_x(k, carry):
        for r0 in range(0, ROWS, 16):
            q0, q1, gm2, gm1, g0, g1, g2 = x_parts(TS[k, pl.ds(PAD + r0, 16), :])
            XU[k, pl.ds(r0, 16), :] = q0 + correction(gm2, gm1, g0, g1)
            XD[k, pl.ds(r0, 16), :] = q1 - correction(g2, g1, g0, gm1)
        return carry

    lax.fori_loop(0, 8, tracer_x, 0)

    for d in (NORTH, SOUTH):
        send_to_earlier(d)
    for d in (NORTH, SOUTH, EAST, NE, SE):
        send_to_later(d)
    for d in (NORTH, SOUTH):
        wait_from(d)

    zero16 = jnp.zeros((16, COLS), F32)
    FY[pl.ds(SPAN, 8), :] = jnp.zeros((8, COLS), F32)

    @pl.when(lat == 0)
    def _():
        for k in range(8):
            UV[k, under, :] = zero16
            TS[k, under, :] = zero16
        WE[0, under, :] = zero16
        WE[1, under, :] = zero16

    @pl.when(lat == n_lat - 1)
    def _():
        for k in range(8):
            UV[k, over, :] = zero16
            TS[k, over, :] = zero16
        WE[0, over, :] = zero16
        WE[1, over, :] = zero16

    def tendency(q_plane, u_plane, v_plane, out):
        for r0 in range(0, SPAN, 8):
            base = LO - 1 + r0
            FY[pl.ds(r0, 8), :] = UV[v_plane, pl.ds(base, 8), :] * upwind_value(
                UV[v_plane, pl.ds(base, 8), :], *y_parts(UV, q_plane, base, 8))
        for r0 in range(0, SPAN, 16):
            flow = UV[u_plane, pl.ds(LO + r0, 16), :]
            flux = flow * upwind_value(flow, *x_parts(UV[q_plane, pl.ds(LO + r0, 16), :]))
            TEND[out, pl.ds(r0, 16), :] = -(flux - lanes(flux, 1) + (
                FY[pl.ds(r0 + 1, 16), :] - FY[pl.ds(r0, 16), :]))

    def momentum(k, carry):
        tendency(k, k, V_MAIN + k, k)
        tendency(V_MAIN + k, k, V_MAIN + k, V_MAIN + k)
        return carry

    lax.fori_loop(0, LEVELS, momentum, 0)

    def tracer_y(k, carry):
        for r0 in range(0, 40, 8):
            q0, q1, gm2, gm1, g0, g1, g2 = y_parts(TS, k, PAD - 1 + r0, 8)
            YU[k, pl.ds(r0, 8), :] = q0 + correction(gm2, gm1, g0, g1)
            YD[k, pl.ds(r0, 8), :] = q1 - correction(g2, g1, g0, gm1)
        return carry

    lax.fori_loop(0, 8, tracer_y, 0)

    for d in (WEST, NW, SW):
        send_to_later(d)
    for d in (EAST, WEST, NE, SE, NW, SW):
        wait_from(d)

    @pl.when(lat == 0)
    def _():
        for i in range(2):
            RW[i, under, :] = zero16
            RE[i, under, :] = zero16

    @pl.when(lat == n_lat - 1)
    def _():
        for i in range(2):
            RW[i, over, :] = zero16
            RE[i, over, :] = zero16

    lane64 = lax.broadcasted_iota(jnp.int32, (EXT, COLS), 1)
    half = lax.rem(lane64, 32) < 16
    ring_u = ring([UV[U_MAIN + k] for k in range(LEVELS)])
    ring_v = ring([UV[V_MAIN + k] for k in range(LEVELS)])
    UV[U_SW] = jnp.where(half, RW[0], ring_u)
    UV[V_SW] = jnp.where(half, lanes(RW[0], -16), ring_v)
    UV[U_SE] = jnp.where(half, ring_u, lanes(RE[0], 16))
    UV[V_SE] = jnp.where(half, ring_v, RE[0])

    def strips(i, carry):
        tendency(U_SW + i, U_SW + i, V_SW + i, U_SW + i)
        tendency(V_SW + i, U_SW + i, V_SW + i, V_SW + i)
        return carry

    lax.fori_loop(0, 2, strips, 0)

    lane = lax.broadcasted_iota(jnp.int32, (SPAN, COLS), 1)
    level = (lane // 32).astype(F32)
    BAND = pl.ds(LO, SPAN)

    def band(x):
        return x[LO:LO + SPAN]

    def joined(sw, main, se):
        return jnp.where(lane < 24, sw, jnp.where(lane < 64, lanes(main, 16), jnp.where(lane < 104, lanes(main, -16), se)))

    def shifted_up(x):
        return rows(x, -1)

    wet_main = WE[0]
    wet_own = lanes(wet_main, 16)
    wet_sw = spread(jnp.where(lane64 < 16, lanes(RW[1], -8), wet_own), 0)
    wet_se = spread(jnp.where(lane64 < 16, wet_own, lanes(RE[1], -8)), 0)
    eta_main = WE[1, BAND, :]
    eta_own = lanes(eta_main, 16)
    eta_side = joined(spread(jnp.where(lane < 16, lanes(RW[1, BAND, :], 8), eta_own), 0), eta_main,
                      spread(jnp.where(lane < 16, eta_own, lanes(RE[1, BAND, :], 8)), 0))

    def faces(w):
        here = band(w)
        return jnp.minimum(here, lanes(here, -1)), jnp.minimum(here, band(shifted_up(w)))

    wx_main, wy_main = faces(wet_main)
    wx_sw, wy_sw = faces(wet_sw)
    wx_se, wy_se = faces(wet_se)
    wx_side = joined(wx_sw, wx_main, wx_se)
    wy_side = joined(wy_sw, wy_main, wy_se)

    def main_sum(ref, first, where_rows, limit=None):
        total = None
        for k in range(LEVELS):
            term = ref[first + k, where_rows, :]
            if limit is not None:
                term = jnp.where(limit > k, term, 0.0)
            total = term if total is None else total + term
        return total

    def side_sum(ref, plane, where_rows, limit=None):
        term = ref[plane, where_rows, :]
        if limit is not None:
            term = jnp.where(limit > level, term, 0.0)
        return level_sum(term)

    ALL = pl.ds(0, SPAN)
    scale = STEP / SUB
    push_x = main_sum(TEND, U_MAIN, ALL, wx_main)
    push_y = main_sum(TEND, V_MAIN, ALL, wy_main)
    push_x_sw = side_sum(TEND, U_SW, ALL, wx_sw)
    push_x_se = side_sum(TEND, U_SE, ALL, wx_se)
    push_y_sw = side_sum(TEND, V_SW, ALL, wy_sw)
    push_y_se = side_sum(TEND, V_SE, ALL, wy_se)
    tx0 = main_sum(UV, U_MAIN, BAND)
    ty0 = main_sum(UV, V_MAIN, BAND)
    tx0_sw, tx0_se = side_sum(UV, U_SW, BAND), side_sum(UV, U_SE, BAND)
    ty0_sw, ty0_se = side_sum(UV, V_SW, BAND), side_sum(UV, V_SE, BAND)
    LOWER = pl.ds(LO - 1, SPAN)
    tym_main = main_sum(UV, V_MAIN, LOWER)
    tym_side = joined(side_sum(UV, V_SW, LOWER), tym_main, side_sum(UV, V_SE, LOWER))

    def substeps(height, tx, ty, tym, fx, fy, cx, cy):
        for n in range(SUB):
            below = tym if n == 0 else rows(ty, 1)
            height = height - (tx - lanes(tx, 1) + ty - below)
            tx = tx - cx * (lanes(height, -1) - height) + fx
            ty = ty - cy * (rows(height, -1) - height) + fy
        return height, tx, ty

    h_main, tx_main, ty_main = substeps(
        eta_main, tx0, ty0, tym_main, scale * push_x, scale * push_y, WAVE * wx_main, WAVE * wy_main)
    h_side, tx_side, ty_side = substeps(
        eta_side, joined(tx0_sw, tx0, tx0_se), joined(ty0_sw, ty0, ty0_se), tym_side,
        scale * joined(push_x_sw, push_x, push_x_se), scale * joined(push_y_sw, push_y, push_y_se),
        WAVE * wx_side, WAVE * wy_side)

    own = slice(PAD - LO, PAD - LO + ROWS)
    result[16] = jnp.where(lane < 16, lanes(h_side, -16), jnp.where(lane >= 112, lanes(h_side, 16), h_main))[own]

    def fresh_side(flow_plane, tend_plane, total, depth, trans):
        safe = jnp.maximum(depth, 1.0)
        step = UV[flow_plane, BAND, :] + STEP * TEND[tend_plane, ALL, :]
        return jnp.where(depth > level, step + (trans - total) / safe, 0.0)

    def total_of(trans0, push):
        return trans0 + STEP * push

    u_sw = fresh_side(U_SW, U_SW, total_of(tx0_sw, push_x_sw), wx_sw, spread(tx_side, 0))
    u_se = fresh_side(U_SE, U_SE, total_of(tx0_se, push_x_se), wx_se, spread(tx_side, 96))
    v_sw = fresh_side(V_SW, V_SW, total_of(ty0_sw, push_y_sw), wy_sw, spread(ty_side, 0))
    v_se = fresh_side(V_SE, V_SE, total_of(ty0_se, push_y_se), wy_se, spread(ty_side, 96))

    gain_x = (tx_main - total_of(tx0, push_x)) / jnp.maximum(wx_main, 1.0)
    gain_y = (ty_main - total_of(ty0, push_y)) / jnp.maximum(wy_main, 1.0)
    for k in range(LEVELS):
        fresh = jnp.where(wx_main > k, UV[U_MAIN + k, BAND, :] + STEP * TEND[U_MAIN + k, ALL, :] + gain_x, 0.0)
        fresh = jnp.where(lane < 12, lanes(u_sw, -(32 * k + 16)), jnp.where(lane >= 116, lanes(u_se, 112 - 32 * k), fresh))
        NU[k] = fresh[own]
        result[k] = fresh[own]
        fresh = jnp.where(wy_main > k, UV[V_MAIN + k, BAND, :] + STEP * TEND[V_MAIN + k, ALL, :] + gain_y, 0.0)
        fresh = jnp.where(lane < 12, lanes(v_sw, -(32 * k + 16)), jnp.where(lane >= 116, lanes(v_se, 112 - 32 * k), fresh))
        NV[k] = fresh
        result[4 + k] = fresh[own]

    ring_t = ring([TS[k, OWN, :] for k in range(LEVELS)])
    ring_s = ring([TS[4 + k, OWN, :] for k in range(LEVELS)])

    def side_flux(cells, flow):
        flux = flow * upwind_value(flow, *x_parts(cells))
        return flux - lanes(flux, 1)

    XS[0] = side_flux(jnp.where(half32, RW[1, OWN, :], ring_t), u_sw[own])
    XS[1] = side_flux(jnp.where(half32, ring_t, lanes(RE[1, OWN, :], 16)), u_se[own])
    XS[2] = side_flux(jnp.where(half32, lanes(RW[1, OWN, :], -16), ring_s), u_sw[own])
    XS[3] = side_flux(jnp.where(half32, ring_s, RE[1, OWN, :]), u_se[own])

    for field in range(2):
        for k in range(LEVELS):
            p = 4 * field + k
            flow = NU[k]
            flux = flow * jnp.where(flow >= 0.0, XU[p], XD[p])
            div_x = flux - lanes(flux, 1)
            div_x = jnp.where(lane32 < 8, lanes(XS[2 * field], -(32 * k + 16)),
                              jnp.where(lane32 >= 120, lanes(XS[2 * field + 1], 112 - 32 * k), div_x))
            up = NV[k, pl.ds(8, ROWS), :]
            down = NV[k, pl.ds(7, ROWS), :]
            flux_up = up * jnp.where(up >= 0.0, YU[p, pl.ds(1, ROWS), :], YD[p, pl.ds(1, ROWS), :])
            flux_down = down * jnp.where(down >= 0.0, YU[p, pl.ds(0, ROWS), :], YD[p, pl.ds(0, ROWS), :])
            cells = TS[p, OWN, :]
            fresh = cells - STEP * (div_x + (flux_up - flux_down))
            result[8 + p] = jnp.where(wet[0] > k, fresh, 0.0)

    for d in range(8):
        for copy in copies(d):
            copy.wait_send()


def deal(result, u_out, v_out, t_out, s_out, e_out):
    for i, out in enumerate((u_out, v_out, t_out, s_out)):
        for k in range(LEVELS):
            out[k] = result[LEVELS * i + k]
    e_out[...] = result[16]


def solution(mesh):
    n_lat, n_lon = mesh.shape["lat"], mesh.shape["lon"]

    def step(u_vel, v_vel, temp, salt, eta, wet_levels):
        levels = jax.ShapeDtypeStruct((LEVELS, ROWS, COLS), F32)
        plane = jax.ShapeDtypeStruct((ROWS, COLS), F32)
        hbm = pl.BlockSpec(memory_space=pl.ANY)
        vmem = pl.BlockSpec(memory_space=pltpu.VMEM)

        def body(*refs):
            kernel(n_lat, n_lon, *refs)

        def buffer(*shape):
            return pltpu.VMEM(shape, F32)

        result = pl.pallas_call(
            body,
            out_shape=jax.ShapeDtypeStruct((17, ROWS, COLS), F32),
            in_specs=[hbm] * 6,
            out_specs=vmem,
            scratch_shapes=[
                buffer(16, ROWS, COLS),
                buffer(ROWS, COLS),
                pltpu.VMEM((3, ROWS, COLS), jnp.int32),
                buffer(12, EXT, COLS),
                buffer(8, EXT, COLS),
                buffer(2, EXT, COLS),
                buffer(2, EXT, COLS),
                buffer(2, EXT, COLS),
                buffer(2, EXT, COLS),
                buffer(2, EXT, COLS),
                buffer(12, SPAN, COLS),
                buffer(SPAN + 8, COLS),
                buffer(8, ROWS, COLS),
                buffer(8, ROWS, COLS),
                buffer(8, 40, COLS),
                buffer(8, 40, COLS),
                buffer(4, SPAN, COLS),
                buffer(4, ROWS, COLS),
                buffer(4, ROWS, COLS),
                pltpu.SemaphoreType.DMA((6,)),
                pltpu.SemaphoreType.REGULAR((8,)),
                pltpu.SemaphoreType.DMA((12,)),
                pltpu.SemaphoreType.DMA((12,)),
            ],
            compiler_params=pltpu.CompilerParams(collective_id=0, has_side_effects=True),
        )(u_vel, v_vel, temp, salt, eta, wet_levels)
        return pl.pallas_call(
            deal,
            out_shape=(levels, levels, levels, levels, plane),
            in_specs=[vmem],
            out_specs=(vmem,) * 5,
        )(result)

    tile, flat = P(None, "lat", "lon"), P("lat", "lon")
    return jax.shard_map(
        step, mesh=mesh, in_specs=(tile, tile, tile, tile, flat, tile),
        out_specs=(tile, tile, tile, tile, flat), check_vma=False)
```

```python
import jax
import jax.numpy as jnp
from jax import lax
from jax.experimental import pallas as pl
from jax.experimental.pallas import tpu as pltpu
from jax.sharding import PartitionSpec as P

MESH = pl.DeviceIdType.MESH
F32 = jnp.float32
LEVELS = 4
SUB = 8
BLOCK = 8
STEP = 0.4
WAVE = 0.45 / 4
EPS = 1e-6 * 12.0 / 13.0
ROWS = 32
COLS = 128
PAD = 16
EXT = ROWS + 2 * PAD
LO = 8
SPAN = 48

U_MAIN, V_MAIN, U_SW, U_SE, V_SW, V_SE = 0, 4, 8, 9, 10, 11


def lanes(x, shift):
    shift = shift % COLS
    return x if shift == 0 else pltpu.roll(x, shift, 1)


def rows(x, shift):
    return pltpu.roll(x, shift % x.shape[0], 0)


def correction(d0, d1, d2, d3):
    x0 = d1 - d0
    x1 = d2 - d1
    x2 = d3 - d2
    m1 = d1 + d1
    m2 = d2 + d2
    y0 = x0 + m1
    y1 = d1 + d2
    y2 = x2 - m2
    e0 = x0 * x0 + (y0 * y0) * (3.0 / 13.0) + EPS
    e1 = x1 * x1 + (y1 * y1) * (3.0 / 13.0) + EPS
    e2 = x2 * x2 + (y2 * y2) * (3.0 / 13.0) + EPS
    a0 = e1 * e2
    a1 = e0 * e2
    a2 = e0 * e1
    w0 = a0 * a0
    w1 = (a1 * a1) * 6.0
    w2 = (a2 * a2) * 3.0
    top = w0 * (5.0 * d1 - 2.0 * d0) + w1 * (d1 + m2) + w2 * (4.0 * d2 - d3)
    return top / ((w0 + w1 + w2) * 6.0)


def upwind_value(flow, q0, q1, gm2, gm1, g0, g1, g2):
    ahead = flow >= 0.0
    fix = correction(jnp.where(ahead, gm2, g2), jnp.where(ahead, gm1, g1), g0, jnp.where(ahead, g1, gm1))
    return jnp.where(ahead, q0 + fix, q1 - fix)


def x_parts(q):
    q1 = lanes(q, -1)
    g = q1 - q
    return q, q1, lanes(g, 2), lanes(g, 1), g, lanes(g, -1), lanes(g, -2)


def y_parts(ref, k, r0, n):
    q = [ref[k, pl.ds(r0 + s, n), :] for s in range(-2, 4)]
    g = [q[i + 1] - q[i] for i in range(5)]
    return q[2], q[3], g[0], g[1], g[2], g[3], g[4]


def ring(parts):
    lane = lax.broadcasted_iota(jnp.int32, parts[0].shape, 1)
    out = lanes(parts[0], 16)
    for k in range(1, LEVELS):
        out = jnp.where(lane >= 32 * k, lanes(parts[k], 32 * k + 16), out)
    return out


def level_sum(x):
    y = x + lanes(x, 64)
    return y + lanes(y, 32)


def spread(x, start):
    lane = lax.broadcasted_iota(jnp.int32, x.shape, 1)
    return level_sum(jnp.where((lane >= start) & (lane < start + 32), x, 0.0))


DIRS = ((1, 0), (-1, 0), (0, 1), (0, -1), (1, 1), (-1, 1), (1, -1), (-1, -1))
NORTH, SOUTH, EAST, WEST, NE, SE, NW, SW = range(8)


def kernel(n_lat, n_lon, u_hbm, v_hbm, t_hbm, s_hbm, e_hbm, w_hbm,
           result,
           raw, raw2, wet, UV, TS, WE, PE, PW, RW, RE, HUB, KEPT,
           TEND, FY, XU, XD, YU, YD, NV, NU, XS,
           in_sem, ready, send_sem, recv_sem):
    lat = lax.axis_index("lat")
    lon = lax.axis_index("lon")

    def start_rank(i, j):
        group = j // BLOCK
        group = jnp.where(group == 2, 3, jnp.where(group == 3, 2, group))
        return (group * BLOCK + lax.rem(i, BLOCK)) * (n_lat * n_lon) + i * n_lon + j

    peers = [(lax.rem(lat + n_lat + di, n_lat), lax.rem(lon + n_lon + dj, n_lon)) for di, dj in DIRS]
    here = start_rank(lat, lon)
    earlier = [start_rank(*peer) < here for peer in peers]
    first_row, last_row = lax.rem(lat, BLOCK) == 0, lax.rem(lat, BLOCK) == BLOCK - 1
    first_column, last_column = lax.rem(lon, BLOCK) == 0, lax.rem(lon, BLOCK) == BLOCK - 1
    far_a = first_row & last_column
    far_b = last_row & first_column
    hub = first_row & first_column
    later = [jnp.logical_not(flag) for flag in earlier]
    for d, far in ((SE, far_a), (NW, far_b)):
        earlier[d] = earlier[d] & jnp.logical_not(far)
        later[d] = later[d] & jnp.logical_not(far)

    barrier = pltpu.get_barrier_semaphore()
    expected = 0
    for d in range(8):
        expected = expected + jnp.where(earlier[d], 1, 0)

        @pl.when(later[d])
        def _():
            pl.semaphore_signal(barrier, inc=1, device_id=peers[d], device_id_type=MESH)

    loads = [
        pltpu.make_async_copy(w_hbm, wet, in_sem.at[0]),
        pltpu.make_async_copy(u_hbm, raw.at[pl.ds(0, 4)], in_sem.at[1]),
        pltpu.make_async_copy(v_hbm, raw.at[pl.ds(4, 4)], in_sem.at[2]),
        pltpu.make_async_copy(t_hbm, raw.at[pl.ds(8, 4)], in_sem.at[3]),
        pltpu.make_async_copy(s_hbm, raw.at[pl.ds(12, 4)], in_sem.at[4]),
        pltpu.make_async_copy(e_hbm, raw2, in_sem.at[5]),
    ]
    for load in loads:
        load.start()
    for load in loads:
        load.wait()

    OWN = pl.ds(PAD, ROWS)
    for k in range(LEVELS):
        UV[U_MAIN + k, OWN, :] = jnp.where(wet[1] > k, raw[k], 0.0)
        UV[V_MAIN + k, OWN, :] = jnp.where(wet[2] > k, raw[4 + k], 0.0)
        TS[k, OWN, :] = jnp.where(wet[0] > k, raw[8 + k], 0.0)
        TS[4 + k, OWN, :] = jnp.where(wet[0] > k, raw[12 + k], 0.0)
    WE[0, OWN, :] = wet[0].astype(F32)
    WE[1, OWN, :] = raw2[...]

    lane32 = lax.broadcasted_iota(jnp.int32, (ROWS, COLS), 1)
    half32 = lax.rem(lane32, 32) < 16
    ring_u = ring([UV[U_MAIN + k, OWN, :] for k in range(LEVELS)])
    ring_v = ring([UV[V_MAIN + k, OWN, :] for k in range(LEVELS)])
    ring_t = ring([TS[k, OWN, :] for k in range(LEVELS)])
    ring_s = ring([TS[4 + k, OWN, :] for k in range(LEVELS)])
    eta8, wet24 = lanes(raw2[...], 8), lanes(wet[0].astype(F32), 24)
    PE[0, OWN, :] = jnp.where(half32, ring_u, lanes(ring_v, 16))
    PW[0, OWN, :] = jnp.where(half32, lanes(ring_u, -16), ring_v)
    PE[1, OWN, :] = jnp.where(lane32 < 8, eta8, jnp.where(
        (lane32 >= 16) & (lane32 < 24), wet24, jnp.where(half32, ring_t, lanes(ring_s, 16))))
    PW[1, OWN, :] = jnp.where((lane32 >= 8) & (lane32 < 16), eta8, jnp.where(
        (lane32 >= 24) & (lane32 < 32), wet24, jnp.where(half32, lanes(ring_t, -16), ring_s)))

    top, bottom = pl.ds(32, 16), pl.ds(16, 16)
    under, over = pl.ds(0, 16), pl.ds(48, 16)
    every = pl.ds(0, 8)
    parcels = {
        NORTH: [(UV.at[every, pl.ds(36, 12), :], UV.at[every, pl.ds(4, 12), :]),
                (WE.at[:, pl.ds(40, 8), :], WE.at[:, pl.ds(8, 8), :]),
                (TS.at[:, pl.ds(45, 3), :], TS.at[:, pl.ds(13, 3), :])],
        SOUTH: [(UV.at[every, pl.ds(16, 12), :], UV.at[every, pl.ds(48, 12), :]),
                (WE.at[:, pl.ds(16, 8), :], WE.at[:, pl.ds(48, 8), :]),
                (TS.at[:, pl.ds(16, 3), :], TS.at[:, pl.ds(48, 3), :])],
        EAST: [(PE.at[:, OWN, :], RW.at[:, OWN, :])],
        WEST: [(PW.at[:, OWN, :], RE.at[:, OWN, :])],
        NE: [(PE.at[:, pl.ds(36, 12), :], RW.at[:, pl.ds(4, 12), :])],
        SE: [(PE.at[:, pl.ds(16, 12), :], RW.at[:, pl.ds(48, 12), :])],
        NW: [(PW.at[:, pl.ds(36, 12), :], RE.at[:, pl.ds(4, 12), :])],
        SW: [(PW.at[:, pl.ds(16, 12), :], RE.at[:, pl.ds(48, 12), :])],
    }
    first_slot, slots = {}, 0
    for d in range(8):
        first_slot[d] = slots
        slots += len(parcels[d])

    def copies(d):
        return [
            pltpu.make_async_remote_copy(
                src_ref=src, dst_ref=dst, send_sem=send_sem.at[first_slot[d] + i], recv_sem=recv_sem.at[first_slot[d] + i],
                device_id=peers[d], device_id_type=MESH)
            for i, (src, dst) in enumerate(parcels[d])]

    def send_to_earlier(d):
        @pl.when(earlier[d])
        def _():
            for copy in copies(d):
                copy.start()

    def send_to_later(d):
        @pl.when(later[d])
        def _():
            pl.semaphore_wait(ready.at[d], 1)
            for copy in copies(d):
                copy.start()

    def wait_from(d):
        for copy in copies(d):
            copy.wait_recv()

    def extra(slot, src, dst, arrival, peer):
        return pltpu.make_async_remote_copy(
            src_ref=src, dst_ref=dst, send_sem=send_sem.at[slot], recv_sem=recv_sem.at[arrival],
            device_id=peer, device_id_type=MESH)

    to_hub = extra(slots, PW.at[:, pl.ds(36, 12), :], HUB.at[:, pl.ds(4, 12), :], slots, peers[NORTH])
    hub_west = extra(slots + 1, HUB.at[:, pl.ds(4, 12), :], RE.at[:, pl.ds(4, 12), :], first_slot[NW], peers[WEST])
    hub_south = extra(slots + 2, RW.at[:, pl.ds(16, 12), :], RW.at[:, pl.ds(48, 12), :], first_slot[SE], peers[SOUTH])

    @pl.when(expected > 0)
    def _():
        pl.semaphore_wait(barrier, expected)

    for d in range(8):
        @pl.when(earlier[d])
        def _():
            pl.semaphore_signal(ready.at[DIRS.index((-DIRS[d][0], -DIRS[d][1]))], inc=1, device_id=peers[d], device_id_type=MESH)

    for d in (EAST, NE, SE, WEST, NW, SW, NORTH, SOUTH):
        send_to_earlier(d)

    @pl.when(far_b & earlier[NORTH])
    def _():
        to_hub.start()

    def flux_x(q_plane, u_plane, r0, n):
        flow = UV[u_plane, pl.ds(r0, n), :]
        flux = flow * upwind_value(flow, *x_parts(UV[q_plane, pl.ds(r0, n), :]))
        return flux - lanes(flux, 1)

    def flux_y(q_plane, v_plane, r0):
        flow = UV[v_plane, pl.ds(r0, 8), :]
        return flow * upwind_value(flow, *y_parts(UV, q_plane, r0, 8))

    def put_x(q_plane, u_plane, r0, n):
        TEND[q_plane, pl.ds(r0 - LO, n), :] = flux_x(q_plane, u_plane, r0, n)

    def put_y(q_plane, v_plane, r0):
        FY[q_plane, pl.ds(r0 - LO + 1, 8), :] = flux_y(q_plane, v_plane, r0)

    def combine(q_plane):
        for r0 in range(0, SPAN, 16):
            TEND[q_plane, pl.ds(r0, 16), :] = -(TEND[q_plane, pl.ds(r0, 16), :] + (
                FY[q_plane, pl.ds(r0 + 1, 16), :] - FY[q_plane, pl.ds(r0, 16), :]))

    def tracer_x(k, r0, n):
        q0, q1, gm2, gm1, g0, g1, g2 = x_parts(TS[k, pl.ds(PAD + r0, n), :])
        XU[k, pl.ds(r0, n), :] = q0 + correction(gm2, gm1, g0, g1)
        XD[k, pl.ds(r0, n), :] = q1 - correction(g2, g1, g0, gm1)

    def tracer_y(k, r0):
        q0, q1, gm2, gm1, g0, g1, g2 = y_parts(TS, k, PAD - 1 + r0, 8)
        YU[k, pl.ds(r0, 8), :] = q0 + correction(gm2, gm1, g0, g1)
        YD[k, pl.ds(r0, 8), :] = q1 - correction(g2, g1, g0, gm1)

    def local_part(k, carry):
        plane = lax.rem(k, LEVELS)
        for r0 in (16, 32):
            put_x(k, plane, r0, 16)
        for r0 in (23, 31):
            put_y(k, V_MAIN + plane, r0)
        for r0 in (0, 16):
            tracer_x(k, r0, 16)
        for r0 in (8, 16):
            tracer_y(k, r0)
        return carry

    lax.fori_loop(0, 8, local_part, 0)

    for d in (NORTH, SOUTH, EAST, NE, SE):
        send_to_later(d)

    @pl.when(far_b & later[NORTH])
    def _():
        to_hub.start()

    for d in (NORTH, SOUTH):
        wait_from(d)

    zero16 = jnp.zeros((16, COLS), F32)

    @pl.when(lat == 0)
    def _():
        for k in range(8):
            UV[k, under, :] = zero16
            TS[k, under, :] = zero16
        WE[0, under, :] = zero16
        WE[1, under, :] = zero16

    @pl.when(lat == n_lat - 1)
    def _():
        for k in range(8):
            UV[k, over, :] = zero16
            TS[k, over, :] = zero16
        WE[0, over, :] = zero16
        WE[1, over, :] = zero16

    def edge_part(k, carry):
        plane = lax.rem(k, LEVELS)
        for r0 in (8, 48):
            put_x(k, plane, r0, 8)
        for r0 in (7, 15, 39, 47):
            put_y(k, V_MAIN + plane, r0)
        combine(k)
        for r0 in (0, 24, 32):
            tracer_y(k, r0)
        return carry

    lax.fori_loop(0, 8, edge_part, 0)

    lane64 = lax.broadcasted_iota(jnp.int32, (EXT, COLS), 1)
    half = lax.rem(lane64, 32) < 16
    lane = lax.broadcasted_iota(jnp.int32, (SPAN, COLS), 1)
    level = (lane // 32).astype(F32)
    BAND = pl.ds(LO, SPAN)
    LOWER = pl.ds(LO - 1, SPAN)
    ALL = pl.ds(0, SPAN)
    scale = STEP / SUB
    own = slice(PAD - LO, PAD - LO + ROWS)

    def band(x):
        return x[LO:LO + SPAN]

    def joined(sw, main, se):
        return jnp.where(lane < 24, sw, jnp.where(lane < 64, lanes(main, 16), jnp.where(lane < 104, lanes(main, -16), se)))

    def faces(w):
        at = band(w)
        return jnp.minimum(at, lanes(at, -1)), jnp.minimum(at, band(rows(w, -1)))

    def main_sum(ref, first, where_rows, limit=None):
        total = None
        for k in range(LEVELS):
            term = ref[first + k, where_rows, :]
            if limit is not None:
                term = jnp.where(limit > k, term, 0.0)
            total = term if total is None else total + term
        return total

    def side_sum(ref, plane, where_rows, limit=None):
        term = ref[plane, where_rows, :]
        if limit is not None:
            term = jnp.where(limit > level, term, 0.0)
        return level_sum(term)

    def substeps(height, tx, ty, tym, fx, fy, cx, cy):
        for n in range(SUB):
            below = tym if n == 0 else rows(ty, 1)
            height = height - (tx - lanes(tx, 1) + ty - below)
            tx = tx - cx * (lanes(height, -1) - height) + fx
            ty = ty - cy * (rows(height, -1) - height) + fy
        return height, tx, ty

    wx_main, wy_main = faces(WE[0])
    push_x = main_sum(TEND, U_MAIN, ALL, wx_main)
    push_y = main_sum(TEND, V_MAIN, ALL, wy_main)
    tx0 = main_sum(UV, U_MAIN, BAND)
    ty0 = main_sum(UV, V_MAIN, BAND)
    tym_main = main_sum(UV, V_MAIN, LOWER)
    h_main, tx_main, ty_main = substeps(
        WE[1, BAND, :], tx0, ty0, tym_main, scale * push_x, scale * push_y, WAVE * wx_main, WAVE * wy_main)
    gain_x = (tx_main - (tx0 + STEP * push_x)) / jnp.maximum(wx_main, 1.0)
    gain_y = (ty_main - (ty0 + STEP * push_y)) / jnp.maximum(wy_main, 1.0)
    for k in range(LEVELS):
        NU[k] = jnp.where(wx_main > k, UV[U_MAIN + k, BAND, :] + STEP * TEND[U_MAIN + k, ALL, :] + gain_x, 0.0)[own]
        NV[k] = jnp.where(wy_main > k, UV[V_MAIN + k, BAND, :] + STEP * TEND[V_MAIN + k, ALL, :] + gain_y, 0.0)
    for slot, plane in enumerate((
            h_main, joined(tx0, tx0, tx0), joined(ty0, ty0, ty0), joined(tym_main, tym_main, tym_main),
            joined(push_x, push_x, push_x), joined(push_y, push_y, push_y),
            joined(wx_main, wx_main, wx_main), joined(wy_main, wy_main, wy_main))):
        KEPT[slot] = plane
    rings = [ring([UV[first + k] for k in range(LEVELS)]) for first in (U_MAIN, V_MAIN)]
    UV[U_SW] = rings[0]
    UV[V_SW] = rings[1]

    for d in (WEST, NW, SW):
        send_to_later(d)

    @pl.when(hub)
    def _():
        to_hub.wait_recv()
        hub_west.start()

    wait_from(EAST)

    @pl.when(hub)
    def _():
        hub_south.start()

    for d in (WEST, NE, SE, NW, SW):
        wait_from(d)

    @pl.when(lat == 0)
    def _():
        for i in range(2):
            RW[i, under, :] = zero16
            RE[i, under, :] = zero16

    @pl.when(lat == n_lat - 1)
    def _():
        for i in range(2):
            RW[i, over, :] = zero16
            RE[i, over, :] = zero16

    ring_u, ring_v = UV[U_SW], UV[V_SW]
    UV[U_SE] = jnp.where(half, ring_u, lanes(RE[0], 16))
    UV[V_SE] = jnp.where(half, ring_v, RE[0])
    UV[U_SW] = jnp.where(half, RW[0], ring_u)
    UV[V_SW] = jnp.where(half, lanes(RW[0], -16), ring_v)

    def strips(i, carry):
        for q_plane in (U_SW + i, V_SW + i):
            for r0 in (8, 24, 40):
                put_x(q_plane, U_SW + i, r0, 16)
            for r0 in (7, 15, 23, 31, 39, 47):
                put_y(q_plane, V_SW + i, r0)
            combine(q_plane)
        return carry

    lax.fori_loop(0, 2, strips, 0)

    def kept(slot, sw, se):
        return jnp.where(lane < 24, sw, jnp.where(lane >= 104, se, KEPT[slot]))

    wet_own = lanes(WE[0], 16)
    wx_sw, wy_sw = faces(spread(jnp.where(lane64 < 16, lanes(RW[1], -8), wet_own), 0))
    wx_se, wy_se = faces(spread(jnp.where(lane64 < 16, wet_own, lanes(RE[1], -8)), 0))
    eta_main = WE[1, BAND, :]
    eta_own = lanes(eta_main, 16)
    eta_side = joined(spread(jnp.where(lane < 16, lanes(RW[1, BAND, :], 8), eta_own), 0), eta_main,
                      spread(jnp.where(lane < 16, eta_own, lanes(RE[1, BAND, :], 8)), 0))

    push_x_sw = side_sum(TEND, U_SW, ALL, wx_sw)
    push_x_se = side_sum(TEND, U_SE, ALL, wx_se)
    push_y_sw = side_sum(TEND, V_SW, ALL, wy_sw)
    push_y_se = side_sum(TEND, V_SE, ALL, wy_se)
    tx0_sw, tx0_se = side_sum(UV, U_SW, BAND), side_sum(UV, U_SE, BAND)
    ty0_sw, ty0_se = side_sum(UV, V_SW, BAND), side_sum(UV, V_SE, BAND)

    h_side, tx_side, ty_side = substeps(
        eta_side, kept(1, tx0_sw, tx0_se), kept(2, ty0_sw, ty0_se),
        kept(3, side_sum(UV, V_SW, LOWER), side_sum(UV, V_SE, LOWER)),
        scale * kept(4, push_x_sw, push_x_se), scale * kept(5, push_y_sw, push_y_se),
        WAVE * kept(6, wx_sw, wx_se), WAVE * kept(7, wy_sw, wy_se))

    result[16] = jnp.where(lane < 16, lanes(h_side, -16), jnp.where(lane >= 112, lanes(h_side, 16), KEPT[0]))[own]

    def fresh_side(plane, trans0, push, depth, trans):
        step = UV[plane, BAND, :] + STEP * TEND[plane, ALL, :]
        return jnp.where(depth > level, step + (trans - (trans0 + STEP * push)) / jnp.maximum(depth, 1.0), 0.0)

    u_sw = fresh_side(U_SW, tx0_sw, push_x_sw, wx_sw, spread(tx_side, 0))[own]
    u_se = fresh_side(U_SE, tx0_se, push_x_se, wx_se, spread(tx_side, 96))[own]
    v_sw = fresh_side(V_SW, ty0_sw, push_y_sw, wy_sw, spread(ty_side, 0))
    v_se = fresh_side(V_SE, ty0_se, push_y_se, wy_se, spread(ty_side, 96))

    for k in range(LEVELS):
        fresh = jnp.where(lane32 < 12, lanes(u_sw, -(32 * k + 16)), jnp.where(lane32 >= 116, lanes(u_se, 112 - 32 * k), NU[k]))
        NU[k] = fresh
        result[k] = fresh
        fresh = jnp.where(lane < 12, lanes(v_sw, -(32 * k + 16)), jnp.where(lane >= 116, lanes(v_se, 112 - 32 * k), NV[k]))
        NV[k] = fresh
        result[4 + k] = fresh[own]

    ring_t = ring([TS[k, OWN, :] for k in range(LEVELS)])
    ring_s = ring([TS[4 + k, OWN, :] for k in range(LEVELS)])

    def side_flux(cells, flow):
        flux = flow * upwind_value(flow, *x_parts(cells))
        return flux - lanes(flux, 1)

    XS[0] = side_flux(jnp.where(half32, RW[1, OWN, :], ring_t), u_sw)
    XS[1] = side_flux(jnp.where(half32, ring_t, lanes(RE[1, OWN, :], 16)), u_se)
    XS[2] = side_flux(jnp.where(half32, lanes(RW[1, OWN, :], -16), ring_s), u_sw)
    XS[3] = side_flux(jnp.where(half32, ring_s, RE[1, OWN, :]), u_se)

    for field in range(2):
        for k in range(LEVELS):
            p = 4 * field + k
            flow = NU[k]
            flux = flow * jnp.where(flow >= 0.0, XU[p], XD[p])
            div_x = flux - lanes(flux, 1)
            div_x = jnp.where(lane32 < 8, lanes(XS[2 * field], -(32 * k + 16)),
                              jnp.where(lane32 >= 120, lanes(XS[2 * field + 1], 112 - 32 * k), div_x))
            up = NV[k, pl.ds(8, ROWS), :]
            down = NV[k, pl.ds(7, ROWS), :]
            flux_up = up * jnp.where(up >= 0.0, YU[p, pl.ds(1, ROWS), :], YD[p, pl.ds(1, ROWS), :])
            flux_down = down * jnp.where(down >= 0.0, YU[p, pl.ds(0, ROWS), :], YD[p, pl.ds(0, ROWS), :])
            cells = TS[p, OWN, :]
            fresh = cells - STEP * (div_x + (flux_up - flux_down))
            result[8 + p] = jnp.where(wet[0] > k, fresh, 0.0)

    for d in range(8):
        if d in (SE, NW):
            @pl.when(earlier[d] | later[d])
            def _():
                for copy in copies(d):
                    copy.wait_send()
        else:
            for copy in copies(d):
                copy.wait_send()

    @pl.when(hub)
    def _():
        hub_west.wait_send()
        hub_south.wait_send()

    @pl.when(far_b)
    def _():
        to_hub.wait_send()


def deal(result, u_out, v_out, t_out, s_out, e_out):
    for i, out in enumerate((u_out, v_out, t_out, s_out)):
        for k in range(LEVELS):
            out[k] = result[LEVELS * i + k]
    e_out[...] = result[16]


def solution(mesh):
    n_lat, n_lon = mesh.shape["lat"], mesh.shape["lon"]

    def step(u_vel, v_vel, temp, salt, eta, wet_levels):
        levels = jax.ShapeDtypeStruct((LEVELS, ROWS, COLS), F32)
        plane = jax.ShapeDtypeStruct((ROWS, COLS), F32)
        hbm = pl.BlockSpec(memory_space=pl.ANY)
        vmem = pl.BlockSpec(memory_space=pltpu.VMEM)

        def body(*refs):
            kernel(n_lat, n_lon, *refs)

        def buffer(*shape):
            return pltpu.VMEM(shape, F32)

        result = pl.pallas_call(
            body,
            out_shape=jax.ShapeDtypeStruct((17, ROWS, COLS), F32),
            in_specs=[hbm] * 6,
            out_specs=vmem,
            scratch_shapes=[
                buffer(16, ROWS, COLS),
                buffer(ROWS, COLS),
                pltpu.VMEM((3, ROWS, COLS), jnp.int32),
                buffer(12, EXT, COLS),
                buffer(8, EXT, COLS),
                buffer(2, EXT, COLS),
                buffer(2, EXT, COLS),
                buffer(2, EXT, COLS),
                buffer(2, EXT, COLS),
                buffer(2, EXT, COLS),
                buffer(2, PAD, COLS),
                buffer(8, SPAN, COLS),
                buffer(12, SPAN, COLS),
                buffer(12, SPAN + 8, COLS),
                buffer(8, ROWS, COLS),
                buffer(8, ROWS, COLS),
                buffer(8, 40, COLS),
                buffer(8, 40, COLS),
                buffer(4, SPAN, COLS),
                buffer(4, ROWS, COLS),
                buffer(4, ROWS, COLS),
                pltpu.SemaphoreType.DMA((6,)),
                pltpu.SemaphoreType.REGULAR((8,)),
                pltpu.SemaphoreType.DMA((15,)),
                pltpu.SemaphoreType.DMA((15,)),
            ],
            compiler_params=pltpu.CompilerParams(collective_id=0, has_side_effects=True),
        )(u_vel, v_vel, temp, salt, eta, wet_levels)
        return pl.pallas_call(
            deal,
            out_shape=(levels, levels, levels, levels, plane),
            in_specs=[vmem],
            out_specs=(vmem,) * 5,
        )(result)

    tile, flat = P(None, "lat", "lon"), P("lat", "lon")
    return jax.shard_map(
        step, mesh=mesh, in_specs=(tile, tile, tile, tile, flat, tile),
        out_specs=(tile, tile, tile, tile, flat), check_vma=False)
```

```python
import jax
import jax.numpy as jnp
from jax import lax
from jax.experimental import pallas as pl
from jax.experimental.pallas import tpu as pltpu
from jax.sharding import PartitionSpec as P

MESH = pl.DeviceIdType.MESH
F32 = jnp.float32
LEVELS = 4
SUB = 8
BLOCK = 8
RELAYED_FROM = 2
STEP = 0.4
WAVE = 0.45 / 4
EPS = 1e-6 * 12.0 / 13.0
ROWS = 32
COLS = 128
PAD = 16
EXT = ROWS + 2 * PAD
LO = 8
SPAN = 48

U_MAIN, V_MAIN, U_SW, U_SE, V_SW, V_SE = 0, 4, 8, 9, 10, 11


def lanes(x, shift):
    shift = shift % COLS
    return x if shift == 0 else pltpu.roll(x, shift, 1)


def rows(x, shift):
    return pltpu.roll(x, shift % x.shape[0], 0)


def correction(d0, d1, d2, d3):
    x0 = d1 - d0
    x1 = d2 - d1
    x2 = d3 - d2
    m1 = d1 + d1
    m2 = d2 + d2
    y0 = x0 + m1
    y1 = d1 + d2
    y2 = x2 - m2
    e0 = x0 * x0 + (y0 * y0) * (3.0 / 13.0) + EPS
    e1 = x1 * x1 + (y1 * y1) * (3.0 / 13.0) + EPS
    e2 = x2 * x2 + (y2 * y2) * (3.0 / 13.0) + EPS
    a0 = e1 * e2
    a1 = e0 * e2
    a2 = e0 * e1
    w0 = a0 * a0
    w1 = (a1 * a1) * 6.0
    w2 = (a2 * a2) * 3.0
    top = w0 * (5.0 * d1 - 2.0 * d0) + w1 * (d1 + m2) + w2 * (4.0 * d2 - d3)
    return top / ((w0 + w1 + w2) * 6.0)


def upwind_value(flow, q0, q1, gm2, gm1, g0, g1, g2):
    ahead = flow >= 0.0
    fix = correction(jnp.where(ahead, gm2, g2), jnp.where(ahead, gm1, g1), g0, jnp.where(ahead, g1, gm1))
    return jnp.where(ahead, q0 + fix, q1 - fix)


def x_parts(q):
    q1 = lanes(q, -1)
    g = q1 - q
    return q, q1, lanes(g, 2), lanes(g, 1), g, lanes(g, -1), lanes(g, -2)


def y_parts(ref, k, r0, n):
    q = [ref[k, pl.ds(r0 + s, n), :] for s in range(-2, 4)]
    g = [q[i + 1] - q[i] for i in range(5)]
    return q[2], q[3], g[0], g[1], g[2], g[3], g[4]


def ring(parts):
    lane = lax.broadcasted_iota(jnp.int32, parts[0].shape, 1)
    out = lanes(parts[0], 16)
    for k in range(1, LEVELS):
        out = jnp.where(lane >= 32 * k, lanes(parts[k], 32 * k + 16), out)
    return out


def level_sum(x):
    y = x + lanes(x, 64)
    return y + lanes(y, 32)


def spread(x, start):
    lane = lax.broadcasted_iota(jnp.int32, x.shape, 1)
    return level_sum(jnp.where((lane >= start) & (lane < start + 32), x, 0.0))


DIRS = ((1, 0), (-1, 0), (0, 1), (0, -1), (1, 1), (-1, 1), (1, -1), (-1, -1))
NORTH, SOUTH, EAST, WEST, NE, SE, NW, SW = range(8)


def kernel(n_lat, n_lon, u_hbm, v_hbm, t_hbm, s_hbm, e_hbm, w_hbm,
           result,
           raw, raw2, wet, UV, TS, WE, PE, PW, RW, RE, HUB, KEPT,
           TEND, FY, XU, XD, YU, YD, NV, NU, XS,
           in_sem, ready, send_sem, recv_sem):
    lat = lax.axis_index("lat")
    lon = lax.axis_index("lon")

    def start_rank(i, j):
        group = j // BLOCK
        group = jnp.where(group == 2, 3, jnp.where(group == 3, 2, group))
        rank = (group * BLOCK + lax.rem(i, BLOCK)) * (n_lat * n_lon) + i * n_lon + j
        return jnp.where((i == 0) & (j == 0), 2 * BLOCK * n_lat * n_lon - 1, rank)

    peers = [(lax.rem(lat + n_lat + di, n_lat), lax.rem(lon + n_lon + dj, n_lon)) for di, dj in DIRS]
    here = start_rank(lat, lon)
    earlier = [start_rank(*peer) < here for peer in peers]
    first_row, last_row = lax.rem(lat, BLOCK) == 0, lax.rem(lat, BLOCK) == BLOCK - 1
    first_column, last_column = lax.rem(lon, BLOCK) == 0, lax.rem(lon, BLOCK) == BLOCK - 1
    west_relayed = peers[WEST][1] // BLOCK >= RELAYED_FROM
    far_a = first_row & last_column & (lon // BLOCK >= RELAYED_FROM)
    far_b = last_row & first_column & west_relayed
    hub = first_row & first_column & west_relayed
    later = [jnp.logical_not(flag) for flag in earlier]
    for d, far in ((SE, far_a), (NW, far_b)):
        earlier[d] = earlier[d] & jnp.logical_not(far)
        later[d] = later[d] & jnp.logical_not(far)

    barrier = pltpu.get_barrier_semaphore()
    expected = 0
    for d in range(8):
        expected = expected + jnp.where(earlier[d], 1, 0)

        @pl.when(later[d])
        def _():
            pl.semaphore_signal(barrier, inc=1, device_id=peers[d], device_id_type=MESH)

    loads = [
        pltpu.make_async_copy(w_hbm, wet, in_sem.at[0]),
        pltpu.make_async_copy(u_hbm, raw.at[pl.ds(0, 4)], in_sem.at[1]),
        pltpu.make_async_copy(v_hbm, raw.at[pl.ds(4, 4)], in_sem.at[2]),
        pltpu.make_async_copy(t_hbm, raw.at[pl.ds(8, 4)], in_sem.at[3]),
        pltpu.make_async_copy(s_hbm, raw.at[pl.ds(12, 4)], in_sem.at[4]),
        pltpu.make_async_copy(e_hbm, raw2, in_sem.at[5]),
    ]
    for load in loads:
        load.start()
    for load in loads:
        load.wait()

    OWN = pl.ds(PAD, ROWS)
    for k in range(LEVELS):
        UV[U_MAIN + k, OWN, :] = jnp.where(wet[1] > k, raw[k], 0.0)
        UV[V_MAIN + k, OWN, :] = jnp.where(wet[2] > k, raw[4 + k], 0.0)
        TS[k, OWN, :] = jnp.where(wet[0] > k, raw[8 + k], 0.0)
        TS[4 + k, OWN, :] = jnp.where(wet[0] > k, raw[12 + k], 0.0)
    WE[0, OWN, :] = wet[0].astype(F32)
    WE[1, OWN, :] = raw2[...]

    lane32 = lax.broadcasted_iota(jnp.int32, (ROWS, COLS), 1)
    half32 = lax.rem(lane32, 32) < 16
    ring_u = ring([UV[U_MAIN + k, OWN, :] for k in range(LEVELS)])
    ring_v = ring([UV[V_MAIN + k, OWN, :] for k in range(LEVELS)])
    ring_t = ring([TS[k, OWN, :] for k in range(LEVELS)])
    ring_s = ring([TS[4 + k, OWN, :] for k in range(LEVELS)])
    eta8, wet24 = lanes(raw2[...], 8), lanes(wet[0].astype(F32), 24)
    PE[0, OWN, :] = jnp.where(half32, ring_u, lanes(ring_v, 16))
    PW[0, OWN, :] = jnp.where(half32, lanes(ring_u, -16), ring_v)
    PE[1, OWN, :] = jnp.where(lane32 < 8, eta8, jnp.where(
        (lane32 >= 16) & (lane32 < 24), wet24, jnp.where(half32, ring_t, lanes(ring_s, 16))))
    PW[1, OWN, :] = jnp.where((lane32 >= 8) & (lane32 < 16), eta8, jnp.where(
        (lane32 >= 24) & (lane32 < 32), wet24, jnp.where(half32, lanes(ring_t, -16), ring_s)))

    top, bottom = pl.ds(32, 16), pl.ds(16, 16)
    under, over = pl.ds(0, 16), pl.ds(48, 16)
    every = pl.ds(0, 8)
    parcels = {
        NORTH: [(UV.at[every, pl.ds(36, 12), :], UV.at[every, pl.ds(4, 12), :]),
                (WE.at[:, pl.ds(40, 8), :], WE.at[:, pl.ds(8, 8), :]),
                (TS.at[:, pl.ds(45, 3), :], TS.at[:, pl.ds(13, 3), :])],
        SOUTH: [(UV.at[every, pl.ds(16, 12), :], UV.at[every, pl.ds(48, 12), :]),
                (WE.at[:, pl.ds(16, 8), :], WE.at[:, pl.ds(48, 8), :]),
                (TS.at[:, pl.ds(16, 3), :], TS.at[:, pl.ds(48, 3), :])],
        EAST: [(PE.at[:, OWN, :], RW.at[:, OWN, :])],
        WEST: [(PW.at[:, OWN, :], RE.at[:, OWN, :])],
        NE: [(PE.at[:, pl.ds(36, 12), :], RW.at[:, pl.ds(4, 12), :])],
        SE: [(PE.at[:, pl.ds(16, 12), :], RW.at[:, pl.ds(48, 12), :])],
        NW: [(PW.at[:, pl.ds(36, 12), :], RE.at[:, pl.ds(4, 12), :])],
        SW: [(PW.at[:, pl.ds(16, 12), :], RE.at[:, pl.ds(48, 12), :])],
    }
    first_slot, slots = {}, 0
    for d in range(8):
        first_slot[d] = slots
        slots += len(parcels[d])

    def copies(d):
        return [
            pltpu.make_async_remote_copy(
                src_ref=src, dst_ref=dst, send_sem=send_sem.at[first_slot[d] + i], recv_sem=recv_sem.at[first_slot[d] + i],
                device_id=peers[d], device_id_type=MESH)
            for i, (src, dst) in enumerate(parcels[d])]

    def send_to_earlier(d):
        @pl.when(earlier[d])
        def _():
            for copy in copies(d):
                copy.start()

    def send_to_later(d, also=True):
        @pl.when(later[d] & also)
        def _():
            pl.semaphore_wait(ready.at[d], 1)
            for copy in copies(d):
                copy.start()

    def wait_from(d):
        for copy in copies(d):
            copy.wait_recv()

    def extra(slot, src, dst, arrival, peer):
        return pltpu.make_async_remote_copy(
            src_ref=src, dst_ref=dst, send_sem=send_sem.at[slot], recv_sem=recv_sem.at[arrival],
            device_id=peer, device_id_type=MESH)

    to_hub = extra(slots, PW.at[:, pl.ds(36, 12), :], HUB.at[:, pl.ds(4, 12), :], slots, peers[NORTH])
    hub_west = extra(slots + 1, HUB.at[:, pl.ds(4, 12), :], RE.at[:, pl.ds(4, 12), :], first_slot[NW], peers[WEST])
    hub_south = extra(slots + 2, RW.at[:, pl.ds(16, 12), :], RW.at[:, pl.ds(48, 12), :], first_slot[SE], peers[SOUTH])

    @pl.when(expected > 0)
    def _():
        pl.semaphore_wait(barrier, expected)

    for d in range(8):
        @pl.when(earlier[d])
        def _():
            pl.semaphore_signal(ready.at[DIRS.index((-DIRS[d][0], -DIRS[d][1]))], inc=1, device_id=peers[d], device_id_type=MESH)

    for d in (EAST, NE, SE, WEST, NW, SW, NORTH, SOUTH):
        send_to_earlier(d)

    @pl.when(far_b & earlier[NORTH])
    def _():
        to_hub.start()

    def flux_x(q_plane, u_plane, r0, n):
        flow = UV[u_plane, pl.ds(r0, n), :]
        flux = flow * upwind_value(flow, *x_parts(UV[q_plane, pl.ds(r0, n), :]))
        return flux - lanes(flux, 1)

    def flux_y(q_plane, v_plane, r0):
        flow = UV[v_plane, pl.ds(r0, 8), :]
        return flow * upwind_value(flow, *y_parts(UV, q_plane, r0, 8))

    def put_x(q_plane, u_plane, r0, n):
        TEND[q_plane, pl.ds(r0 - LO, n), :] = flux_x(q_plane, u_plane, r0, n)

    def put_y(q_plane, v_plane, r0):
        FY[q_plane, pl.ds(r0 - LO + 1, 8), :] = flux_y(q_plane, v_plane, r0)

    def combine(q_plane):
        for r0 in range(0, SPAN, 16):
            TEND[q_plane, pl.ds(r0, 16), :] = -(TEND[q_plane, pl.ds(r0, 16), :] + (
                FY[q_plane, pl.ds(r0 + 1, 16), :] - FY[q_plane, pl.ds(r0, 16), :]))

    def tracer_x(k, r0, n):
        q0, q1, gm2, gm1, g0, g1, g2 = x_parts(TS[k, pl.ds(PAD + r0, n), :])
        XU[k, pl.ds(r0, n), :] = q0 + correction(gm2, gm1, g0, g1)
        XD[k, pl.ds(r0, n), :] = q1 - correction(g2, g1, g0, gm1)

    def tracer_y(k, r0):
        q0, q1, gm2, gm1, g0, g1, g2 = y_parts(TS, k, PAD - 1 + r0, 8)
        YU[k, pl.ds(r0, 8), :] = q0 + correction(gm2, gm1, g0, g1)
        YD[k, pl.ds(r0, 8), :] = q1 - correction(g2, g1, g0, gm1)

    def local_part(k, carry):
        plane = lax.rem(k, LEVELS)
        for r0 in (16, 32):
            put_x(k, plane, r0, 16)
        for r0 in (23, 31):
            put_y(k, V_MAIN + plane, r0)
        for r0 in (0, 16):
            tracer_x(k, r0, 16)
        for r0 in (8, 16):
            tracer_y(k, r0)
        return carry

    lax.fori_loop(0, 8, local_part, 0)

    send_to_later(NORTH)
    for d in (EAST, NE):
        send_to_later(d, jnp.logical_not(last_column))
    for d in (SOUTH, SE):
        send_to_later(d)
    for d in (EAST, NE):
        send_to_later(d, last_column)

    @pl.when(far_b & later[NORTH])
    def _():
        to_hub.start()

    for d in (NORTH, SOUTH):
        wait_from(d)

    zero16 = jnp.zeros((16, COLS), F32)

    @pl.when(lat == 0)
    def _():
        for k in range(8):
            UV[k, under, :] = zero16
            TS[k, under, :] = zero16
        WE[0, under, :] = zero16
        WE[1, under, :] = zero16

    @pl.when(lat == n_lat - 1)
    def _():
        for k in range(8):
            UV[k, over, :] = zero16
            TS[k, over, :] = zero16
        WE[0, over, :] = zero16
        WE[1, over, :] = zero16

    def edge_part(k, carry):
        plane = lax.rem(k, LEVELS)
        for r0 in (8, 48):
            put_x(k, plane, r0, 8)
        for r0 in (7, 15, 39, 47):
            put_y(k, V_MAIN + plane, r0)
        combine(k)
        for r0 in (0, 24, 32):
            tracer_y(k, r0)
        return carry

    lax.fori_loop(0, 8, edge_part, 0)

    lane64 = lax.broadcasted_iota(jnp.int32, (EXT, COLS), 1)
    half = lax.rem(lane64, 32) < 16
    lane = lax.broadcasted_iota(jnp.int32, (SPAN, COLS), 1)
    level = (lane // 32).astype(F32)
    BAND = pl.ds(LO, SPAN)
    LOWER = pl.ds(LO - 1, SPAN)
    ALL = pl.ds(0, SPAN)
    scale = STEP / SUB
    own = slice(PAD - LO, PAD - LO + ROWS)

    def band(x):
        return x[LO:LO + SPAN]

    def joined(sw, main, se):
        return jnp.where(lane < 24, sw, jnp.where(lane < 64, lanes(main, 16), jnp.where(lane < 104, lanes(main, -16), se)))

    def faces(w):
        at = band(w)
        return jnp.minimum(at, lanes(at, -1)), jnp.minimum(at, band(rows(w, -1)))

    def main_sum(ref, first, where_rows, limit=None):
        total = None
        for k in range(LEVELS):
            term = ref[first + k, where_rows, :]
            if limit is not None:
                term = jnp.where(limit > k, term, 0.0)
            total = term if total is None else total + term
        return total

    def side_sum(ref, plane, where_rows, limit=None):
        term = ref[plane, where_rows, :]
        if limit is not None:
            term = jnp.where(limit > level, term, 0.0)
        return level_sum(term)

    def substeps(height, tx, ty, tym, fx, fy, cx, cy):
        for n in range(SUB):
            below = tym if n == 0 else rows(ty, 1)
            height = height - (tx - lanes(tx, 1) + ty - below)
            tx = tx - cx * (lanes(height, -1) - height) + fx
            ty = ty - cy * (rows(height, -1) - height) + fy
        return height, tx, ty

    wx_main, wy_main = faces(WE[0])
    push_x = main_sum(TEND, U_MAIN, ALL, wx_main)
    push_y = main_sum(TEND, V_MAIN, ALL, wy_main)
    tx0 = main_sum(UV, U_MAIN, BAND)
    ty0 = main_sum(UV, V_MAIN, BAND)
    tym_main = main_sum(UV, V_MAIN, LOWER)
    h_main, tx_main, ty_main = substeps(
        WE[1, BAND, :], tx0, ty0, tym_main, scale * push_x, scale * push_y, WAVE * wx_main, WAVE * wy_main)
    gain_x = (tx_main - (tx0 + STEP * push_x)) / jnp.maximum(wx_main, 1.0)
    gain_y = (ty_main - (ty0 + STEP * push_y)) / jnp.maximum(wy_main, 1.0)
    for k in range(LEVELS):
        NU[k] = jnp.where(wx_main > k, UV[U_MAIN + k, BAND, :] + STEP * TEND[U_MAIN + k, ALL, :] + gain_x, 0.0)[own]
        NV[k] = jnp.where(wy_main > k, UV[V_MAIN + k, BAND, :] + STEP * TEND[V_MAIN + k, ALL, :] + gain_y, 0.0)
    for slot, plane in enumerate((
            h_main, joined(tx0, tx0, tx0), joined(ty0, ty0, ty0), joined(tym_main, tym_main, tym_main),
            joined(push_x, push_x, push_x), joined(push_y, push_y, push_y),
            joined(wx_main, wx_main, wx_main), joined(wy_main, wy_main, wy_main))):
        KEPT[slot] = plane
    rings = [ring([UV[first + k] for k in range(LEVELS)]) for first in (U_MAIN, V_MAIN)]
    UV[U_SW] = rings[0]
    UV[V_SW] = rings[1]

    for d in (WEST, NW, SW):
        send_to_later(d)

    @pl.when(hub)
    def _():
        to_hub.wait_recv()
        hub_west.start()

    wait_from(EAST)

    @pl.when(hub)
    def _():
        hub_south.start()

    for d in (WEST, NE, SE, NW, SW):
        wait_from(d)

    @pl.when(lat == 0)
    def _():
        for i in range(2):
            RW[i, under, :] = zero16
            RE[i, under, :] = zero16

    @pl.when(lat == n_lat - 1)
    def _():
        for i in range(2):
            RW[i, over, :] = zero16
            RE[i, over, :] = zero16

    ring_u, ring_v = UV[U_SW], UV[V_SW]
    UV[U_SE] = jnp.where(half, ring_u, lanes(RE[0], 16))
    UV[V_SE] = jnp.where(half, ring_v, RE[0])
    UV[U_SW] = jnp.where(half, RW[0], ring_u)
    UV[V_SW] = jnp.where(half, lanes(RW[0], -16), ring_v)

    def strips(i, carry):
        for q_plane in (U_SW + i, V_SW + i):
            for r0 in (8, 24, 40):
                put_x(q_plane, U_SW + i, r0, 16)
            for r0 in (7, 15, 23, 31, 39, 47):
                put_y(q_plane, V_SW + i, r0)
            combine(q_plane)
        return carry

    lax.fori_loop(0, 2, strips, 0)

    def kept(slot, sw, se):
        return jnp.where(lane < 24, sw, jnp.where(lane >= 104, se, KEPT[slot]))

    wet_own = lanes(WE[0], 16)
    wx_sw, wy_sw = faces(spread(jnp.where(lane64 < 16, lanes(RW[1], -8), wet_own), 0))
    wx_se, wy_se = faces(spread(jnp.where(lane64 < 16, wet_own, lanes(RE[1], -8)), 0))
    eta_main = WE[1, BAND, :]
    eta_own = lanes(eta_main, 16)
    eta_side = joined(spread(jnp.where(lane < 16, lanes(RW[1, BAND, :], 8), eta_own), 0), eta_main,
                      spread(jnp.where(lane < 16, eta_own, lanes(RE[1, BAND, :], 8)), 0))

    push_x_sw = side_sum(TEND, U_SW, ALL, wx_sw)
    push_x_se = side_sum(TEND, U_SE, ALL, wx_se)
    push_y_sw = side_sum(TEND, V_SW, ALL, wy_sw)
    push_y_se = side_sum(TEND, V_SE, ALL, wy_se)
    tx0_sw, tx0_se = side_sum(UV, U_SW, BAND), side_sum(UV, U_SE, BAND)
    ty0_sw, ty0_se = side_sum(UV, V_SW, BAND), side_sum(UV, V_SE, BAND)

    h_side, tx_side, ty_side = substeps(
        eta_side, kept(1, tx0_sw, tx0_se), kept(2, ty0_sw, ty0_se),
        kept(3, side_sum(UV, V_SW, LOWER), side_sum(UV, V_SE, LOWER)),
        scale * kept(4, push_x_sw, push_x_se), scale * kept(5, push_y_sw, push_y_se),
        WAVE * kept(6, wx_sw, wx_se), WAVE * kept(7, wy_sw, wy_se))

    result[16] = jnp.where(lane < 16, lanes(h_side, -16), jnp.where(lane >= 112, lanes(h_side, 16), KEPT[0]))[own]

    def fresh_side(plane, trans0, push, depth, trans):
        step = UV[plane, BAND, :] + STEP * TEND[plane, ALL, :]
        return jnp.where(depth > level, step + (trans - (trans0 + STEP * push)) / jnp.maximum(depth, 1.0), 0.0)

    u_sw = fresh_side(U_SW, tx0_sw, push_x_sw, wx_sw, spread(tx_side, 0))[own]
    u_se = fresh_side(U_SE, tx0_se, push_x_se, wx_se, spread(tx_side, 96))[own]
    v_sw = fresh_side(V_SW, ty0_sw, push_y_sw, wy_sw, spread(ty_side, 0))
    v_se = fresh_side(V_SE, ty0_se, push_y_se, wy_se, spread(ty_side, 96))

    for k in range(LEVELS):
        fresh = jnp.where(lane32 < 12, lanes(u_sw, -(32 * k + 16)), jnp.where(lane32 >= 116, lanes(u_se, 112 - 32 * k), NU[k]))
        NU[k] = fresh
        result[k] = fresh
        fresh = jnp.where(lane < 12, lanes(v_sw, -(32 * k + 16)), jnp.where(lane >= 116, lanes(v_se, 112 - 32 * k), NV[k]))
        NV[k] = fresh
        result[4 + k] = fresh[own]

    ring_t = ring([TS[k, OWN, :] for k in range(LEVELS)])
    ring_s = ring([TS[4 + k, OWN, :] for k in range(LEVELS)])

    def side_flux(cells, flow):
        flux = flow * upwind_value(flow, *x_parts(cells))
        return flux - lanes(flux, 1)

    XS[0] = side_flux(jnp.where(half32, RW[1, OWN, :], ring_t), u_sw)
    XS[1] = side_flux(jnp.where(half32, ring_t, lanes(RE[1, OWN, :], 16)), u_se)
    XS[2] = side_flux(jnp.where(half32, lanes(RW[1, OWN, :], -16), ring_s), u_sw)
    XS[3] = side_flux(jnp.where(half32, ring_s, RE[1, OWN, :]), u_se)

    for field in range(2):
        for k in range(LEVELS):
            p = 4 * field + k
            flow = NU[k]
            flux = flow * jnp.where(flow >= 0.0, XU[p], XD[p])
            div_x = flux - lanes(flux, 1)
            div_x = jnp.where(lane32 < 8, lanes(XS[2 * field], -(32 * k + 16)),
                              jnp.where(lane32 >= 120, lanes(XS[2 * field + 1], 112 - 32 * k), div_x))
            up = NV[k, pl.ds(8, ROWS), :]
            down = NV[k, pl.ds(7, ROWS), :]
            flux_up = up * jnp.where(up >= 0.0, YU[p, pl.ds(1, ROWS), :], YD[p, pl.ds(1, ROWS), :])
            flux_down = down * jnp.where(down >= 0.0, YU[p, pl.ds(0, ROWS), :], YD[p, pl.ds(0, ROWS), :])
            cells = TS[p, OWN, :]
            fresh = cells - STEP * (div_x + (flux_up - flux_down))
            result[8 + p] = jnp.where(wet[0] > k, fresh, 0.0)

    for d in range(8):
        if d in (SE, NW):
            @pl.when(earlier[d] | later[d])
            def _():
                for copy in copies(d):
                    copy.wait_send()
        else:
            for copy in copies(d):
                copy.wait_send()

    @pl.when(hub)
    def _():
        hub_west.wait_send()
        hub_south.wait_send()

    @pl.when(far_b)
    def _():
        to_hub.wait_send()


def deal(result, u_out, v_out, t_out, s_out, e_out, sem):
    copies = [pltpu.make_async_copy(result.at[pl.ds(LEVELS * i, LEVELS)], out, sem.at[i])
              for i, out in enumerate((u_out, v_out, t_out, s_out))]
    copies.append(pltpu.make_async_copy(result.at[16], e_out, sem.at[4]))
    for copy in copies:
        copy.start()
    for copy in copies:
        copy.wait()


def solution(mesh):
    n_lat, n_lon = mesh.shape["lat"], mesh.shape["lon"]

    def step(u_vel, v_vel, temp, salt, eta, wet_levels):
        levels = jax.ShapeDtypeStruct((LEVELS, ROWS, COLS), F32)
        plane = jax.ShapeDtypeStruct((ROWS, COLS), F32)
        hbm = pl.BlockSpec(memory_space=pl.ANY)
        vmem = pl.BlockSpec(memory_space=pltpu.VMEM)

        def body(*refs):
            kernel(n_lat, n_lon, *refs)

        def buffer(*shape):
            return pltpu.VMEM(shape, F32)

        result = pl.pallas_call(
            body,
            out_shape=pltpu.VMEM((17, ROWS, COLS), F32),
            in_specs=[hbm] * 6,
            out_specs=vmem,
            scratch_shapes=[
                buffer(16, ROWS, COLS),
                buffer(ROWS, COLS),
                pltpu.VMEM((3, ROWS, COLS), jnp.int32),
                buffer(12, EXT, COLS),
                buffer(8, EXT, COLS),
                buffer(2, EXT, COLS),
                buffer(2, EXT, COLS),
                buffer(2, EXT, COLS),
                buffer(2, EXT, COLS),
                buffer(2, EXT, COLS),
                buffer(2, PAD, COLS),
                buffer(8, SPAN, COLS),
                buffer(12, SPAN, COLS),
                buffer(12, SPAN + 8, COLS),
                buffer(8, ROWS, COLS),
                buffer(8, ROWS, COLS),
                buffer(8, 40, COLS),
                buffer(8, 40, COLS),
                buffer(4, SPAN, COLS),
                buffer(4, ROWS, COLS),
                buffer(4, ROWS, COLS),
                pltpu.SemaphoreType.DMA((6,)),
                pltpu.SemaphoreType.REGULAR((8,)),
                pltpu.SemaphoreType.DMA((15,)),
                pltpu.SemaphoreType.DMA((15,)),
            ],
            compiler_params=pltpu.CompilerParams(collective_id=0, has_side_effects=True),
        )(u_vel, v_vel, temp, salt, eta, wet_levels)
        return pl.pallas_call(
            deal,
            out_shape=(levels, levels, levels, levels, plane),
            in_specs=[vmem],
            out_specs=(hbm,) * 5,
            scratch_shapes=[pltpu.SemaphoreType.DMA((5,))],
            compiler_params=pltpu.CompilerParams(vmem_limit_bytes=1 << 20),
        )(result)

    tile, flat = P(None, "lat", "lon"), P("lat", "lon")
    return jax.shard_map(
        step, mesh=mesh, in_specs=(tile, tile, tile, tile, flat, tile),
        out_specs=(tile, tile, tile, tile, flat), check_vma=False)
```

```python
import jax
import jax.numpy as jnp
from jax import lax
from jax.experimental import pallas as pl
from jax.experimental.pallas import tpu as pltpu
from jax.sharding import PartitionSpec as P

MESH = pl.DeviceIdType.MESH
F32 = jnp.float32
LEVELS = 4
SUB = 8
BLOCK = 8
RELAYED_FROM = 2
STEP = 0.4
WAVE = 0.45 / 4
EPS = 1e-6 * 12.0 / 13.0
ROWS = 32
COLS = 128
PAD = 16
EXT = ROWS + 2 * PAD
LO = 8
SPAN = 48

U_MAIN, V_MAIN, U_SW, U_SE, V_SW, V_SE = 0, 4, 8, 9, 10, 11


def lanes(x, shift):
    shift = shift % COLS
    return x if shift == 0 else pltpu.roll(x, shift, 1)


def rows(x, shift):
    return pltpu.roll(x, shift % x.shape[0], 0)


def correction(d0, d1, d2, d3):
    x0 = d1 - d0
    x1 = d2 - d1
    x2 = d3 - d2
    m1 = d1 + d1
    m2 = d2 + d2
    y0 = x0 + m1
    y1 = d1 + d2
    y2 = x2 - m2
    e0 = x0 * x0 + (y0 * y0) * (3.0 / 13.0) + EPS
    e1 = x1 * x1 + (y1 * y1) * (3.0 / 13.0) + EPS
    e2 = x2 * x2 + (y2 * y2) * (3.0 / 13.0) + EPS
    a0 = e1 * e2
    a1 = e0 * e2
    a2 = e0 * e1
    w0 = a0 * a0
    w1 = (a1 * a1) * 6.0
    w2 = (a2 * a2) * 3.0
    top = w0 * (5.0 * d1 - 2.0 * d0) + w1 * (d1 + m2) + w2 * (4.0 * d2 - d3)
    return top / ((w0 + w1 + w2) * 6.0)


def upwind_value(flow, q0, q1, gm2, gm1, g0, g1, g2):
    ahead = flow >= 0.0
    fix = correction(jnp.where(ahead, gm2, g2), jnp.where(ahead, gm1, g1), g0, jnp.where(ahead, g1, gm1))
    return jnp.where(ahead, q0 + fix, q1 - fix)


def x_parts(q):
    q1 = lanes(q, -1)
    g = q1 - q
    return q, q1, lanes(g, 2), lanes(g, 1), g, lanes(g, -1), lanes(g, -2)


def y_parts(ref, k, r0, n):
    q = [ref[k, pl.ds(r0 + s, n), :] for s in range(-2, 4)]
    g = [q[i + 1] - q[i] for i in range(5)]
    return q[2], q[3], g[0], g[1], g[2], g[3], g[4]


def ring(parts):
    lane = lax.broadcasted_iota(jnp.int32, parts[0].shape, 1)
    out = lanes(parts[0], 16)
    for k in range(1, LEVELS):
        out = jnp.where(lane >= 32 * k, lanes(parts[k], 32 * k + 16), out)
    return out


def level_sum(x):
    y = x + lanes(x, 64)
    return y + lanes(y, 32)


def spread(x, start):
    lane = lax.broadcasted_iota(jnp.int32, x.shape, 1)
    return level_sum(jnp.where((lane >= start) & (lane < start + 32), x, 0.0))


DIRS = ((1, 0), (-1, 0), (0, 1), (0, -1), (1, 1), (-1, 1), (1, -1), (-1, -1))
NORTH, SOUTH, EAST, WEST, NE, SE, NW, SW = range(8)


def kernel(n_lat, n_lon, u_hbm, v_hbm, t_hbm, s_hbm, e_hbm, w_hbm,
           result,
           raw, raw2, wet, UV, TS, WE, PE, PW, RW, RE, HUB, KEPT,
           TEND, FY, XU, XD, YU, YD, NV, NU, XS,
           in_sem, ready, send_sem, recv_sem):
    lat = lax.axis_index("lat")
    lon = lax.axis_index("lon")

    def start_rank(i, j):
        group = j // BLOCK
        group = jnp.where(group == 2, 3, jnp.where(group == 3, 2, group))
        rank = (group * BLOCK + lax.rem(i, BLOCK)) * (n_lat * n_lon) + i * n_lon + j
        return jnp.where((i == 0) & (j == 0), 2 * BLOCK * n_lat * n_lon - 1, rank)

    peers = [(lax.rem(lat + n_lat + di, n_lat), lax.rem(lon + n_lon + dj, n_lon)) for di, dj in DIRS]
    here = start_rank(lat, lon)
    earlier = [start_rank(*peer) < here for peer in peers]
    first_row, last_row = lax.rem(lat, BLOCK) == 0, lax.rem(lat, BLOCK) == BLOCK - 1
    first_column, last_column = lax.rem(lon, BLOCK) == 0, lax.rem(lon, BLOCK) == BLOCK - 1
    inner_west, inner_east = jnp.logical_not(first_column), jnp.logical_not(last_column)
    relayed = lon // BLOCK >= RELAYED_FROM
    west_relayed = peers[WEST][1] // BLOCK >= RELAYED_FROM
    corner_a, corner_b, corner_hub = first_row & last_column, last_row & first_column, first_row & first_column
    later = [jnp.logical_not(flag) for flag in earlier]
    earlier[SE] = earlier[SE] & jnp.logical_not(corner_a)
    later[SE] = later[SE] & jnp.logical_not(corner_a)
    earlier[NW] = (earlier[NW] & jnp.logical_not(corner_b)) | (corner_b & jnp.logical_not(west_relayed))
    later[NW] = later[NW] & jnp.logical_not(corner_b)

    barrier = pltpu.get_barrier_semaphore()
    expected = 0
    for d in range(8):
        expected = expected + jnp.where(earlier[d], 1, 0)

        @pl.when(later[d])
        def _():
            pl.semaphore_signal(barrier, inc=1, device_id=peers[d], device_id_type=MESH)

    @pl.when(corner_a & jnp.logical_not(relayed))
    def _():
        pl.semaphore_signal(barrier, inc=1, device_id=peers[SE], device_id_type=MESH)

    loads = [
        pltpu.make_async_copy(w_hbm, wet, in_sem.at[0]),
        pltpu.make_async_copy(u_hbm, raw.at[pl.ds(0, 4)], in_sem.at[1]),
        pltpu.make_async_copy(v_hbm, raw.at[pl.ds(4, 4)], in_sem.at[2]),
        pltpu.make_async_copy(t_hbm, raw.at[pl.ds(8, 4)], in_sem.at[3]),
        pltpu.make_async_copy(s_hbm, raw.at[pl.ds(12, 4)], in_sem.at[4]),
        pltpu.make_async_copy(e_hbm, raw2, in_sem.at[5]),
    ]
    for load in loads:
        load.start()
    for load in loads:
        load.wait()

    OWN = pl.ds(PAD, ROWS)
    for k in range(LEVELS):
        UV[U_MAIN + k, OWN, :] = jnp.where(wet[1] > k, raw[k], 0.0)
        UV[V_MAIN + k, OWN, :] = jnp.where(wet[2] > k, raw[4 + k], 0.0)
        TS[k, OWN, :] = jnp.where(wet[0] > k, raw[8 + k], 0.0)
        TS[4 + k, OWN, :] = jnp.where(wet[0] > k, raw[12 + k], 0.0)
    WE[0, OWN, :] = wet[0].astype(F32)
    WE[1, OWN, :] = raw2[...]

    lane32 = lax.broadcasted_iota(jnp.int32, (ROWS, COLS), 1)
    half32 = lax.rem(lane32, 32) < 16
    ring_u = ring([UV[U_MAIN + k, OWN, :] for k in range(LEVELS)])
    ring_v = ring([UV[V_MAIN + k, OWN, :] for k in range(LEVELS)])
    ring_t = ring([TS[k, OWN, :] for k in range(LEVELS)])
    ring_s = ring([TS[4 + k, OWN, :] for k in range(LEVELS)])
    eta8, wet24 = lanes(raw2[...], 8), lanes(wet[0].astype(F32), 24)
    PE[0, OWN, :] = jnp.where(half32, ring_u, lanes(ring_v, 16))
    PW[0, OWN, :] = jnp.where(half32, lanes(ring_u, -16), ring_v)
    PE[1, OWN, :] = jnp.where(lane32 < 8, eta8, jnp.where(
        (lane32 >= 16) & (lane32 < 24), wet24, jnp.where(half32, ring_t, lanes(ring_s, 16))))
    PW[1, OWN, :] = jnp.where((lane32 >= 8) & (lane32 < 16), eta8, jnp.where(
        (lane32 >= 24) & (lane32 < 32), wet24, jnp.where(half32, lanes(ring_t, -16), ring_s)))

    top, bottom = pl.ds(32, 16), pl.ds(16, 16)
    under, over = pl.ds(0, 16), pl.ds(48, 16)
    every = pl.ds(0, 8)
    parcels = {
        NORTH: [(UV.at[every, pl.ds(36, 12), :], UV.at[every, pl.ds(4, 12), :]),
                (WE.at[:, pl.ds(40, 8), :], WE.at[:, pl.ds(8, 8), :]),
                (TS.at[:, pl.ds(45, 3), :], TS.at[:, pl.ds(13, 3), :])],
        SOUTH: [(UV.at[every, pl.ds(16, 12), :], UV.at[every, pl.ds(48, 12), :]),
                (WE.at[:, pl.ds(16, 8), :], WE.at[:, pl.ds(48, 8), :]),
                (TS.at[:, pl.ds(16, 3), :], TS.at[:, pl.ds(48, 3), :])],
        EAST: [(PE.at[:, OWN, :], RW.at[:, OWN, :])],
        WEST: [(PW.at[:, OWN, :], RE.at[:, OWN, :])],
        NE: [(PE.at[:, pl.ds(36, 12), :], RW.at[:, pl.ds(4, 12), :])],
        SE: [(PE.at[:, pl.ds(16, 12), :], RW.at[:, pl.ds(48, 12), :])],
        NW: [(PW.at[:, pl.ds(36, 12), :], RE.at[:, pl.ds(4, 12), :])],
        SW: [(PW.at[:, pl.ds(16, 12), :], RE.at[:, pl.ds(48, 12), :])],
    }
    first_slot, slots = {}, 0
    for d in range(8):
        first_slot[d] = slots
        slots += len(parcels[d])

    def copies(d):
        return [
            pltpu.make_async_remote_copy(
                src_ref=src, dst_ref=dst, send_sem=send_sem.at[first_slot[d] + i], recv_sem=recv_sem.at[first_slot[d] + i],
                device_id=peers[d], device_id_type=MESH)
            for i, (src, dst) in enumerate(parcels[d])]

    def send_to_earlier(d, also=True):
        @pl.when(earlier[d] & also)
        def _():
            for copy in copies(d):
                copy.start()

    def send_to_later(d, also=True):
        @pl.when(later[d] & also)
        def _():
            pl.semaphore_wait(ready.at[d], 1)
            for copy in copies(d):
                copy.start()

    def wait_from(d):
        for copy in copies(d):
            copy.wait_recv()

    def extra(slot, src, dst, arrival, peer):
        return pltpu.make_async_remote_copy(
            src_ref=src, dst_ref=dst, send_sem=send_sem.at[slot], recv_sem=recv_sem.at[arrival],
            device_id=peer, device_id_type=MESH)

    to_hub = extra(slots, PW.at[:, pl.ds(36, 12), :], HUB.at[:, pl.ds(4, 12), :], slots, peers[NORTH])
    hub_west = extra(slots + 1, HUB.at[:, pl.ds(4, 12), :], RE.at[:, pl.ds(4, 12), :], first_slot[NW], peers[WEST])
    hub_south = extra(slots + 2, RW.at[:, pl.ds(16, 12), :], RW.at[:, pl.ds(48, 12), :], first_slot[SE], peers[SOUTH])

    @pl.when(expected > 0)
    def _():
        pl.semaphore_wait(barrier, expected)

    for d in range(8):
        @pl.when(earlier[d] & jnp.logical_not(corner_b) if d == NW else earlier[d])
        def _():
            pl.semaphore_signal(ready.at[DIRS.index((-DIRS[d][0], -DIRS[d][1]))], inc=1, device_id=peers[d], device_id_type=MESH)

    send_to_earlier(NW, corner_b)
    for d in (EAST, NE, SE, WEST, SW):
        send_to_earlier(d)
    send_to_earlier(NW, jnp.logical_not(corner_b))
    for d in (NORTH, SOUTH):
        send_to_earlier(d)

    @pl.when(corner_b & west_relayed & earlier[NORTH])
    def _():
        to_hub.start()

    def flux_x(q_plane, u_plane, r0, n):
        flow = UV[u_plane, pl.ds(r0, n), :]
        flux = flow * upwind_value(flow, *x_parts(UV[q_plane, pl.ds(r0, n), :]))
        return flux - lanes(flux, 1)

    def flux_y(q_plane, v_plane, r0):
        flow = UV[v_plane, pl.ds(r0, 8), :]
        return flow * upwind_value(flow, *y_parts(UV, q_plane, r0, 8))

    def put_x(q_plane, u_plane, r0, n):
        TEND[q_plane, pl.ds(r0 - LO, n), :] = flux_x(q_plane, u_plane, r0, n)

    def put_y(q_plane, v_plane, r0):
        FY[q_plane, pl.ds(r0 - LO + 1, 8), :] = flux_y(q_plane, v_plane, r0)

    def combine(q_plane):
        for r0 in range(0, SPAN, 16):
            TEND[q_plane, pl.ds(r0, 16), :] = -(TEND[q_plane, pl.ds(r0, 16), :] + (
                FY[q_plane, pl.ds(r0 + 1, 16), :] - FY[q_plane, pl.ds(r0, 16), :]))

    def tracer_x(k, r0, n):
        q0, q1, gm2, gm1, g0, g1, g2 = x_parts(TS[k, pl.ds(PAD + r0, n), :])
        XU[k, pl.ds(r0, n), :] = q0 + correction(gm2, gm1, g0, g1)
        XD[k, pl.ds(r0, n), :] = q1 - correction(g2, g1, g0, gm1)

    def tracer_y(k, r0):
        q0, q1, gm2, gm1, g0, g1, g2 = y_parts(TS, k, PAD - 1 + r0, 8)
        YU[k, pl.ds(r0, 8), :] = q0 + correction(gm2, gm1, g0, g1)
        YD[k, pl.ds(r0, 8), :] = q1 - correction(g2, g1, g0, gm1)

    def local_part(k, carry):
        plane = lax.rem(k, LEVELS)
        for r0 in (16, 32):
            put_x(k, plane, r0, 16)
        for r0 in (23, 31):
            put_y(k, V_MAIN + plane, r0)
        for r0 in (0, 16):
            tracer_x(k, r0, 16)
        for r0 in (8, 16):
            tracer_y(k, r0)
        return carry

    lax.fori_loop(0, 8, local_part, 0)

    send_to_later(NORTH)

    @pl.when(corner_b & west_relayed & later[NORTH])
    def _():
        to_hub.start()

    send_to_later(EAST, inner_east)
    send_to_later(NE, inner_east)
    send_to_later(WEST, inner_west)
    send_to_later(NW, inner_west)
    send_to_later(SOUTH)
    send_to_later(SE, inner_east)
    send_to_later(SW, inner_west)
    for d in (EAST, NE, SE):
        send_to_later(d, last_column)

    for d in (NORTH, SOUTH):
        wait_from(d)

    zero16 = jnp.zeros((16, COLS), F32)

    @pl.when(lat == 0)
    def _():
        for k in range(8):
            UV[k, under, :] = zero16
            TS[k, under, :] = zero16
        WE[0, under, :] = zero16
        WE[1, under, :] = zero16

    @pl.when(lat == n_lat - 1)
    def _():
        for k in range(8):
            UV[k, over, :] = zero16
            TS[k, over, :] = zero16
        WE[0, over, :] = zero16
        WE[1, over, :] = zero16

    def edge_part(k, carry):
        plane = lax.rem(k, LEVELS)
        for r0 in (8, 48):
            put_x(k, plane, r0, 8)
        for r0 in (7, 15, 39, 47):
            put_y(k, V_MAIN + plane, r0)
        combine(k)
        for r0 in (0, 24, 32):
            tracer_y(k, r0)
        return carry

    lax.fori_loop(0, 8, edge_part, 0)

    lane64 = lax.broadcasted_iota(jnp.int32, (EXT, COLS), 1)
    half = lax.rem(lane64, 32) < 16
    lane = lax.broadcasted_iota(jnp.int32, (SPAN, COLS), 1)
    level = (lane // 32).astype(F32)
    BAND = pl.ds(LO, SPAN)
    LOWER = pl.ds(LO - 1, SPAN)
    ALL = pl.ds(0, SPAN)
    scale = STEP / SUB
    own = slice(PAD - LO, PAD - LO + ROWS)

    def band(x):
        return x[LO:LO + SPAN]

    def joined(sw, main, se):
        return jnp.where(lane < 24, sw, jnp.where(lane < 64, lanes(main, 16), jnp.where(lane < 104, lanes(main, -16), se)))

    def faces(w):
        at = band(w)
        return jnp.minimum(at, lanes(at, -1)), jnp.minimum(at, band(rows(w, -1)))

    def main_sum(ref, first, where_rows, limit=None):
        total = None
        for k in range(LEVELS):
            term = ref[first + k, where_rows, :]
            if limit is not None:
                term = jnp.where(limit > k, term, 0.0)
            total = term if total is None else total + term
        return total

    def side_sum(ref, plane, where_rows, limit=None):
        term = ref[plane, where_rows, :]
        if limit is not None:
            term = jnp.where(limit > level, term, 0.0)
        return level_sum(term)

    def substeps(height, tx, ty, tym, fx, fy, cx, cy):
        for n in range(SUB):
            below = tym if n == 0 else rows(ty, 1)
            height = height - (tx - lanes(tx, 1) + ty - below)
            tx = tx - cx * (lanes(height, -1) - height) + fx
            ty = ty - cy * (rows(height, -1) - height) + fy
        return height, tx, ty

    wx_main, wy_main = faces(WE[0])
    push_x = main_sum(TEND, U_MAIN, ALL, wx_main)
    push_y = main_sum(TEND, V_MAIN, ALL, wy_main)
    tx0 = main_sum(UV, U_MAIN, BAND)
    ty0 = main_sum(UV, V_MAIN, BAND)
    tym_main = main_sum(UV, V_MAIN, LOWER)
    h_main, tx_main, ty_main = substeps(
        WE[1, BAND, :], tx0, ty0, tym_main, scale * push_x, scale * push_y, WAVE * wx_main, WAVE * wy_main)
    gain_x = (tx_main - (tx0 + STEP * push_x)) / jnp.maximum(wx_main, 1.0)
    gain_y = (ty_main - (ty0 + STEP * push_y)) / jnp.maximum(wy_main, 1.0)
    for k in range(LEVELS):
        NU[k] = jnp.where(wx_main > k, UV[U_MAIN + k, BAND, :] + STEP * TEND[U_MAIN + k, ALL, :] + gain_x, 0.0)[own]
        NV[k] = jnp.where(wy_main > k, UV[V_MAIN + k, BAND, :] + STEP * TEND[V_MAIN + k, ALL, :] + gain_y, 0.0)
    for slot, plane in enumerate((
            h_main, joined(tx0, tx0, tx0), joined(ty0, ty0, ty0), joined(tym_main, tym_main, tym_main),
            joined(push_x, push_x, push_x), joined(push_y, push_y, push_y),
            joined(wx_main, wx_main, wx_main), joined(wy_main, wy_main, wy_main))):
        KEPT[slot] = plane
    rings = [ring([UV[first + k] for k in range(LEVELS)]) for first in (U_MAIN, V_MAIN)]
    UV[U_SW] = rings[0]
    UV[V_SW] = rings[1]

    for d in (WEST, NW, SW):
        send_to_later(d, first_column)

    @pl.when(corner_hub & west_relayed)
    def _():
        to_hub.wait_recv()
        hub_west.start()

    wait_from(EAST)

    @pl.when(corner_hub)
    def _():
        hub_south.start()

    for d in (WEST, NE, SE, NW, SW):
        wait_from(d)

    @pl.when(lat == 0)
    def _():
        for i in range(2):
            RW[i, under, :] = zero16
            RE[i, under, :] = zero16

    @pl.when(lat == n_lat - 1)
    def _():
        for i in range(2):
            RW[i, over, :] = zero16
            RE[i, over, :] = zero16

    ring_u, ring_v = UV[U_SW], UV[V_SW]
    UV[U_SE] = jnp.where(half, ring_u, lanes(RE[0], 16))
    UV[V_SE] = jnp.where(half, ring_v, RE[0])
    UV[U_SW] = jnp.where(half, RW[0], ring_u)
    UV[V_SW] = jnp.where(half, lanes(RW[0], -16), ring_v)

    def strips(i, carry):
        for q_plane in (U_SW + i, V_SW + i):
            for r0 in (8, 24, 40):
                put_x(q_plane, U_SW + i, r0, 16)
            for r0 in (7, 15, 23, 31, 39, 47):
                put_y(q_plane, V_SW + i, r0)
            combine(q_plane)
        return carry

    lax.fori_loop(0, 2, strips, 0)

    def kept(slot, sw, se):
        return jnp.where(lane < 24, sw, jnp.where(lane >= 104, se, KEPT[slot]))

    wet_own = lanes(WE[0], 16)
    wx_sw, wy_sw = faces(spread(jnp.where(lane64 < 16, lanes(RW[1], -8), wet_own), 0))
    wx_se, wy_se = faces(spread(jnp.where(lane64 < 16, wet_own, lanes(RE[1], -8)), 0))
    eta_main = WE[1, BAND, :]
    eta_own = lanes(eta_main, 16)
    eta_side = joined(spread(jnp.where(lane < 16, lanes(RW[1, BAND, :], 8), eta_own), 0), eta_main,
                      spread(jnp.where(lane < 16, eta_own, lanes(RE[1, BAND, :], 8)), 0))

    push_x_sw = side_sum(TEND, U_SW, ALL, wx_sw)
    push_x_se = side_sum(TEND, U_SE, ALL, wx_se)
    push_y_sw = side_sum(TEND, V_SW, ALL, wy_sw)
    push_y_se = side_sum(TEND, V_SE, ALL, wy_se)
    tx0_sw, tx0_se = side_sum(UV, U_SW, BAND), side_sum(UV, U_SE, BAND)
    ty0_sw, ty0_se = side_sum(UV, V_SW, BAND), side_sum(UV, V_SE, BAND)

    h_side, tx_side, ty_side = substeps(
        eta_side, kept(1, tx0_sw, tx0_se), kept(2, ty0_sw, ty0_se),
        kept(3, side_sum(UV, V_SW, LOWER), side_sum(UV, V_SE, LOWER)),
        scale * kept(4, push_x_sw, push_x_se), scale * kept(5, push_y_sw, push_y_se),
        WAVE * kept(6, wx_sw, wx_se), WAVE * kept(7, wy_sw, wy_se))

    result[16] = jnp.where(lane < 16, lanes(h_side, -16), jnp.where(lane >= 112, lanes(h_side, 16), KEPT[0]))[own]

    def fresh_side(plane, trans0, push, depth, trans):
        step = UV[plane, BAND, :] + STEP * TEND[plane, ALL, :]
        return jnp.where(depth > level, step + (trans - (trans0 + STEP * push)) / jnp.maximum(depth, 1.0), 0.0)

    u_sw = fresh_side(U_SW, tx0_sw, push_x_sw, wx_sw, spread(tx_side, 0))[own]
    u_se = fresh_side(U_SE, tx0_se, push_x_se, wx_se, spread(tx_side, 96))[own]
    v_sw = fresh_side(V_SW, ty0_sw, push_y_sw, wy_sw, spread(ty_side, 0))
    v_se = fresh_side(V_SE, ty0_se, push_y_se, wy_se, spread(ty_side, 96))

    for k in range(LEVELS):
        fresh = jnp.where(lane32 < 12, lanes(u_sw, -(32 * k + 16)), jnp.where(lane32 >= 116, lanes(u_se, 112 - 32 * k), NU[k]))
        NU[k] = fresh
        result[k] = fresh
        fresh = jnp.where(lane < 12, lanes(v_sw, -(32 * k + 16)), jnp.where(lane >= 116, lanes(v_se, 112 - 32 * k), NV[k]))
        NV[k] = fresh
        result[4 + k] = fresh[own]

    ring_t = ring([TS[k, OWN, :] for k in range(LEVELS)])
    ring_s = ring([TS[4 + k, OWN, :] for k in range(LEVELS)])

    def side_flux(cells, flow):
        flux = flow * upwind_value(flow, *x_parts(cells))
        return flux - lanes(flux, 1)

    XS[0] = side_flux(jnp.where(half32, RW[1, OWN, :], ring_t), u_sw)
    XS[1] = side_flux(jnp.where(half32, ring_t, lanes(RE[1, OWN, :], 16)), u_se)
    XS[2] = side_flux(jnp.where(half32, lanes(RW[1, OWN, :], -16), ring_s), u_sw)
    XS[3] = side_flux(jnp.where(half32, ring_s, RE[1, OWN, :]), u_se)

    for field in range(2):
        for k in range(LEVELS):
            p = 4 * field + k
            flow = NU[k]
            flux = flow * jnp.where(flow >= 0.0, XU[p], XD[p])
            div_x = flux - lanes(flux, 1)
            div_x = jnp.where(lane32 < 8, lanes(XS[2 * field], -(32 * k + 16)),
                              jnp.where(lane32 >= 120, lanes(XS[2 * field + 1], 112 - 32 * k), div_x))
            up = NV[k, pl.ds(8, ROWS), :]
            down = NV[k, pl.ds(7, ROWS), :]
            flux_up = up * jnp.where(up >= 0.0, YU[p, pl.ds(1, ROWS), :], YD[p, pl.ds(1, ROWS), :])
            flux_down = down * jnp.where(down >= 0.0, YU[p, pl.ds(0, ROWS), :], YD[p, pl.ds(0, ROWS), :])
            cells = TS[p, OWN, :]
            fresh = cells - STEP * (div_x + (flux_up - flux_down))
            result[8 + p] = jnp.where(wet[0] > k, fresh, 0.0)

    for d in range(8):
        if d in (SE, NW):
            @pl.when(earlier[d] | later[d])
            def _():
                for copy in copies(d):
                    copy.wait_send()
        else:
            for copy in copies(d):
                copy.wait_send()

    @pl.when(corner_hub)
    def _():
        hub_south.wait_send()

    @pl.when(corner_hub & west_relayed)
    def _():
        hub_west.wait_send()

    @pl.when(corner_b & west_relayed)
    def _():
        to_hub.wait_send()


def deal(result, u_out, v_out, t_out, s_out, e_out, sem):
    copies = [pltpu.make_async_copy(result.at[pl.ds(LEVELS * i, LEVELS)], out, sem.at[i])
              for i, out in enumerate((u_out, v_out, t_out, s_out))]
    copies.append(pltpu.make_async_copy(result.at[16], e_out, sem.at[4]))
    for copy in copies:
        copy.start()
    for copy in copies:
        copy.wait()


def solution(mesh):
    n_lat, n_lon = mesh.shape["lat"], mesh.shape["lon"]

    def step(u_vel, v_vel, temp, salt, eta, wet_levels):
        levels = jax.ShapeDtypeStruct((LEVELS, ROWS, COLS), F32)
        plane = jax.ShapeDtypeStruct((ROWS, COLS), F32)
        hbm = pl.BlockSpec(memory_space=pl.ANY)
        vmem = pl.BlockSpec(memory_space=pltpu.VMEM)

        def body(*refs):
            kernel(n_lat, n_lon, *refs)

        def buffer(*shape):
            return pltpu.VMEM(shape, F32)

        result = pl.pallas_call(
            body,
            out_shape=pltpu.VMEM((17, ROWS, COLS), F32),
            in_specs=[hbm] * 6,
            out_specs=vmem,
            scratch_shapes=[
                buffer(16, ROWS, COLS),
                buffer(ROWS, COLS),
                pltpu.VMEM((3, ROWS, COLS), jnp.int32),
                buffer(12, EXT, COLS),
                buffer(8, EXT, COLS),
                buffer(2, EXT, COLS),
                buffer(2, EXT, COLS),
                buffer(2, EXT, COLS),
                buffer(2, EXT, COLS),
                buffer(2, EXT, COLS),
                buffer(2, PAD, COLS),
                buffer(8, SPAN, COLS),
                buffer(12, SPAN, COLS),
                buffer(12, SPAN + 8, COLS),
                buffer(8, ROWS, COLS),
                buffer(8, ROWS, COLS),
                buffer(8, 40, COLS),
                buffer(8, 40, COLS),
                buffer(4, SPAN, COLS),
                buffer(4, ROWS, COLS),
                buffer(4, ROWS, COLS),
                pltpu.SemaphoreType.DMA((6,)),
                pltpu.SemaphoreType.REGULAR((8,)),
                pltpu.SemaphoreType.DMA((15,)),
                pltpu.SemaphoreType.DMA((15,)),
            ],
            compiler_params=pltpu.CompilerParams(collective_id=0, has_side_effects=True),
        )(u_vel, v_vel, temp, salt, eta, wet_levels)
        return pl.pallas_call(
            deal,
            out_shape=(levels, levels, levels, levels, plane),
            in_specs=[vmem],
            out_specs=(hbm,) * 5,
            scratch_shapes=[pltpu.SemaphoreType.DMA((5,))],
            compiler_params=pltpu.CompilerParams(vmem_limit_bytes=1 << 20),
        )(result)

    tile, flat = P(None, "lat", "lon"), P("lat", "lon")
    return jax.shard_map(
        step, mesh=mesh, in_specs=(tile, tile, tile, tile, flat, tile),
        out_specs=(tile, tile, tile, tile, flat), check_vma=False)
```

```python
import jax
import jax.numpy as jnp
from jax import lax
from jax.experimental import pallas as pl
from jax.experimental.pallas import tpu as pltpu
from jax.sharding import PartitionSpec as P

MESH = pl.DeviceIdType.MESH
F32 = jnp.float32
LEVELS = 4
SUB = 8
BLOCK = 8
RELAYED_FROM = 2
STEP = 0.4
WAVE = 0.45 / 4
EPS = 1e-6 * 12.0 / 13.0
ROWS = 32
COLS = 128
PAD = 16
EXT = ROWS + 2 * PAD
LO = 8
SPAN = 48

U_MAIN, V_MAIN, U_SW, U_SE, V_SW, V_SE = 0, 4, 8, 9, 10, 11


def lanes(x, shift):
    shift = shift % COLS
    return x if shift == 0 else pltpu.roll(x, shift, 1)


def rows(x, shift):
    return pltpu.roll(x, shift % x.shape[0], 0)


def correction(d0, d1, d2, d3):
    x0 = d1 - d0
    x1 = d2 - d1
    x2 = d3 - d2
    m1 = d1 + d1
    m2 = d2 + d2
    y0 = x0 + m1
    y1 = d1 + d2
    y2 = x2 - m2
    e0 = x0 * x0 + (y0 * y0) * (3.0 / 13.0) + EPS
    e1 = x1 * x1 + (y1 * y1) * (3.0 / 13.0) + EPS
    e2 = x2 * x2 + (y2 * y2) * (3.0 / 13.0) + EPS
    a0 = e1 * e2
    a1 = e0 * e2
    a2 = e0 * e1
    w0 = a0 * a0
    w1 = (a1 * a1) * 6.0
    w2 = (a2 * a2) * 3.0
    top = w0 * (5.0 * d1 - 2.0 * d0) + w1 * (d1 + m2) + w2 * (4.0 * d2 - d3)
    return top / ((w0 + w1 + w2) * 6.0)


def upwind_value(flow, q0, q1, gm2, gm1, g0, g1, g2):
    ahead = flow >= 0.0
    fix = correction(jnp.where(ahead, gm2, g2), jnp.where(ahead, gm1, g1), g0, jnp.where(ahead, g1, gm1))
    return jnp.where(ahead, q0 + fix, q1 - fix)


def x_parts(q):
    q1 = lanes(q, -1)
    g = q1 - q
    return q, q1, lanes(g, 2), lanes(g, 1), g, lanes(g, -1), lanes(g, -2)


def y_parts(ref, k, r0, n):
    q = [ref[k, pl.ds(r0 + s, n), :] for s in range(-2, 4)]
    g = [q[i + 1] - q[i] for i in range(5)]
    return q[2], q[3], g[0], g[1], g[2], g[3], g[4]


def ring(parts):
    lane = lax.broadcasted_iota(jnp.int32, parts[0].shape, 1)
    out = lanes(parts[0], 16)
    for k in range(1, LEVELS):
        out = jnp.where(lane >= 32 * k, lanes(parts[k], 32 * k + 16), out)
    return out


def level_sum(x):
    y = x + lanes(x, 64)
    return y + lanes(y, 32)


def spread(x, start):
    lane = lax.broadcasted_iota(jnp.int32, x.shape, 1)
    return level_sum(jnp.where((lane >= start) & (lane < start + 32), x, 0.0))


DIRS = ((1, 0), (-1, 0), (0, 1), (0, -1), (1, 1), (-1, 1), (1, -1), (-1, -1))
NORTH, SOUTH, EAST, WEST, NE, SE, NW, SW = range(8)


def kernel(n_lat, n_lon, u_hbm, v_hbm, t_hbm, s_hbm, e_hbm, w_hbm,
           result,
           raw, raw2, wet, UV, TS, WE, PE, PW, RW, RE, HUB, KEPT, RINGS,
           TEND, FY, XU, XD, YU, YD, NV, NU, XS,
           in_sem, ready, send_sem, recv_sem):
    lat = lax.axis_index("lat")
    lon = lax.axis_index("lon")

    def start_rank(i, j):
        group = j // BLOCK
        group = jnp.where(group == 2, 3, jnp.where(group == 3, 2, group))
        rank = (group * BLOCK + lax.rem(i, BLOCK)) * (n_lat * n_lon) + i * n_lon + j
        return jnp.where((i == 0) & (j == 0), 2 * BLOCK * n_lat * n_lon - 1, rank)

    peers = [(lax.rem(lat + n_lat + di, n_lat), lax.rem(lon + n_lon + dj, n_lon)) for di, dj in DIRS]
    here = start_rank(lat, lon)
    earlier = [start_rank(*peer) < here for peer in peers]
    first_row, last_row = lax.rem(lat, BLOCK) == 0, lax.rem(lat, BLOCK) == BLOCK - 1
    first_column, last_column = lax.rem(lon, BLOCK) == 0, lax.rem(lon, BLOCK) == BLOCK - 1
    inner_west, inner_east = jnp.logical_not(first_column), jnp.logical_not(last_column)
    relayed = lon // BLOCK >= RELAYED_FROM
    west_relayed = peers[WEST][1] // BLOCK >= RELAYED_FROM
    corner_a, corner_b, corner_hub = first_row & last_column, last_row & first_column, first_row & first_column
    later = [jnp.logical_not(flag) for flag in earlier]
    earlier[SE] = earlier[SE] & jnp.logical_not(corner_a)
    later[SE] = later[SE] & jnp.logical_not(corner_a)
    earlier[NW] = (earlier[NW] & jnp.logical_not(corner_b)) | (corner_b & jnp.logical_not(west_relayed))
    later[NW] = later[NW] & jnp.logical_not(corner_b)

    barrier = pltpu.get_barrier_semaphore()
    expected = 0
    for d in range(8):
        expected = expected + jnp.where(earlier[d], 1, 0)

        @pl.when(later[d])
        def _():
            pl.semaphore_signal(barrier, inc=1, device_id=peers[d], device_id_type=MESH)

    @pl.when(corner_a & jnp.logical_not(relayed))
    def _():
        pl.semaphore_signal(barrier, inc=1, device_id=peers[SE], device_id_type=MESH)

    loads = [
        pltpu.make_async_copy(w_hbm, wet, in_sem.at[0]),
        pltpu.make_async_copy(u_hbm, raw.at[pl.ds(0, 4)], in_sem.at[1]),
        pltpu.make_async_copy(v_hbm, raw.at[pl.ds(4, 4)], in_sem.at[2]),
        pltpu.make_async_copy(t_hbm, raw.at[pl.ds(8, 4)], in_sem.at[3]),
        pltpu.make_async_copy(s_hbm, raw.at[pl.ds(12, 4)], in_sem.at[4]),
        pltpu.make_async_copy(e_hbm, raw2, in_sem.at[5]),
    ]
    for load in loads:
        load.start()
    for load in loads:
        load.wait()

    OWN = pl.ds(PAD, ROWS)
    for k in range(LEVELS):
        UV[U_MAIN + k, OWN, :] = jnp.where(wet[1] > k, raw[k], 0.0)
        UV[V_MAIN + k, OWN, :] = jnp.where(wet[2] > k, raw[4 + k], 0.0)
        TS[k, OWN, :] = jnp.where(wet[0] > k, raw[8 + k], 0.0)
        TS[4 + k, OWN, :] = jnp.where(wet[0] > k, raw[12 + k], 0.0)
    WE[0, OWN, :] = wet[0].astype(F32)
    WE[1, OWN, :] = raw2[...]

    lane32 = lax.broadcasted_iota(jnp.int32, (ROWS, COLS), 1)
    half32 = lax.rem(lane32, 32) < 16
    ring_u = ring([UV[U_MAIN + k, OWN, :] for k in range(LEVELS)])
    ring_v = ring([UV[V_MAIN + k, OWN, :] for k in range(LEVELS)])
    ring_t = ring([TS[k, OWN, :] for k in range(LEVELS)])
    ring_s = ring([TS[4 + k, OWN, :] for k in range(LEVELS)])
    eta8 = lanes(raw2[...], 8)
    wet8 = lanes(ring([wet[0].astype(F32)] * LEVELS), 8)
    spot = lax.rem(lane32, 32)
    PE[0, OWN, :] = jnp.where(half32, ring_u, lanes(ring_v, 16))
    PW[0, OWN, :] = jnp.where(half32, lanes(ring_u, -16), ring_v)
    PE[1, OWN, :] = jnp.where(lane32 < 8, eta8, jnp.where(
        (spot >= 16) & (spot < 24), wet8, jnp.where(half32, ring_t, lanes(ring_s, 16))))
    PW[1, OWN, :] = jnp.where((lane32 >= 8) & (lane32 < 16), eta8, jnp.where(
        spot >= 24, wet8, jnp.where(half32, lanes(ring_t, -16), ring_s)))

    RINGS[0, pl.ds(0, ROWS), :] = ring_t
    RINGS[1, pl.ds(0, ROWS), :] = ring_s
    top, bottom = pl.ds(32, 16), pl.ds(16, 16)
    under, over = pl.ds(0, 16), pl.ds(48, 16)
    every = pl.ds(0, 8)
    parcels = {
        NORTH: [(UV.at[every, pl.ds(36, 12), :], UV.at[every, pl.ds(4, 12), :]),
                (WE.at[:, pl.ds(40, 8), :], WE.at[:, pl.ds(8, 8), :]),
                (TS.at[:, pl.ds(45, 3), :], TS.at[:, pl.ds(13, 3), :])],
        SOUTH: [(UV.at[every, pl.ds(16, 12), :], UV.at[every, pl.ds(48, 12), :]),
                (WE.at[:, pl.ds(16, 8), :], WE.at[:, pl.ds(48, 8), :]),
                (TS.at[:, pl.ds(16, 3), :], TS.at[:, pl.ds(48, 3), :])],
        EAST: [(PE.at[:, OWN, :], RW.at[:, OWN, :])],
        WEST: [(PW.at[:, OWN, :], RE.at[:, OWN, :])],
        NE: [(PE.at[:, pl.ds(36, 12), :], RW.at[:, pl.ds(4, 12), :])],
        SE: [(PE.at[:, pl.ds(16, 12), :], RW.at[:, pl.ds(48, 12), :])],
        NW: [(PW.at[:, pl.ds(36, 12), :], RE.at[:, pl.ds(4, 12), :])],
        SW: [(PW.at[:, pl.ds(16, 12), :], RE.at[:, pl.ds(48, 12), :])],
    }
    first_slot, slots = {}, 0
    for d in range(8):
        first_slot[d] = slots
        slots += len(parcels[d])

    def copies(d):
        return [
            pltpu.make_async_remote_copy(
                src_ref=src, dst_ref=dst, send_sem=send_sem.at[first_slot[d] + i], recv_sem=recv_sem.at[first_slot[d] + i],
                device_id=peers[d], device_id_type=MESH)
            for i, (src, dst) in enumerate(parcels[d])]

    def send_to_earlier(d, also=True):
        @pl.when(earlier[d] & also)
        def _():
            for copy in copies(d):
                copy.start()

    def send_to_later(d, also=True):
        @pl.when(later[d] & also)
        def _():
            pl.semaphore_wait(ready.at[d], 1)
            for copy in copies(d):
                copy.start()

    def wait_from(d):
        for copy in copies(d):
            copy.wait_recv()

    def extra(slot, src, dst, arrival, peer):
        return pltpu.make_async_remote_copy(
            src_ref=src, dst_ref=dst, send_sem=send_sem.at[slot], recv_sem=recv_sem.at[arrival],
            device_id=peer, device_id_type=MESH)

    to_hub = extra(slots, PW.at[:, pl.ds(36, 12), :], HUB.at[:, pl.ds(4, 12), :], slots, peers[NORTH])
    hub_west = extra(slots + 1, HUB.at[:, pl.ds(4, 12), :], RE.at[:, pl.ds(4, 12), :], first_slot[NW], peers[WEST])
    hub_south = extra(slots + 2, RW.at[:, pl.ds(16, 12), :], RW.at[:, pl.ds(48, 12), :], first_slot[SE], peers[SOUTH])

    @pl.when(expected > 0)
    def _():
        pl.semaphore_wait(barrier, expected)

    for d in range(8):
        @pl.when(earlier[d] & jnp.logical_not(corner_b) if d == NW else earlier[d])
        def _():
            pl.semaphore_signal(ready.at[DIRS.index((-DIRS[d][0], -DIRS[d][1]))], inc=1, device_id=peers[d], device_id_type=MESH)

    send_to_earlier(NW, corner_b)
    for d in (EAST, NE, SE, WEST, SW):
        send_to_earlier(d)
    send_to_earlier(NW, jnp.logical_not(corner_b))
    for d in (NORTH, SOUTH):
        send_to_earlier(d)

    @pl.when(corner_b & west_relayed & earlier[NORTH])
    def _():
        to_hub.start()

    def flux_x(q_plane, u_plane, r0, n):
        flow = UV[u_plane, pl.ds(r0, n), :]
        flux = flow * upwind_value(flow, *x_parts(UV[q_plane, pl.ds(r0, n), :]))
        return flux - lanes(flux, 1)

    def flux_y(q_plane, v_plane, r0):
        flow = UV[v_plane, pl.ds(r0, 8), :]
        return flow * upwind_value(flow, *y_parts(UV, q_plane, r0, 8))

    def put_x(q_plane, u_plane, r0, n):
        TEND[q_plane, pl.ds(r0 - LO, n), :] = flux_x(q_plane, u_plane, r0, n)

    def put_y(q_plane, v_plane, r0):
        FY[q_plane, pl.ds(r0 - LO + 1, 8), :] = flux_y(q_plane, v_plane, r0)

    def combine(q_plane):
        for r0 in range(0, SPAN, 16):
            TEND[q_plane, pl.ds(r0, 16), :] = -(TEND[q_plane, pl.ds(r0, 16), :] + (
                FY[q_plane, pl.ds(r0 + 1, 16), :] - FY[q_plane, pl.ds(r0, 16), :]))

    def tracer_x(k, r0, n):
        q0, q1, gm2, gm1, g0, g1, g2 = x_parts(TS[k, pl.ds(PAD + r0, n), :])
        XU[k, pl.ds(r0, n), :] = q0 + correction(gm2, gm1, g0, g1)
        XD[k, pl.ds(r0, n), :] = q1 - correction(g2, g1, g0, gm1)

    def tracer_y(k, r0):
        q0, q1, gm2, gm1, g0, g1, g2 = y_parts(TS, k, PAD - 1 + r0, 8)
        YU[k, pl.ds(r0, 8), :] = q0 + correction(gm2, gm1, g0, g1)
        YD[k, pl.ds(r0, 8), :] = q1 - correction(g2, g1, g0, gm1)

    def local_part(k, carry):
        plane = lax.rem(k, LEVELS)
        for r0 in (16, 32):
            put_x(k, plane, r0, 16)
        for r0 in (23, 31):
            put_y(k, V_MAIN + plane, r0)
        for r0 in (0, 16):
            tracer_x(k, r0, 16)
        for r0 in (8, 16):
            tracer_y(k, r0)
        return carry

    lax.fori_loop(0, 8, local_part, 0)

    send_to_later(NORTH)

    @pl.when(corner_b & west_relayed & later[NORTH])
    def _():
        to_hub.start()

    send_to_later(EAST, inner_east)
    send_to_later(NE, inner_east)
    send_to_later(WEST, inner_west)
    send_to_later(NW, inner_west)
    send_to_later(SOUTH)
    send_to_later(SE, inner_east)
    send_to_later(SW, inner_west)
    for d in (EAST, NE, SE):
        send_to_later(d, last_column)

    for d in (NORTH, SOUTH):
        wait_from(d)

    zero16 = jnp.zeros((16, COLS), F32)

    @pl.when(lat == 0)
    def _():
        for k in range(8):
            UV[k, under, :] = zero16
            TS[k, under, :] = zero16
        WE[0, under, :] = zero16
        WE[1, under, :] = zero16

    @pl.when(lat == n_lat - 1)
    def _():
        for k in range(8):
            UV[k, over, :] = zero16
            TS[k, over, :] = zero16
        WE[0, over, :] = zero16
        WE[1, over, :] = zero16

    def edge_part(k, carry):
        plane = lax.rem(k, LEVELS)
        for r0 in (8, 48):
            put_x(k, plane, r0, 8)
        for r0 in (7, 15, 39, 47):
            put_y(k, V_MAIN + plane, r0)
        combine(k)
        for r0 in (0, 24, 32):
            tracer_y(k, r0)
        return carry

    lax.fori_loop(0, 8, edge_part, 0)

    lane64 = lax.broadcasted_iota(jnp.int32, (EXT, COLS), 1)
    half = lax.rem(lane64, 32) < 16
    lane = lax.broadcasted_iota(jnp.int32, (SPAN, COLS), 1)
    level = (lane // 32).astype(F32)
    BAND = pl.ds(LO, SPAN)
    LOWER = pl.ds(LO - 1, SPAN)
    ALL = pl.ds(0, SPAN)
    scale = STEP / SUB
    own = slice(PAD - LO, PAD - LO + ROWS)

    def band(x):
        return x[LO:LO + SPAN]

    def laid(main):
        return jnp.where(lane < 48, lanes(main, 16), lanes(main, -48))

    def faces(w):
        at = band(w)
        return jnp.minimum(at, lanes(at, -1)), jnp.minimum(at, band(rows(w, -1)))

    def main_sum(ref, first, where_rows, limit=None):
        total = None
        for k in range(LEVELS):
            term = ref[first + k, where_rows, :]
            if limit is not None:
                term = jnp.where(limit > k, term, 0.0)
            total = term if total is None else total + term
        return total

    def pair_sum(sw, se):
        low = lane < 64
        folded = jnp.where(low, sw, se) + lanes(jnp.where(low, se, sw), 64)
        return folded + lanes(folded, -32)

    def substeps(height, tx, ty, tym, fx, fy, cx, cy):
        for n in range(SUB):
            below = tym if n == 0 else rows(ty, 1)
            height = height - (tx - lanes(tx, 1) + ty - below)
            tx = tx - cx * (lanes(height, -1) - height) + fx
            ty = ty - cy * (rows(height, -1) - height) + fy
        return height, tx, ty

    wx_main, wy_main = faces(WE[0])
    push_x = main_sum(TEND, U_MAIN, ALL, wx_main)
    push_y = main_sum(TEND, V_MAIN, ALL, wy_main)
    tx0 = main_sum(UV, U_MAIN, BAND)
    ty0 = main_sum(UV, V_MAIN, BAND)
    tym_main = main_sum(UV, V_MAIN, LOWER)
    h_main, tx_main, ty_main = substeps(
        WE[1, BAND, :], tx0, ty0, tym_main, scale * push_x, scale * push_y, WAVE * wx_main, WAVE * wy_main)
    gain_x = (tx_main - (tx0 + STEP * push_x)) / jnp.maximum(wx_main, 1.0)
    gain_y = (ty_main - (ty0 + STEP * push_y)) / jnp.maximum(wy_main, 1.0)
    for k in range(LEVELS):
        NU[k] = jnp.where(wx_main > k, UV[U_MAIN + k, BAND, :] + STEP * TEND[U_MAIN + k, ALL, :] + gain_x, 0.0)[own]
        NV[k] = jnp.where(wy_main > k, UV[V_MAIN + k, BAND, :] + STEP * TEND[V_MAIN + k, ALL, :] + gain_y, 0.0)
    KEPT[0] = h_main
    for slot, plane in enumerate((tx0, ty0, tym_main, push_x, push_y, wx_main, wy_main, WE[1, BAND, :])):
        KEPT[slot + 1] = laid(plane)
    RINGS[2] = ring([UV[U_MAIN + k] for k in range(LEVELS)])
    RINGS[3] = ring([UV[V_MAIN + k] for k in range(LEVELS)])
    RINGS[4] = ring([WE[0]] * LEVELS)

    def clear_poles(ref):
        @pl.when(lat == 0)
        def _():
            for i in range(2):
                ref[i, under, :] = zero16

        @pl.when(lat == n_lat - 1)
        def _():
            for i in range(2):
                ref[i, over, :] = zero16

    def strip(u_plane, v_plane):
        def one(i, carry):
            q_plane = u_plane + i * (v_plane - u_plane)
            for r0 in (8, 24, 40):
                put_x(q_plane, u_plane, r0, 16)
            for r0 in (7, 15, 23, 31, 39, 47):
                put_y(q_plane, v_plane, r0)
            combine(q_plane)
            return carry

        lax.fori_loop(0, 2, one, 0)

    def western_strip():
        for d in (NE, SE):
            wait_from(d)
        clear_poles(RW)
        UV[U_SW] = jnp.where(half, RW[0], RINGS[2])
        UV[V_SW] = jnp.where(half, lanes(RW[0], -16), RINGS[3])
        strip(U_SW, V_SW)

    def eastern_strip():
        for d in (WEST, NW, SW):
            wait_from(d)
        clear_poles(RE)
        UV[U_SE] = jnp.where(half, RINGS[2], lanes(RE[0], 16))
        UV[V_SE] = jnp.where(half, RINGS[3], RE[0])
        strip(U_SE, V_SE)

    @pl.when(first_column)
    def _():
        eastern_strip()

    for d in (WEST, NW, SW):
        send_to_later(d, first_column)

    @pl.when(corner_hub & west_relayed)
    def _():
        to_hub.wait_recv()
        hub_west.start()

    wait_from(EAST)

    @pl.when(corner_hub)
    def _():
        hub_south.start()

    western_strip()

    @pl.when(inner_west)
    def _():
        eastern_strip()

    in_sw, in_se = lane < 24, (lane >= 72) & (lane < 96)

    def kept(slot, sides):
        return jnp.where(in_sw | in_se, sides, KEPT[slot])

    wx_sw, wy_sw = faces(jnp.where(half, lanes(RW[1], -8), RINGS[4]))
    wx_se, wy_se = faces(jnp.where(half, RINGS[4], lanes(RE[1], -8)))
    wx_side = kept(6, jnp.where(lane < 64, wx_sw, wx_se))
    wy_side = kept(7, jnp.where(lane < 64, wy_sw, wy_se))
    eta_side = jnp.where(lane < 16, lanes(RW[1, BAND, :], 8), jnp.where(
        (lane >= 80) & (lane < 88), lanes(RE[1, BAND, :], 72), KEPT[8]))

    def masked(plane, limit):
        return jnp.where(limit > level, TEND[plane, ALL, :], 0.0)

    push_x_side = kept(4, pair_sum(masked(U_SW, wx_sw), masked(U_SE, wx_se)))
    push_y_side = kept(5, pair_sum(masked(V_SW, wy_sw), masked(V_SE, wy_se)))
    tx0_side = kept(1, pair_sum(UV[U_SW, BAND, :], UV[U_SE, BAND, :]))
    ty0_side = kept(2, pair_sum(UV[V_SW, BAND, :], UV[V_SE, BAND, :]))
    tym_side = kept(3, pair_sum(UV[V_SW, LOWER, :], UV[V_SE, LOWER, :]))

    h_side, tx_side, ty_side = substeps(
        eta_side, tx0_side, ty0_side, tym_side, scale * push_x_side, scale * push_y_side, WAVE * wx_side, WAVE * wy_side)

    result[16] = jnp.where(lane < 16, lanes(h_side, -16), jnp.where(lane >= 112, lanes(h_side, 48), KEPT[0]))[own]

    gain_x = (tx_side - (tx0_side + STEP * push_x_side)) / jnp.maximum(wx_side, 1.0)
    gain_y = (ty_side - (ty0_side + STEP * push_y_side)) / jnp.maximum(wy_side, 1.0)

    def fresh_side(plane, depth, gain):
        return jnp.where(depth > level, UV[plane, BAND, :] + STEP * TEND[plane, ALL, :] + gain, 0.0)

    u_sw = fresh_side(U_SW, wx_sw, spread(gain_x, 0))[own]
    u_se = fresh_side(U_SE, wx_se, spread(gain_x, 64))[own]
    v_sw = fresh_side(V_SW, wy_sw, spread(gain_y, 0))
    v_se = fresh_side(V_SE, wy_se, spread(gain_y, 64))

    for k in range(LEVELS):
        fresh = jnp.where(lane32 < 12, lanes(u_sw, -(32 * k + 16)), jnp.where(lane32 >= 116, lanes(u_se, 112 - 32 * k), NU[k]))
        NU[k] = fresh
        result[k] = fresh
        fresh = jnp.where(lane < 12, lanes(v_sw, -(32 * k + 16)), jnp.where(lane >= 116, lanes(v_se, 112 - 32 * k), NV[k]))
        NV[k] = fresh
        result[4 + k] = fresh[own]

    ring_t, ring_s = RINGS[0, pl.ds(0, ROWS), :], RINGS[1, pl.ds(0, ROWS), :]

    def side_flux(cells, flow):
        flux = flow * upwind_value(flow, *x_parts(cells))
        return flux - lanes(flux, 1)

    XS[0] = side_flux(jnp.where(half32, RW[1, OWN, :], ring_t), u_sw)
    XS[1] = side_flux(jnp.where(half32, ring_t, lanes(RE[1, OWN, :], 16)), u_se)
    XS[2] = side_flux(jnp.where(half32, lanes(RW[1, OWN, :], -16), ring_s), u_sw)
    XS[3] = side_flux(jnp.where(half32, ring_s, RE[1, OWN, :]), u_se)

    for field in range(2):
        for k in range(LEVELS):
            p = 4 * field + k
            flow = NU[k]
            flux = flow * jnp.where(flow >= 0.0, XU[p], XD[p])
            div_x = flux - lanes(flux, 1)
            div_x = jnp.where(lane32 < 8, lanes(XS[2 * field], -(32 * k + 16)),
                              jnp.where(lane32 >= 120, lanes(XS[2 * field + 1], 112 - 32 * k), div_x))
            up = NV[k, pl.ds(8, ROWS), :]
            down = NV[k, pl.ds(7, ROWS), :]
            flux_up = up * jnp.where(up >= 0.0, YU[p, pl.ds(1, ROWS), :], YD[p, pl.ds(1, ROWS), :])
            flux_down = down * jnp.where(down >= 0.0, YU[p, pl.ds(0, ROWS), :], YD[p, pl.ds(0, ROWS), :])
            cells = TS[p, OWN, :]
            fresh = cells - STEP * (div_x + (flux_up - flux_down))
            result[8 + p] = jnp.where(wet[0] > k, fresh, 0.0)

    for d in range(8):
        if d in (SE, NW):
            @pl.when(earlier[d] | later[d])
            def _():
                for copy in copies(d):
                    copy.wait_send()
        else:
            for copy in copies(d):
                copy.wait_send()

    @pl.when(corner_hub)
    def _():
        hub_south.wait_send()

    @pl.when(corner_hub & west_relayed)
    def _():
        hub_west.wait_send()

    @pl.when(corner_b & west_relayed)
    def _():
        to_hub.wait_send()


def deal(result, u_out, v_out, t_out, s_out, e_out, sem):
    copies = [pltpu.make_async_copy(result.at[pl.ds(LEVELS * i, LEVELS)], out, sem.at[i])
              for i, out in enumerate((u_out, v_out, t_out, s_out))]
    copies.append(pltpu.make_async_copy(result.at[16], e_out, sem.at[4]))
    for copy in copies:
        copy.start()
    for copy in copies:
        copy.wait()


def solution(mesh):
    n_lat, n_lon = mesh.shape["lat"], mesh.shape["lon"]

    def step(u_vel, v_vel, temp, salt, eta, wet_levels):
        levels = jax.ShapeDtypeStruct((LEVELS, ROWS, COLS), F32)
        plane = jax.ShapeDtypeStruct((ROWS, COLS), F32)
        hbm = pl.BlockSpec(memory_space=pl.ANY)
        vmem = pl.BlockSpec(memory_space=pltpu.VMEM)

        def body(*refs):
            kernel(n_lat, n_lon, *refs)

        def buffer(*shape):
            return pltpu.VMEM(shape, F32)

        result = pl.pallas_call(
            body,
            out_shape=pltpu.VMEM((17, ROWS, COLS), F32),
            in_specs=[hbm] * 6,
            out_specs=vmem,
            scratch_shapes=[
                buffer(16, ROWS, COLS),
                buffer(ROWS, COLS),
                pltpu.VMEM((3, ROWS, COLS), jnp.int32),
                buffer(12, EXT, COLS),
                buffer(8, EXT, COLS),
                buffer(2, EXT, COLS),
                buffer(2, EXT, COLS),
                buffer(2, EXT, COLS),
                buffer(2, EXT, COLS),
                buffer(2, EXT, COLS),
                buffer(2, PAD, COLS),
                buffer(9, SPAN, COLS),
                buffer(5, EXT, COLS),
                buffer(12, SPAN, COLS),
                buffer(12, SPAN + 8, COLS),
                buffer(8, ROWS, COLS),
                buffer(8, ROWS, COLS),
                buffer(8, 40, COLS),
                buffer(8, 40, COLS),
                buffer(4, SPAN, COLS),
                buffer(4, ROWS, COLS),
                buffer(4, ROWS, COLS),
                pltpu.SemaphoreType.DMA((6,)),
                pltpu.SemaphoreType.REGULAR((8,)),
                pltpu.SemaphoreType.DMA((15,)),
                pltpu.SemaphoreType.DMA((15,)),
            ],
            compiler_params=pltpu.CompilerParams(collective_id=0, has_side_effects=True),
        )(u_vel, v_vel, temp, salt, eta, wet_levels)
        return pl.pallas_call(
            deal,
            out_shape=(levels, levels, levels, levels, plane),
            in_specs=[vmem],
            out_specs=(hbm,) * 5,
            scratch_shapes=[pltpu.SemaphoreType.DMA((5,))],
            compiler_params=pltpu.CompilerParams(vmem_limit_bytes=1 << 20),
        )(result)

    tile, flat = P(None, "lat", "lon"), P("lat", "lon")
    return jax.shard_map(
        step, mesh=mesh, in_specs=(tile, tile, tile, tile, flat, tile),
        out_specs=(tile, tile, tile, tile, flat), check_vma=False)
```

```python
import jax
import jax.numpy as jnp
from jax import lax
from jax.experimental import pallas as pl
from jax.experimental.pallas import tpu as pltpu
from jax.sharding import PartitionSpec as P

MESH = pl.DeviceIdType.MESH
F32 = jnp.float32
LEVELS = 4
SUB = 8
BLOCK = 8
RELAYED_FROM = 2
STEP = 0.4
WAVE = 0.45 / 4
EPS = 1e-6 * 12.0 / 13.0
ROWS = 32
COLS = 128
PAD = 16
EXT = ROWS + 2 * PAD
LO = 8
SPAN = 48

U_MAIN, V_MAIN, U_SW, U_SE, V_SW, V_SE = 0, 4, 8, 9, 10, 11


def lanes(x, shift):
    shift = shift % COLS
    return x if shift == 0 else pltpu.roll(x, shift, 1)


def rows(x, shift):
    return pltpu.roll(x, shift % x.shape[0], 0)


def correction(d0, d1, d2, d3):
    x0 = d1 - d0
    x1 = d2 - d1
    x2 = d3 - d2
    m1 = d1 + d1
    m2 = d2 + d2
    y0 = x0 + m1
    y1 = d1 + d2
    y2 = x2 - m2
    e0 = x0 * x0 + (y0 * y0) * (3.0 / 13.0) + EPS
    e1 = x1 * x1 + (y1 * y1) * (3.0 / 13.0) + EPS
    e2 = x2 * x2 + (y2 * y2) * (3.0 / 13.0) + EPS
    a0 = e1 * e2
    a1 = e0 * e2
    a2 = e0 * e1
    w0 = a0 * a0
    w1 = (a1 * a1) * 6.0
    w2 = (a2 * a2) * 3.0
    top = w0 * (5.0 * d1 - 2.0 * d0) + w1 * (d1 + m2) + w2 * (4.0 * d2 - d3)
    return top / ((w0 + w1 + w2) * 6.0)


def upwind_value(flow, q0, q1, gm2, gm1, g0, g1, g2):
    ahead = flow >= 0.0
    fix = correction(jnp.where(ahead, gm2, g2), jnp.where(ahead, gm1, g1), g0, jnp.where(ahead, g1, gm1))
    return jnp.where(ahead, q0 + fix, q1 - fix)


def x_parts(q):
    q1 = lanes(q, -1)
    g = q1 - q
    return q, q1, lanes(g, 2), lanes(g, 1), g, lanes(g, -1), lanes(g, -2)


def y_parts(ref, k, r0, n):
    q = [ref[k, pl.ds(r0 + s, n), :] for s in range(-2, 4)]
    g = [q[i + 1] - q[i] for i in range(5)]
    return q[2], q[3], g[0], g[1], g[2], g[3], g[4]


def ring(parts):
    lane = lax.broadcasted_iota(jnp.int32, parts[0].shape, 1)
    out = lanes(parts[0], 16)
    for k in range(1, LEVELS):
        out = jnp.where(lane >= 32 * k, lanes(parts[k], 32 * k + 16), out)
    return out


def level_sum(x):
    y = x + lanes(x, 64)
    return y + lanes(y, 32)


def spread(x, start):
    lane = lax.broadcasted_iota(jnp.int32, x.shape, 1)
    return level_sum(jnp.where((lane >= start) & (lane < start + 32), x, 0.0))


DIRS = ((1, 0), (-1, 0), (0, 1), (0, -1), (1, 1), (-1, 1), (1, -1), (-1, -1))
NORTH, SOUTH, EAST, WEST, NE, SE, NW, SW = range(8)


def kernel(n_lat, n_lon, u_hbm, v_hbm, t_hbm, s_hbm, e_hbm, w_hbm,
           result,
           raw, raw2, wet, UV, TS, WE, PE, PW, RW, RE, HUB, KEPT, RINGS,
           TEND, FY, XU, XD, YU, YD, NV, NU, XS,
           in_sem, ready, send_sem, recv_sem):
    loads = [
        pltpu.make_async_copy(w_hbm, wet, in_sem.at[0]),
        pltpu.make_async_copy(u_hbm, raw.at[pl.ds(0, 4)], in_sem.at[1]),
        pltpu.make_async_copy(v_hbm, raw.at[pl.ds(4, 4)], in_sem.at[2]),
        pltpu.make_async_copy(t_hbm, raw.at[pl.ds(8, 4)], in_sem.at[3]),
        pltpu.make_async_copy(s_hbm, raw.at[pl.ds(12, 4)], in_sem.at[4]),
        pltpu.make_async_copy(e_hbm, raw2, in_sem.at[5]),
    ]
    for load in loads:
        load.start()

    lat = lax.axis_index("lat")
    lon = lax.axis_index("lon")

    def start_rank(i, j):
        group = j // BLOCK
        group = jnp.where(group == 2, 3, jnp.where(group == 3, 2, group))
        rank = (group * BLOCK + lax.rem(i, BLOCK)) * (n_lat * n_lon) + i * n_lon + j
        return jnp.where((i == 0) & (j == 0), 2 * BLOCK * n_lat * n_lon - 1, rank)

    peers = [(lax.rem(lat + n_lat + di, n_lat), lax.rem(lon + n_lon + dj, n_lon)) for di, dj in DIRS]
    here = start_rank(lat, lon)
    earlier = [start_rank(*peer) < here for peer in peers]
    first_row, last_row = lax.rem(lat, BLOCK) == 0, lax.rem(lat, BLOCK) == BLOCK - 1
    first_column, last_column = lax.rem(lon, BLOCK) == 0, lax.rem(lon, BLOCK) == BLOCK - 1
    inner_west, inner_east = jnp.logical_not(first_column), jnp.logical_not(last_column)
    relayed = lon // BLOCK >= RELAYED_FROM
    west_relayed = peers[WEST][1] // BLOCK >= RELAYED_FROM
    corner_a, corner_b, corner_hub = first_row & last_column, last_row & first_column, first_row & first_column
    later = [jnp.logical_not(flag) for flag in earlier]
    earlier[SE] = earlier[SE] & jnp.logical_not(corner_a)
    later[SE] = later[SE] & jnp.logical_not(corner_a)
    earlier[NW] = (earlier[NW] & jnp.logical_not(corner_b)) | (corner_b & jnp.logical_not(west_relayed))
    later[NW] = later[NW] & jnp.logical_not(corner_b)

    barrier = pltpu.get_barrier_semaphore()
    expected = 0
    for d in range(8):
        expected = expected + jnp.where(earlier[d], 1, 0)

        @pl.when(later[d])
        def _():
            pl.semaphore_signal(barrier, inc=1, device_id=peers[d], device_id_type=MESH)

    @pl.when(corner_a & jnp.logical_not(relayed))
    def _():
        pl.semaphore_signal(barrier, inc=1, device_id=peers[SE], device_id_type=MESH)

    for load in loads:
        load.wait()

    OWN = pl.ds(PAD, ROWS)

    def wetted(first, face):
        return [jnp.where(wet[face] > k, raw[first + k], 0.0) for k in range(LEVELS)]

    lane32 = lax.broadcasted_iota(jnp.int32, (ROWS, COLS), 1)
    half32 = lax.rem(lane32, 32) < 16
    ring_u, ring_v, ring_t, ring_s = ring(wetted(0, 1)), ring(wetted(4, 2)), ring(wetted(8, 0)), ring(wetted(12, 0))
    eta8 = lanes(raw2[...], 8)
    wet8 = lanes(ring([wet[0].astype(F32)] * LEVELS), 8)
    spot = lax.rem(lane32, 32)
    PE[0, OWN, :] = jnp.where(half32, ring_u, lanes(ring_v, 16))
    PW[0, OWN, :] = jnp.where(half32, lanes(ring_u, -16), ring_v)
    PE[1, OWN, :] = jnp.where(lane32 < 8, eta8, jnp.where(
        (spot >= 16) & (spot < 24), wet8, jnp.where(half32, ring_t, lanes(ring_s, 16))))
    PW[1, OWN, :] = jnp.where((lane32 >= 8) & (lane32 < 16), eta8, jnp.where(
        spot >= 24, wet8, jnp.where(half32, lanes(ring_t, -16), ring_s)))

    RINGS[0, pl.ds(0, ROWS), :] = ring_t
    RINGS[1, pl.ds(0, ROWS), :] = ring_s
    top, bottom = pl.ds(32, 16), pl.ds(16, 16)
    under, over = pl.ds(0, 16), pl.ds(48, 16)
    every = pl.ds(0, 8)
    parcels = {
        NORTH: [(UV.at[every, pl.ds(36, 12), :], UV.at[every, pl.ds(4, 12), :]),
                (WE.at[:, pl.ds(40, 8), :], WE.at[:, pl.ds(8, 8), :]),
                (TS.at[:, pl.ds(45, 3), :], TS.at[:, pl.ds(13, 3), :])],
        SOUTH: [(UV.at[every, pl.ds(16, 12), :], UV.at[every, pl.ds(48, 12), :]),
                (WE.at[:, pl.ds(16, 8), :], WE.at[:, pl.ds(48, 8), :]),
                (TS.at[:, pl.ds(16, 3), :], TS.at[:, pl.ds(48, 3), :])],
        EAST: [(PE.at[:, OWN, :], RW.at[:, OWN, :])],
        WEST: [(PW.at[:, OWN, :], RE.at[:, OWN, :])],
        NE: [(PE.at[:, pl.ds(36, 12), :], RW.at[:, pl.ds(4, 12), :])],
        SE: [(PE.at[:, pl.ds(16, 12), :], RW.at[:, pl.ds(48, 12), :])],
        NW: [(PW.at[:, pl.ds(36, 12), :], RE.at[:, pl.ds(4, 12), :])],
        SW: [(PW.at[:, pl.ds(16, 12), :], RE.at[:, pl.ds(48, 12), :])],
    }
    first_slot, slots = {}, 0
    for d in range(8):
        first_slot[d] = slots
        slots += len(parcels[d])

    def copies(d):
        return [
            pltpu.make_async_remote_copy(
                src_ref=src, dst_ref=dst, send_sem=send_sem.at[first_slot[d] + i], recv_sem=recv_sem.at[first_slot[d] + i],
                device_id=peers[d], device_id_type=MESH)
            for i, (src, dst) in enumerate(parcels[d])]

    def send_to_earlier(d, also=True):
        @pl.when(earlier[d] & also)
        def _():
            for copy in copies(d):
                copy.start()

    def send_to_later(d, also=True):
        @pl.when(later[d] & also)
        def _():
            pl.semaphore_wait(ready.at[d], 1)
            for copy in copies(d):
                copy.start()

    def wait_from(d):
        for copy in copies(d):
            copy.wait_recv()

    def extra(slot, src, dst, arrival, peer):
        return pltpu.make_async_remote_copy(
            src_ref=src, dst_ref=dst, send_sem=send_sem.at[slot], recv_sem=recv_sem.at[arrival],
            device_id=peer, device_id_type=MESH)

    to_hub = extra(slots, PW.at[:, pl.ds(36, 12), :], HUB.at[:, pl.ds(4, 12), :], slots, peers[NORTH])
    hub_west = extra(slots + 1, HUB.at[:, pl.ds(4, 12), :], RE.at[:, pl.ds(4, 12), :], first_slot[NW], peers[WEST])
    hub_south = extra(slots + 2, RW.at[:, pl.ds(16, 12), :], RW.at[:, pl.ds(48, 12), :], first_slot[SE], peers[SOUTH])

    @pl.when(expected > 0)
    def _():
        pl.semaphore_wait(barrier, expected)

    for d in range(8):
        @pl.when(earlier[d] & jnp.logical_not(corner_b) if d == NW else earlier[d])
        def _():
            pl.semaphore_signal(ready.at[DIRS.index((-DIRS[d][0], -DIRS[d][1]))], inc=1, device_id=peers[d], device_id_type=MESH)

    send_to_earlier(NW, corner_b)
    for d in (EAST, NE, SE, WEST, SW):
        send_to_earlier(d)
    send_to_earlier(NW, jnp.logical_not(corner_b))

    for first, face, planes in ((0, 1, UV), (4, 2, UV), (8, 0, TS), (12, 0, TS)):
        for k, plane in enumerate(wetted(first, face)):
            planes[first % 8 + k, OWN, :] = plane
    WE[0, OWN, :] = wet[0].astype(F32)
    WE[1, OWN, :] = raw2[...]

    for d in (NORTH, SOUTH):
        send_to_earlier(d)

    @pl.when(corner_b & west_relayed & earlier[NORTH])
    def _():
        to_hub.start()

    def flux_x(q_plane, u_plane, r0, n):
        flow = UV[u_plane, pl.ds(r0, n), :]
        flux = flow * upwind_value(flow, *x_parts(UV[q_plane, pl.ds(r0, n), :]))
        return flux - lanes(flux, 1)

    def flux_y(q_plane, v_plane, r0):
        flow = UV[v_plane, pl.ds(r0, 8), :]
        return flow * upwind_value(flow, *y_parts(UV, q_plane, r0, 8))

    def put_x(q_plane, u_plane, r0, n):
        TEND[q_plane, pl.ds(r0 - LO, n), :] = flux_x(q_plane, u_plane, r0, n)

    def put_y(q_plane, v_plane, r0):
        FY[q_plane, pl.ds(r0 - LO + 1, 8), :] = flux_y(q_plane, v_plane, r0)

    def combine(q_plane):
        for r0 in range(0, SPAN, 16):
            TEND[q_plane, pl.ds(r0, 16), :] = -(TEND[q_plane, pl.ds(r0, 16), :] + (
                FY[q_plane, pl.ds(r0 + 1, 16), :] - FY[q_plane, pl.ds(r0, 16), :]))

    def tracer_x(k, r0, n):
        q0, q1, gm2, gm1, g0, g1, g2 = x_parts(TS[k, pl.ds(PAD + r0, n), :])
        XU[k, pl.ds(r0, n), :] = q0 + correction(gm2, gm1, g0, g1)
        XD[k, pl.ds(r0, n), :] = q1 - correction(g2, g1, g0, gm1)

    def tracer_y(k, r0):
        q0, q1, gm2, gm1, g0, g1, g2 = y_parts(TS, k, PAD - 1 + r0, 8)
        YU[k, pl.ds(r0, 8), :] = q0 + correction(gm2, gm1, g0, g1)
        YD[k, pl.ds(r0, 8), :] = q1 - correction(g2, g1, g0, gm1)

    def local_part(k, carry):
        plane = lax.rem(k, LEVELS)
        for r0 in (16, 32):
            put_x(k, plane, r0, 16)
        for r0 in (23, 31):
            put_y(k, V_MAIN + plane, r0)
        for r0 in (0, 16):
            tracer_x(k, r0, 16)
        for r0 in (8, 16):
            tracer_y(k, r0)
        return carry

    lax.fori_loop(0, 8, local_part, 0)

    send_to_later(NORTH)

    @pl.when(corner_b & west_relayed & later[NORTH])
    def _():
        to_hub.start()

    send_to_later(EAST, inner_east)
    send_to_later(NE, inner_east)
    send_to_later(WEST, inner_west)
    send_to_later(NW, inner_west)
    send_to_later(SOUTH)
    send_to_later(SE, inner_east)
    send_to_later(SW, inner_west)
    for d in (EAST, NE, SE):
        send_to_later(d, last_column)

    for d in (NORTH, SOUTH):
        wait_from(d)

    zero16 = jnp.zeros((16, COLS), F32)

    @pl.when(lat == 0)
    def _():
        for k in range(8):
            UV[k, under, :] = zero16
            TS[k, under, :] = zero16
        WE[0, under, :] = zero16
        WE[1, under, :] = zero16

    @pl.when(lat == n_lat - 1)
    def _():
        for k in range(8):
            UV[k, over, :] = zero16
            TS[k, over, :] = zero16
        WE[0, over, :] = zero16
        WE[1, over, :] = zero16

    def edge_part(k, carry):
        plane = lax.rem(k, LEVELS)
        for r0 in (8, 48):
            put_x(k, plane, r0, 8)
        for r0 in (7, 15, 39, 47):
            put_y(k, V_MAIN + plane, r0)
        combine(k)
        for r0 in (0, 24, 32):
            tracer_y(k, r0)
        return carry

    lax.fori_loop(0, 8, edge_part, 0)

    lane64 = lax.broadcasted_iota(jnp.int32, (EXT, COLS), 1)
    half = lax.rem(lane64, 32) < 16
    lane = lax.broadcasted_iota(jnp.int32, (SPAN, COLS), 1)
    level = (lane // 32).astype(F32)
    BAND = pl.ds(LO, SPAN)
    LOWER = pl.ds(LO - 1, SPAN)
    ALL = pl.ds(0, SPAN)
    scale = STEP / SUB
    own = slice(PAD - LO, PAD - LO + ROWS)

    def band(x):
        return x[LO:LO + SPAN]

    def laid(main):
        return jnp.where(lane < 48, lanes(main, 16), lanes(main, -48))

    def faces(w):
        at = band(w)
        return jnp.minimum(at, lanes(at, -1)), jnp.minimum(at, band(rows(w, -1)))

    def main_sum(ref, first, where_rows, limit=None):
        total = None
        for k in range(LEVELS):
            term = ref[first + k, where_rows, :]
            if limit is not None:
                term = jnp.where(limit > k, term, 0.0)
            total = term if total is None else total + term
        return total

    def pair_sum(sw, se):
        low = lane < 64
        folded = jnp.where(low, sw, se) + lanes(jnp.where(low, se, sw), 64)
        return folded + lanes(folded, -32)

    def substeps(height, tx, ty, tym, fx, fy, cx, cy):
        for n in range(SUB):
            below = tym if n == 0 else rows(ty, 1)
            height = height - (tx - lanes(tx, 1) + ty - below)
            tx = tx - cx * (lanes(height, -1) - height) + fx
            ty = ty - cy * (rows(height, -1) - height) + fy
        return height, tx, ty

    wx_main, wy_main = faces(WE[0])
    push_x = main_sum(TEND, U_MAIN, ALL, wx_main)
    push_y = main_sum(TEND, V_MAIN, ALL, wy_main)
    tx0 = main_sum(UV, U_MAIN, BAND)
    ty0 = main_sum(UV, V_MAIN, BAND)
    tym_main = main_sum(UV, V_MAIN, LOWER)
    h_main, tx_main, ty_main = substeps(
        WE[1, BAND, :], tx0, ty0, tym_main, scale * push_x, scale * push_y, WAVE * wx_main, WAVE * wy_main)
    gain_x = (tx_main - (tx0 + STEP * push_x)) / jnp.maximum(wx_main, 1.0)
    gain_y = (ty_main - (ty0 + STEP * push_y)) / jnp.maximum(wy_main, 1.0)
    for k in range(LEVELS):
        NU[k] = jnp.where(wx_main > k, UV[U_MAIN + k, BAND, :] + STEP * TEND[U_MAIN + k, ALL, :] + gain_x, 0.0)[own]
        NV[k] = jnp.where(wy_main > k, UV[V_MAIN + k, BAND, :] + STEP * TEND[V_MAIN + k, ALL, :] + gain_y, 0.0)
    KEPT[0] = h_main
    for slot, plane in enumerate((tx0, ty0, tym_main, push_x, push_y, wx_main, wy_main, WE[1, BAND, :])):
        KEPT[slot + 1] = laid(plane)
    RINGS[2] = ring([UV[U_MAIN + k] for k in range(LEVELS)])
    RINGS[3] = ring([UV[V_MAIN + k] for k in range(LEVELS)])
    RINGS[4] = ring([WE[0]] * LEVELS)

    def clear_poles(ref):
        @pl.when(lat == 0)
        def _():
            for i in range(2):
                ref[i, under, :] = zero16

        @pl.when(lat == n_lat - 1)
        def _():
            for i in range(2):
                ref[i, over, :] = zero16

    def strip(u_plane, v_plane):
        def one(i, carry):
            q_plane = u_plane + i * (v_plane - u_plane)
            for r0 in (8, 24, 40):
                put_x(q_plane, u_plane, r0, 16)
            for r0 in (7, 15, 23, 31, 39, 47):
                put_y(q_plane, v_plane, r0)
            combine(q_plane)
            return carry

        lax.fori_loop(0, 2, one, 0)

    def western_strip():
        for d in (NE, SE):
            wait_from(d)
        clear_poles(RW)
        UV[U_SW] = jnp.where(half, RW[0], RINGS[2])
        UV[V_SW] = jnp.where(half, lanes(RW[0], -16), RINGS[3])
        strip(U_SW, V_SW)

    def eastern_strip():
        for d in (WEST, NW, SW):
            wait_from(d)
        clear_poles(RE)
        UV[U_SE] = jnp.where(half, RINGS[2], lanes(RE[0], 16))
        UV[V_SE] = jnp.where(half, RINGS[3], RE[0])
        strip(U_SE, V_SE)

    @pl.when(first_column)
    def _():
        eastern_strip()

    for d in (WEST, NW, SW):
        send_to_later(d, first_column)

    @pl.when(corner_hub & west_relayed)
    def _():
        to_hub.wait_recv()
        hub_west.start()

    wait_from(EAST)

    @pl.when(corner_hub)
    def _():
        hub_south.start()

    western_strip()

    @pl.when(inner_west)
    def _():
        eastern_strip()

    in_sw, in_se = lane < 24, (lane >= 72) & (lane < 96)

    def kept(slot, sides):
        return jnp.where(in_sw | in_se, sides, KEPT[slot])

    wx_sw, wy_sw = faces(jnp.where(half, lanes(RW[1], -8), RINGS[4]))
    wx_se, wy_se = faces(jnp.where(half, RINGS[4], lanes(RE[1], -8)))
    wx_side = kept(6, jnp.where(lane < 64, wx_sw, wx_se))
    wy_side = kept(7, jnp.where(lane < 64, wy_sw, wy_se))
    eta_side = jnp.where(lane < 16, lanes(RW[1, BAND, :], 8), jnp.where(
        (lane >= 80) & (lane < 88), lanes(RE[1, BAND, :], 72), KEPT[8]))

    def masked(plane, limit):
        return jnp.where(limit > level, TEND[plane, ALL, :], 0.0)

    push_x_side = kept(4, pair_sum(masked(U_SW, wx_sw), masked(U_SE, wx_se)))
    push_y_side = kept(5, pair_sum(masked(V_SW, wy_sw), masked(V_SE, wy_se)))
    tx0_side = kept(1, pair_sum(UV[U_SW, BAND, :], UV[U_SE, BAND, :]))
    ty0_side = kept(2, pair_sum(UV[V_SW, BAND, :], UV[V_SE, BAND, :]))
    tym_side = kept(3, pair_sum(UV[V_SW, LOWER, :], UV[V_SE, LOWER, :]))

    h_side, tx_side, ty_side = substeps(
        eta_side, tx0_side, ty0_side, tym_side, scale * push_x_side, scale * push_y_side, WAVE * wx_side, WAVE * wy_side)

    result[16] = jnp.where(lane < 16, lanes(h_side, -16), jnp.where(lane >= 112, lanes(h_side, 48), KEPT[0]))[own]

    gain_x = (tx_side - (tx0_side + STEP * push_x_side)) / jnp.maximum(wx_side, 1.0)
    gain_y = (ty_side - (ty0_side + STEP * push_y_side)) / jnp.maximum(wy_side, 1.0)

    def fresh_side(plane, depth, gain):
        return jnp.where(depth > level, UV[plane, BAND, :] + STEP * TEND[plane, ALL, :] + gain, 0.0)

    u_sw = fresh_side(U_SW, wx_sw, spread(gain_x, 0))[own]
    u_se = fresh_side(U_SE, wx_se, spread(gain_x, 64))[own]
    v_sw = fresh_side(V_SW, wy_sw, spread(gain_y, 0))
    v_se = fresh_side(V_SE, wy_se, spread(gain_y, 64))

    for k in range(LEVELS):
        fresh = jnp.where(lane32 < 12, lanes(u_sw, -(32 * k + 16)), jnp.where(lane32 >= 116, lanes(u_se, 112 - 32 * k), NU[k]))
        NU[k] = fresh
        result[k] = fresh
        fresh = jnp.where(lane < 12, lanes(v_sw, -(32 * k + 16)), jnp.where(lane >= 116, lanes(v_se, 112 - 32 * k), NV[k]))
        NV[k] = fresh
        result[4 + k] = fresh[own]

    ring_t, ring_s = RINGS[0, pl.ds(0, ROWS), :], RINGS[1, pl.ds(0, ROWS), :]

    def side_flux(cells, flow):
        flux = flow * upwind_value(flow, *x_parts(cells))
        return flux - lanes(flux, 1)

    XS[0] = side_flux(jnp.where(half32, RW[1, OWN, :], ring_t), u_sw)
    XS[1] = side_flux(jnp.where(half32, ring_t, lanes(RE[1, OWN, :], 16)), u_se)
    XS[2] = side_flux(jnp.where(half32, lanes(RW[1, OWN, :], -16), ring_s), u_sw)
    XS[3] = side_flux(jnp.where(half32, ring_s, RE[1, OWN, :]), u_se)

    for field in range(2):
        for k in range(LEVELS):
            p = 4 * field + k
            flow = NU[k]
            flux = flow * jnp.where(flow >= 0.0, XU[p], XD[p])
            div_x = flux - lanes(flux, 1)
            div_x = jnp.where(lane32 < 8, lanes(XS[2 * field], -(32 * k + 16)),
                              jnp.where(lane32 >= 120, lanes(XS[2 * field + 1], 112 - 32 * k), div_x))
            up = NV[k, pl.ds(8, ROWS), :]
            down = NV[k, pl.ds(7, ROWS), :]
            flux_up = up * jnp.where(up >= 0.0, YU[p, pl.ds(1, ROWS), :], YD[p, pl.ds(1, ROWS), :])
            flux_down = down * jnp.where(down >= 0.0, YU[p, pl.ds(0, ROWS), :], YD[p, pl.ds(0, ROWS), :])
            cells = TS[p, OWN, :]
            fresh = cells - STEP * (div_x + (flux_up - flux_down))
            result[8 + p] = jnp.where(wet[0] > k, fresh, 0.0)

    for d in range(8):
        if d in (SE, NW):
            @pl.when(earlier[d] | later[d])
            def _():
                for copy in copies(d):
                    copy.wait_send()
        else:
            for copy in copies(d):
                copy.wait_send()

    @pl.when(corner_hub)
    def _():
        hub_south.wait_send()

    @pl.when(corner_hub & west_relayed)
    def _():
        hub_west.wait_send()

    @pl.when(corner_b & west_relayed)
    def _():
        to_hub.wait_send()


def deal(result, u_out, v_out, t_out, s_out, e_out, sem):
    copies = [pltpu.make_async_copy(result.at[pl.ds(LEVELS * i, LEVELS)], out, sem.at[i])
              for i, out in enumerate((u_out, v_out, t_out, s_out))]
    copies.append(pltpu.make_async_copy(result.at[16], e_out, sem.at[4]))
    for copy in copies:
        copy.start()
    for copy in copies:
        copy.wait()


def solution(mesh):
    n_lat, n_lon = mesh.shape["lat"], mesh.shape["lon"]

    def step(u_vel, v_vel, temp, salt, eta, wet_levels):
        levels = jax.ShapeDtypeStruct((LEVELS, ROWS, COLS), F32)
        plane = jax.ShapeDtypeStruct((ROWS, COLS), F32)
        hbm = pl.BlockSpec(memory_space=pl.ANY)
        vmem = pl.BlockSpec(memory_space=pltpu.VMEM)

        def body(*refs):
            kernel(n_lat, n_lon, *refs)

        def buffer(*shape):
            return pltpu.VMEM(shape, F32)

        result = pl.pallas_call(
            body,
            out_shape=pltpu.VMEM((17, ROWS, COLS), F32),
            in_specs=[hbm] * 6,
            out_specs=vmem,
            scratch_shapes=[
                buffer(16, ROWS, COLS),
                buffer(ROWS, COLS),
                pltpu.VMEM((3, ROWS, COLS), jnp.int32),
                buffer(12, EXT, COLS),
                buffer(8, EXT, COLS),
                buffer(2, EXT, COLS),
                buffer(2, EXT, COLS),
                buffer(2, EXT, COLS),
                buffer(2, EXT, COLS),
                buffer(2, EXT, COLS),
                buffer(2, PAD, COLS),
                buffer(9, SPAN, COLS),
                buffer(5, EXT, COLS),
                buffer(12, SPAN, COLS),
                buffer(12, SPAN + 8, COLS),
                buffer(8, ROWS, COLS),
                buffer(8, ROWS, COLS),
                buffer(8, 40, COLS),
                buffer(8, 40, COLS),
                buffer(4, SPAN, COLS),
                buffer(4, ROWS, COLS),
                buffer(4, ROWS, COLS),
                pltpu.SemaphoreType.DMA((6,)),
                pltpu.SemaphoreType.REGULAR((8,)),
                pltpu.SemaphoreType.DMA((15,)),
                pltpu.SemaphoreType.DMA((15,)),
            ],
            compiler_params=pltpu.CompilerParams(collective_id=0, has_side_effects=True),
        )(u_vel, v_vel, temp, salt, eta, wet_levels)
        return pl.pallas_call(
            deal,
            out_shape=(levels, levels, levels, levels, plane),
            in_specs=[vmem],
            out_specs=(hbm,) * 5,
            scratch_shapes=[pltpu.SemaphoreType.DMA((5,))],
            compiler_params=pltpu.CompilerParams(vmem_limit_bytes=1 << 20),
        )(result)

    tile, flat = P(None, "lat", "lon"), P("lat", "lon")
    return jax.shard_map(
        step, mesh=mesh, in_specs=(tile, tile, tile, tile, flat, tile),
        out_specs=(tile, tile, tile, tile, flat), check_vma=False)
```

```python
import jax
import jax.numpy as jnp
from jax import lax
from jax.experimental import pallas as pl
from jax.experimental.pallas import tpu as pltpu
from jax.sharding import PartitionSpec as P

MESH = pl.DeviceIdType.MESH
F32 = jnp.float32
LEVELS = 4
SUB = 8
BLOCK = 8
RELAYED_FROM = 2
STEP = 0.4
WAVE = 0.45 / 4
EPS = 1e-6 * 12.0 / 13.0
ROWS = 32
COLS = 128
PAD = 16
EXT = ROWS + 2 * PAD
LO = 8
SPAN = 48

U_MAIN, V_MAIN, U_SW, U_SE, V_SW, V_SE = 0, 4, 8, 9, 10, 11


def lanes(x, shift):
    shift = shift % COLS
    return x if shift == 0 else pltpu.roll(x, shift, 1)


def rows(x, shift):
    return pltpu.roll(x, shift % x.shape[0], 0)


def correction(d0, d1, d2, d3):
    x0 = d1 - d0
    x1 = d2 - d1
    x2 = d3 - d2
    m1 = d1 + d1
    m2 = d2 + d2
    y0 = x0 + m1
    y1 = d1 + d2
    y2 = x2 - m2
    e0 = x0 * x0 + (y0 * y0) * (3.0 / 13.0) + EPS
    e1 = x1 * x1 + (y1 * y1) * (3.0 / 13.0) + EPS
    e2 = x2 * x2 + (y2 * y2) * (3.0 / 13.0) + EPS
    a0 = e1 * e2
    a1 = e0 * e2
    a2 = e0 * e1
    w0 = a0 * a0
    w1 = (a1 * a1) * 6.0
    w2 = (a2 * a2) * 3.0
    top = w0 * (5.0 * d1 - 2.0 * d0) + w1 * (d1 + m2) + w2 * (4.0 * d2 - d3)
    return top / ((w0 + w1 + w2) * 6.0)


def upwind_value(flow, q0, q1, gm2, gm1, g0, g1, g2):
    ahead = flow >= 0.0
    fix = correction(jnp.where(ahead, gm2, g2), jnp.where(ahead, gm1, g1), g0, jnp.where(ahead, g1, gm1))
    return jnp.where(ahead, q0 + fix, q1 - fix)


def x_parts(q):
    q1 = lanes(q, -1)
    g = q1 - q
    return q, q1, lanes(g, 2), lanes(g, 1), g, lanes(g, -1), lanes(g, -2)


def y_parts(ref, k, r0, n):
    q = [ref[k, pl.ds(r0 + s, n), :] for s in range(-2, 4)]
    g = [q[i + 1] - q[i] for i in range(5)]
    return q[2], q[3], g[0], g[1], g[2], g[3], g[4]


def ring(parts):
    lane = lax.broadcasted_iota(jnp.int32, parts[0].shape, 1)
    out = lanes(parts[0], 16)
    for k in range(1, LEVELS):
        out = jnp.where(lane >= 32 * k, lanes(parts[k], 32 * k + 16), out)
    return out


def level_sum(x):
    y = x + lanes(x, 64)
    return y + lanes(y, 32)


def spread(x, start):
    lane = lax.broadcasted_iota(jnp.int32, x.shape, 1)
    return level_sum(jnp.where((lane >= start) & (lane < start + 32), x, 0.0))


DIRS = ((1, 0), (-1, 0), (0, 1), (0, -1), (1, 1), (-1, 1), (1, -1), (-1, -1))
NORTH, SOUTH, EAST, WEST, NE, SE, NW, SW = range(8)


def kernel(n_lat, n_lon, u_hbm, v_hbm, t_hbm, s_hbm, e_hbm, w_hbm,
           result,
           raw, raw2, wet, UV, TS, WE, PE, PW, RW, RE, HUB, KEPT, RINGS,
           TEND, FY, XU, XD, YU, YD, NV, NU, XS,
           in_sem, ready, send_sem, recv_sem):
    loads = [
        pltpu.make_async_copy(w_hbm, wet, in_sem.at[0]),
        pltpu.make_async_copy(u_hbm, raw.at[pl.ds(0, 4)], in_sem.at[1]),
        pltpu.make_async_copy(v_hbm, raw.at[pl.ds(4, 4)], in_sem.at[2]),
        pltpu.make_async_copy(t_hbm, raw.at[pl.ds(8, 4)], in_sem.at[3]),
        pltpu.make_async_copy(s_hbm, raw.at[pl.ds(12, 4)], in_sem.at[4]),
        pltpu.make_async_copy(e_hbm, raw2, in_sem.at[5]),
    ]
    for load in loads:
        load.start()

    lat = lax.axis_index("lat")
    lon = lax.axis_index("lon")

    def start_rank(i, j):
        group = j // BLOCK
        group = jnp.where(group == 2, 3, jnp.where(group == 3, 2, group))
        rank = (group * BLOCK + lax.rem(i, BLOCK)) * (n_lat * n_lon) + i * n_lon + j
        return jnp.where((i == 0) & (j == 0), 2 * BLOCK * n_lat * n_lon - 1, rank)

    peers = [(lax.rem(lat + n_lat + di, n_lat), lax.rem(lon + n_lon + dj, n_lon)) for di, dj in DIRS]
    here = start_rank(lat, lon)
    earlier = [start_rank(*peer) < here for peer in peers]
    first_row, last_row = lax.rem(lat, BLOCK) == 0, lax.rem(lat, BLOCK) == BLOCK - 1
    first_column, last_column = lax.rem(lon, BLOCK) == 0, lax.rem(lon, BLOCK) == BLOCK - 1
    inner_west, inner_east = jnp.logical_not(first_column), jnp.logical_not(last_column)
    relayed = lon // BLOCK >= RELAYED_FROM
    west_relayed = peers[WEST][1] // BLOCK >= RELAYED_FROM
    corner_a, corner_b, corner_hub = first_row & last_column, last_row & first_column, first_row & first_column
    later = [jnp.logical_not(flag) for flag in earlier]
    earlier[SE] = earlier[SE] & jnp.logical_not(corner_a)
    later[SE] = later[SE] & jnp.logical_not(corner_a)
    earlier[NW] = (earlier[NW] & jnp.logical_not(corner_b)) | (corner_b & jnp.logical_not(west_relayed))
    later[NW] = later[NW] & jnp.logical_not(corner_b)

    barrier = pltpu.get_barrier_semaphore()
    expected = 0
    for d in range(8):
        expected = expected + jnp.where(earlier[d], 1, 0)

        @pl.when(later[d])
        def _():
            pl.semaphore_signal(barrier, inc=1, device_id=peers[d], device_id_type=MESH)

    @pl.when(corner_a & jnp.logical_not(relayed))
    def _():
        pl.semaphore_signal(barrier, inc=1, device_id=peers[SE], device_id_type=MESH)

    for load in loads:
        load.wait()

    OWN = pl.ds(PAD, ROWS)

    def wetted(first, face):
        return [jnp.where(wet[face] > k, raw[first + k], 0.0) for k in range(LEVELS)]

    lane32 = lax.broadcasted_iota(jnp.int32, (ROWS, COLS), 1)
    half32 = lax.rem(lane32, 32) < 16
    ring_u, ring_v, ring_t, ring_s = ring(wetted(0, 1)), ring(wetted(4, 2)), ring(wetted(8, 0)), ring(wetted(12, 0))
    eta8 = lanes(raw2[...], 8)
    wet8 = lanes(ring([wet[0].astype(F32)] * LEVELS), 8)
    spot = lax.rem(lane32, 32)
    PE[0, OWN, :] = jnp.where(half32, ring_u, lanes(ring_v, 16))
    PW[0, OWN, :] = jnp.where(half32, lanes(ring_u, -16), ring_v)
    PE[1, OWN, :] = jnp.where(lane32 < 8, eta8, jnp.where(
        (spot >= 16) & (spot < 24), wet8, jnp.where(half32, ring_t, lanes(ring_s, 16))))
    PW[1, OWN, :] = jnp.where((lane32 >= 8) & (lane32 < 16), eta8, jnp.where(
        spot >= 24, wet8, jnp.where(half32, lanes(ring_t, -16), ring_s)))

    RINGS[0, pl.ds(0, ROWS), :] = ring_t
    RINGS[1, pl.ds(0, ROWS), :] = ring_s
    top, bottom = pl.ds(32, 16), pl.ds(16, 16)
    under, over = pl.ds(0, 16), pl.ds(48, 16)
    every = pl.ds(0, 8)
    parcels = {
        NORTH: [(UV.at[every, pl.ds(36, 12), :], UV.at[every, pl.ds(4, 12), :]),
                (WE.at[:, pl.ds(40, 8), :], WE.at[:, pl.ds(8, 8), :]),
                (TS.at[:, pl.ds(45, 3), :], TS.at[:, pl.ds(13, 3), :])],
        SOUTH: [(UV.at[every, pl.ds(16, 12), :], UV.at[every, pl.ds(48, 12), :]),
                (WE.at[:, pl.ds(16, 8), :], WE.at[:, pl.ds(48, 8), :]),
                (TS.at[:, pl.ds(16, 3), :], TS.at[:, pl.ds(48, 3), :])],
        EAST: [(PE.at[:, OWN, :], RW.at[:, OWN, :])],
        WEST: [(PW.at[:, OWN, :], RE.at[:, OWN, :])],
        NE: [(PE.at[:, pl.ds(36, 12), :], RW.at[:, pl.ds(4, 12), :])],
        SE: [(PE.at[:, pl.ds(16, 12), :], RW.at[:, pl.ds(48, 12), :])],
        NW: [(PW.at[:, pl.ds(36, 12), :], RE.at[:, pl.ds(4, 12), :])],
        SW: [(PW.at[:, pl.ds(16, 12), :], RE.at[:, pl.ds(48, 12), :])],
    }
    first_slot, slots = {}, 0
    for d in range(8):
        first_slot[d] = slots
        slots += len(parcels[d])

    def copies(d):
        return [
            pltpu.make_async_remote_copy(
                src_ref=src, dst_ref=dst, send_sem=send_sem.at[first_slot[d] + i], recv_sem=recv_sem.at[first_slot[d] + i],
                device_id=peers[d], device_id_type=MESH)
            for i, (src, dst) in enumerate(parcels[d])]

    def send_to_earlier(d, also=True):
        @pl.when(earlier[d] & also)
        def _():
            for copy in copies(d):
                copy.start()

    def send_to_later(d, also=True):
        @pl.when(later[d] & also)
        def _():
            pl.semaphore_wait(ready.at[d], 1)
            for copy in copies(d):
                copy.start()

    def wait_from(d):
        for copy in copies(d):
            copy.wait_recv()

    def extra(slot, src, dst, arrival, peer):
        return pltpu.make_async_remote_copy(
            src_ref=src, dst_ref=dst, send_sem=send_sem.at[slot], recv_sem=recv_sem.at[arrival],
            device_id=peer, device_id_type=MESH)

    to_hub = extra(slots, PW.at[:, pl.ds(36, 12), :], HUB.at[:, pl.ds(4, 12), :], slots, peers[NORTH])
    hub_west = extra(slots + 1, HUB.at[:, pl.ds(4, 12), :], RE.at[:, pl.ds(4, 12), :], first_slot[NW], peers[WEST])
    hub_south = extra(slots + 2, RW.at[:, pl.ds(16, 12), :], RW.at[:, pl.ds(48, 12), :], first_slot[SE], peers[SOUTH])

    @pl.when(expected > 0)
    def _():
        pl.semaphore_wait(barrier, expected)

    for d in range(8):
        @pl.when(earlier[d] & jnp.logical_not(corner_b) if d == NW else earlier[d])
        def _():
            pl.semaphore_signal(ready.at[DIRS.index((-DIRS[d][0], -DIRS[d][1]))], inc=1, device_id=peers[d], device_id_type=MESH)

    send_to_earlier(NW, corner_b)
    for d in (EAST, NE, SE, WEST, SW):
        send_to_earlier(d)
    send_to_earlier(NW, jnp.logical_not(corner_b))

    for first, face, planes in ((0, 1, UV), (4, 2, UV), (8, 0, TS), (12, 0, TS)):
        for k, plane in enumerate(wetted(first, face)):
            planes[first % 8 + k, OWN, :] = plane
    WE[0, OWN, :] = wet[0].astype(F32)
    WE[1, OWN, :] = raw2[...]

    for d in (NORTH, SOUTH):
        send_to_earlier(d)

    @pl.when(corner_b & west_relayed & earlier[NORTH])
    def _():
        to_hub.start()

    def flux_x(q_plane, u_plane, r0, n):
        flow = UV[u_plane, pl.ds(r0, n), :]
        flux = flow * upwind_value(flow, *x_parts(UV[q_plane, pl.ds(r0, n), :]))
        return flux - lanes(flux, 1)

    def flux_y(q_plane, v_plane, r0):
        flow = UV[v_plane, pl.ds(r0, 8), :]
        return flow * upwind_value(flow, *y_parts(UV, q_plane, r0, 8))

    def put_x(q_plane, u_plane, r0, n):
        TEND[q_plane, pl.ds(r0 - LO, n), :] = flux_x(q_plane, u_plane, r0, n)

    def put_y(q_plane, v_plane, r0):
        FY[q_plane, pl.ds(r0 - LO + 1, 8), :] = flux_y(q_plane, v_plane, r0)

    def combine(q_plane):
        for r0 in range(0, SPAN, 16):
            TEND[q_plane, pl.ds(r0, 16), :] = -(TEND[q_plane, pl.ds(r0, 16), :] + (
                FY[q_plane, pl.ds(r0 + 1, 16), :] - FY[q_plane, pl.ds(r0, 16), :]))

    def tracer_x(k, r0, n):
        q0, q1, gm2, gm1, g0, g1, g2 = x_parts(TS[k, pl.ds(PAD + r0, n), :])
        XU[k, pl.ds(r0, n), :] = q0 + correction(gm2, gm1, g0, g1)
        XD[k, pl.ds(r0, n), :] = q1 - correction(g2, g1, g0, gm1)

    def tracer_y(k, r0):
        q0, q1, gm2, gm1, g0, g1, g2 = y_parts(TS, k, PAD - 1 + r0, 8)
        YU[k, pl.ds(r0, 8), :] = q0 + correction(gm2, gm1, g0, g1)
        YD[k, pl.ds(r0, 8), :] = q1 - correction(g2, g1, g0, gm1)

    def local_part(k, carry):
        plane = lax.rem(k, LEVELS)
        for r0 in (16, 32):
            put_x(k, plane, r0, 16)
        for r0 in (23, 31):
            put_y(k, V_MAIN + plane, r0)
        for r0 in (0, 16):
            tracer_x(k, r0, 16)
        for r0 in (8, 16):
            tracer_y(k, r0)
        return carry

    lax.fori_loop(0, 8, local_part, 0)

    send_to_later(NORTH)

    @pl.when(corner_b & west_relayed & later[NORTH])
    def _():
        to_hub.start()

    send_to_later(EAST, inner_east)
    send_to_later(NE, inner_east)
    send_to_later(WEST, inner_west)
    send_to_later(NW, inner_west)
    send_to_later(SOUTH)
    send_to_later(SE, inner_east)
    send_to_later(SW, inner_west)
    for d in (EAST, NE, SE):
        send_to_later(d, last_column)

    for d in (NORTH, SOUTH):
        wait_from(d)

    zero16 = jnp.zeros((16, COLS), F32)

    @pl.when(lat == 0)
    def _():
        for k in range(8):
            UV[k, under, :] = zero16
            TS[k, under, :] = zero16
        WE[0, under, :] = zero16
        WE[1, under, :] = zero16

    @pl.when(lat == n_lat - 1)
    def _():
        for k in range(8):
            UV[k, over, :] = zero16
            TS[k, over, :] = zero16
        WE[0, over, :] = zero16
        WE[1, over, :] = zero16

    def edge_part(k, carry):
        plane = lax.rem(k, LEVELS)
        for r0 in (8, 48):
            put_x(k, plane, r0, 8)
        for r0 in (7, 15, 39, 47):
            put_y(k, V_MAIN + plane, r0)
        combine(k)
        for r0 in (0, 24, 32):
            tracer_y(k, r0)
        return carry

    lax.fori_loop(0, 8, edge_part, 0)

    lane64 = lax.broadcasted_iota(jnp.int32, (EXT, COLS), 1)
    half = lax.rem(lane64, 32) < 16
    lane = lax.broadcasted_iota(jnp.int32, (SPAN, COLS), 1)
    level = (lane // 32).astype(F32)
    BAND = pl.ds(LO, SPAN)
    LOWER = pl.ds(LO - 1, SPAN)
    ALL = pl.ds(0, SPAN)
    scale = STEP / SUB
    own = slice(PAD - LO, PAD - LO + ROWS)

    def band(x):
        return x[LO:LO + SPAN]

    def laid(main):
        return jnp.where(lane < 48, lanes(main, 16), lanes(main, -48))

    def faces(w):
        at = band(w)
        return jnp.minimum(at, lanes(at, -1)), jnp.minimum(at, band(rows(w, -1)))

    def main_sum(ref, first, where_rows, limit=None):
        total = None
        for k in range(LEVELS):
            term = ref[first + k, where_rows, :]
            if limit is not None:
                term = jnp.where(limit > k, term, 0.0)
            total = term if total is None else total + term
        return total

    def pair_sum(sw, se):
        low = lane < 64
        folded = jnp.where(low, sw, se) + lanes(jnp.where(low, se, sw), 64)
        return folded + lanes(folded, -32)

    def substeps(height, tx, ty, tym, fx, fy, cx, cy):
        for n in range(SUB):
            below = tym if n == 0 else rows(ty, 1)
            height = height - (tx - lanes(tx, 1) + (ty - below))
            tx = (tx + fx) - cx * (lanes(height, -1) - height)
            ty = (ty + fy) - cy * (rows(height, -1) - height)
        return height, tx, ty

    wx_main, wy_main = faces(WE[0])
    push_x = main_sum(TEND, U_MAIN, ALL, wx_main)
    push_y = main_sum(TEND, V_MAIN, ALL, wy_main)
    tx0 = main_sum(UV, U_MAIN, BAND)
    ty0 = main_sum(UV, V_MAIN, BAND)
    tym_main = main_sum(UV, V_MAIN, LOWER)
    h_main, tx_main, ty_main = substeps(
        WE[1, BAND, :], tx0, ty0, tym_main, scale * push_x, scale * push_y, WAVE * wx_main, WAVE * wy_main)
    gain_x = (tx_main - (tx0 + STEP * push_x)) / jnp.maximum(wx_main, 1.0)
    gain_y = (ty_main - (ty0 + STEP * push_y)) / jnp.maximum(wy_main, 1.0)
    for k in range(LEVELS):
        NU[k] = jnp.where(wx_main > k, UV[U_MAIN + k, BAND, :] + STEP * TEND[U_MAIN + k, ALL, :] + gain_x, 0.0)[own]
        NV[k] = jnp.where(wy_main > k, UV[V_MAIN + k, BAND, :] + STEP * TEND[V_MAIN + k, ALL, :] + gain_y, 0.0)
    KEPT[0] = h_main
    for slot, plane in enumerate((tx0, ty0, tym_main, push_x, push_y, wx_main, wy_main, WE[1, BAND, :])):
        KEPT[slot + 1] = laid(plane)
    RINGS[2] = ring([UV[U_MAIN + k] for k in range(LEVELS)])
    RINGS[3] = ring([UV[V_MAIN + k] for k in range(LEVELS)])
    RINGS[4] = ring([WE[0]] * LEVELS)

    def clear_poles(ref):
        @pl.when(lat == 0)
        def _():
            for i in range(2):
                ref[i, under, :] = zero16

        @pl.when(lat == n_lat - 1)
        def _():
            for i in range(2):
                ref[i, over, :] = zero16

    def strip(u_plane, v_plane):
        def one(i, carry):
            q_plane = u_plane + i * (v_plane - u_plane)
            for r0 in (8, 24, 40):
                put_x(q_plane, u_plane, r0, 16)
            for r0 in (7, 15, 23, 31, 39, 47):
                put_y(q_plane, v_plane, r0)
            combine(q_plane)
            return carry

        lax.fori_loop(0, 2, one, 0)

    def western_strip():
        for d in (NE, SE):
            wait_from(d)
        clear_poles(RW)
        UV[U_SW] = jnp.where(half, RW[0], RINGS[2])
        UV[V_SW] = jnp.where(half, lanes(RW[0], -16), RINGS[3])
        strip(U_SW, V_SW)

    def eastern_strip():
        for d in (WEST, NW, SW):
            wait_from(d)
        clear_poles(RE)
        UV[U_SE] = jnp.where(half, RINGS[2], lanes(RE[0], 16))
        UV[V_SE] = jnp.where(half, RINGS[3], RE[0])
        strip(U_SE, V_SE)

    @pl.when(first_column)
    def _():
        eastern_strip()

    for d in (WEST, NW, SW):
        send_to_later(d, first_column)

    @pl.when(corner_hub & west_relayed)
    def _():
        to_hub.wait_recv()
        hub_west.start()

    wait_from(EAST)

    @pl.when(corner_hub)
    def _():
        hub_south.start()

    western_strip()

    @pl.when(inner_west)
    def _():
        eastern_strip()

    in_sw, in_se = lane < 24, (lane >= 72) & (lane < 96)

    def kept(slot, sides):
        return jnp.where(in_sw | in_se, sides, KEPT[slot])

    wx_sw, wy_sw = faces(jnp.where(half, lanes(RW[1], -8), RINGS[4]))
    wx_se, wy_se = faces(jnp.where(half, RINGS[4], lanes(RE[1], -8)))
    wx_side = kept(6, jnp.where(lane < 64, wx_sw, wx_se))
    wy_side = kept(7, jnp.where(lane < 64, wy_sw, wy_se))
    eta_side = jnp.where(lane < 16, lanes(RW[1, BAND, :], 8), jnp.where(
        (lane >= 80) & (lane < 88), lanes(RE[1, BAND, :], 72), KEPT[8]))

    def masked(plane, limit):
        return jnp.where(limit > level, TEND[plane, ALL, :], 0.0)

    push_x_side = kept(4, pair_sum(masked(U_SW, wx_sw), masked(U_SE, wx_se)))
    push_y_side = kept(5, pair_sum(masked(V_SW, wy_sw), masked(V_SE, wy_se)))
    tx0_side = kept(1, pair_sum(UV[U_SW, BAND, :], UV[U_SE, BAND, :]))
    ty0_side = kept(2, pair_sum(UV[V_SW, BAND, :], UV[V_SE, BAND, :]))
    tym_side = kept(3, pair_sum(UV[V_SW, LOWER, :], UV[V_SE, LOWER, :]))

    h_side, tx_side, ty_side = substeps(
        eta_side, tx0_side, ty0_side, tym_side, scale * push_x_side, scale * push_y_side, WAVE * wx_side, WAVE * wy_side)

    result[16] = jnp.where(lane < 16, lanes(h_side, -16), jnp.where(lane >= 112, lanes(h_side, 48), KEPT[0]))[own]

    gain_x = (tx_side - (tx0_side + STEP * push_x_side)) / jnp.maximum(wx_side, 1.0)
    gain_y = (ty_side - (ty0_side + STEP * push_y_side)) / jnp.maximum(wy_side, 1.0)

    def fresh_side(plane, depth, gain):
        return jnp.where(depth > level, UV[plane, BAND, :] + STEP * TEND[plane, ALL, :] + gain, 0.0)

    u_sw = fresh_side(U_SW, wx_sw, spread(gain_x, 0))[own]
    u_se = fresh_side(U_SE, wx_se, spread(gain_x, 64))[own]
    v_sw = fresh_side(V_SW, wy_sw, spread(gain_y, 0))
    v_se = fresh_side(V_SE, wy_se, spread(gain_y, 64))

    for k in range(LEVELS):
        fresh = jnp.where(lane32 < 12, lanes(u_sw, -(32 * k + 16)), jnp.where(lane32 >= 116, lanes(u_se, 112 - 32 * k), NU[k]))
        NU[k] = fresh
        result[k] = fresh
        fresh = jnp.where(lane < 12, lanes(v_sw, -(32 * k + 16)), jnp.where(lane >= 116, lanes(v_se, 112 - 32 * k), NV[k]))
        NV[k] = fresh
        result[4 + k] = fresh[own]

    ring_t, ring_s = RINGS[0, pl.ds(0, ROWS), :], RINGS[1, pl.ds(0, ROWS), :]

    def side_flux(cells, flow):
        flux = flow * upwind_value(flow, *x_parts(cells))
        return flux - lanes(flux, 1)

    XS[0] = side_flux(jnp.where(half32, RW[1, OWN, :], ring_t), u_sw)
    XS[1] = side_flux(jnp.where(half32, ring_t, lanes(RE[1, OWN, :], 16)), u_se)
    XS[2] = side_flux(jnp.where(half32, lanes(RW[1, OWN, :], -16), ring_s), u_sw)
    XS[3] = side_flux(jnp.where(half32, ring_s, RE[1, OWN, :]), u_se)

    for field in range(2):
        for k in range(LEVELS):
            p = 4 * field + k
            flow = NU[k]
            flux = flow * jnp.where(flow >= 0.0, XU[p], XD[p])
            div_x = flux - lanes(flux, 1)
            div_x = jnp.where(lane32 < 8, lanes(XS[2 * field], -(32 * k + 16)),
                              jnp.where(lane32 >= 120, lanes(XS[2 * field + 1], 112 - 32 * k), div_x))
            up = NV[k, pl.ds(8, ROWS), :]
            down = NV[k, pl.ds(7, ROWS), :]
            flux_up = up * jnp.where(up >= 0.0, YU[p, pl.ds(1, ROWS), :], YD[p, pl.ds(1, ROWS), :])
            flux_down = down * jnp.where(down >= 0.0, YU[p, pl.ds(0, ROWS), :], YD[p, pl.ds(0, ROWS), :])
            cells = TS[p, OWN, :]
            fresh = cells - STEP * (div_x + (flux_up - flux_down))
            result[8 + p] = jnp.where(wet[0] > k, fresh, 0.0)

    for d in range(8):
        if d in (SE, NW):
            @pl.when(earlier[d] | later[d])
            def _():
                for copy in copies(d):
                    copy.wait_send()
        else:
            for copy in copies(d):
                copy.wait_send()

    @pl.when(corner_hub)
    def _():
        hub_south.wait_send()

    @pl.when(corner_hub & west_relayed)
    def _():
        hub_west.wait_send()

    @pl.when(corner_b & west_relayed)
    def _():
        to_hub.wait_send()


def deal(result, u_out, v_out, t_out, s_out, e_out, sem):
    copies = [pltpu.make_async_copy(result.at[pl.ds(LEVELS * i, LEVELS)], out, sem.at[i])
              for i, out in enumerate((u_out, v_out, t_out, s_out))]
    copies.append(pltpu.make_async_copy(result.at[16], e_out, sem.at[4]))
    for copy in copies:
        copy.start()
    for copy in copies:
        copy.wait()


def solution(mesh):
    n_lat, n_lon = mesh.shape["lat"], mesh.shape["lon"]

    def step(u_vel, v_vel, temp, salt, eta, wet_levels):
        levels = jax.ShapeDtypeStruct((LEVELS, ROWS, COLS), F32)
        plane = jax.ShapeDtypeStruct((ROWS, COLS), F32)
        hbm = pl.BlockSpec(memory_space=pl.ANY)
        vmem = pl.BlockSpec(memory_space=pltpu.VMEM)

        def body(*refs):
            kernel(n_lat, n_lon, *refs)

        def buffer(*shape):
            return pltpu.VMEM(shape, F32)

        result = pl.pallas_call(
            body,
            out_shape=pltpu.VMEM((17, ROWS, COLS), F32),
            in_specs=[hbm] * 6,
            out_specs=vmem,
            scratch_shapes=[
                buffer(16, ROWS, COLS),
                buffer(ROWS, COLS),
                pltpu.VMEM((3, ROWS, COLS), jnp.int32),
                buffer(12, EXT, COLS),
                buffer(8, EXT, COLS),
                buffer(2, EXT, COLS),
                buffer(2, EXT, COLS),
                buffer(2, EXT, COLS),
                buffer(2, EXT, COLS),
                buffer(2, EXT, COLS),
                buffer(2, PAD, COLS),
                buffer(9, SPAN, COLS),
                buffer(5, EXT, COLS),
                buffer(12, SPAN, COLS),
                buffer(12, SPAN + 8, COLS),
                buffer(8, ROWS, COLS),
                buffer(8, ROWS, COLS),
                buffer(8, 40, COLS),
                buffer(8, 40, COLS),
                buffer(4, SPAN, COLS),
                buffer(4, ROWS, COLS),
                buffer(4, ROWS, COLS),
                pltpu.SemaphoreType.DMA((6,)),
                pltpu.SemaphoreType.REGULAR((8,)),
                pltpu.SemaphoreType.DMA((15,)),
                pltpu.SemaphoreType.DMA((15,)),
            ],
            compiler_params=pltpu.CompilerParams(collective_id=0, has_side_effects=True),
        )(u_vel, v_vel, temp, salt, eta, wet_levels)
        return pl.pallas_call(
            deal,
            out_shape=(levels, levels, levels, levels, plane),
            in_specs=[vmem],
            out_specs=(hbm,) * 5,
            scratch_shapes=[pltpu.SemaphoreType.DMA((5,))],
            compiler_params=pltpu.CompilerParams(vmem_limit_bytes=1 << 20),
        )(result)

    tile, flat = P(None, "lat", "lon"), P("lat", "lon")
    return jax.shard_map(
        step, mesh=mesh, in_specs=(tile, tile, tile, tile, flat, tile),
        out_specs=(tile, tile, tile, tile, flat), check_vma=False)
```

```python
import jax
import jax.numpy as jnp
from jax import lax
from jax.experimental import pallas as pl
from jax.experimental.pallas import tpu as pltpu
from jax.sharding import PartitionSpec as P

MESH = pl.DeviceIdType.MESH
F32 = jnp.float32
LEVELS = 4
SUB = 8
BLOCK = 8
RELAYED_FROM = 2
STEP = 0.4
WAVE = 0.45 / 4
EPS = 1e-6 * 12.0 / 13.0
ROWS = 32
COLS = 128
PAD = 16
EXT = ROWS + 2 * PAD
LO = 8
SPAN = 48

U_MAIN, V_MAIN, U_SW, U_SE, V_SW, V_SE = 0, 4, 8, 9, 10, 11


def lanes(x, shift):
    shift = shift % COLS
    return x if shift == 0 else pltpu.roll(x, shift, 1)


def rows(x, shift):
    return pltpu.roll(x, shift % x.shape[0], 0)


def correction(d0, d1, d2, d3):
    x0 = d1 - d0
    x1 = d2 - d1
    x2 = d3 - d2
    m1 = d1 + d1
    m2 = d2 + d2
    y0 = x0 + m1
    y1 = d1 + d2
    y2 = x2 - m2
    e0 = x0 * x0 + (y0 * y0) * (3.0 / 13.0) + EPS
    e1 = x1 * x1 + (y1 * y1) * (3.0 / 13.0) + EPS
    e2 = x2 * x2 + (y2 * y2) * (3.0 / 13.0) + EPS
    a0 = e1 * e2
    a1 = e0 * e2
    a2 = e0 * e1
    w0 = a0 * a0
    w1 = (a1 * a1) * 6.0
    w2 = (a2 * a2) * 3.0
    top = w0 * (5.0 * d1 - 2.0 * d0) + w1 * (d1 + m2) + w2 * (4.0 * d2 - d3)
    return top / ((w0 + w1 + w2) * 6.0)


def upwind_value(flow, q0, q1, gm2, gm1, g0, g1, g2):
    ahead = flow >= 0.0
    fix = correction(jnp.where(ahead, gm2, g2), jnp.where(ahead, gm1, g1), g0, jnp.where(ahead, g1, gm1))
    return jnp.where(ahead, q0 + fix, q1 - fix)


def x_parts(q):
    q1 = lanes(q, -1)
    g = q1 - q
    return q, q1, lanes(g, 2), lanes(g, 1), g, lanes(g, -1), lanes(g, -2)


def y_parts(ref, k, r0, n):
    q = [ref[k, pl.ds(r0 + s, n), :] for s in range(-2, 4)]
    g = [q[i + 1] - q[i] for i in range(5)]
    return q[2], q[3], g[0], g[1], g[2], g[3], g[4]


def ring(parts):
    lane = lax.broadcasted_iota(jnp.int32, parts[0].shape, 1)
    out = lanes(parts[0], 16)
    for k in range(1, LEVELS):
        out = jnp.where(lane >= 32 * k, lanes(parts[k], 32 * k + 16), out)
    return out


def level_sum(x):
    y = x + lanes(x, 64)
    return y + lanes(y, 32)


def spread(x, start):
    lane = lax.broadcasted_iota(jnp.int32, x.shape, 1)
    return level_sum(jnp.where((lane >= start) & (lane < start + 32), x, 0.0))


DIRS = ((1, 0), (-1, 0), (0, 1), (0, -1), (1, 1), (-1, 1), (1, -1), (-1, -1))
NORTH, SOUTH, EAST, WEST, NE, SE, NW, SW = range(8)


def kernel(n_lat, n_lon, u_hbm, v_hbm, t_hbm, s_hbm, e_hbm, w_hbm,
           result,
           raw, raw2, wet, UV, TS, WE, PE, PW, RW, RE, HUB, KEPT, RINGS,
           TEND, FY, XU, XD, YU, YD, NV, NU, XS,
           in_sem, ready, send_sem, recv_sem):
    loads = [
        pltpu.make_async_copy(w_hbm, wet, in_sem.at[0]),
        pltpu.make_async_copy(u_hbm, raw.at[pl.ds(0, 4)], in_sem.at[1]),
        pltpu.make_async_copy(v_hbm, raw.at[pl.ds(4, 4)], in_sem.at[2]),
        pltpu.make_async_copy(t_hbm, raw.at[pl.ds(8, 4)], in_sem.at[3]),
        pltpu.make_async_copy(s_hbm, raw.at[pl.ds(12, 4)], in_sem.at[4]),
        pltpu.make_async_copy(e_hbm, raw2, in_sem.at[5]),
    ]
    for load in loads:
        load.start()

    lat = lax.axis_index("lat")
    lon = lax.axis_index("lon")

    def start_rank(i, j):
        group = j // BLOCK
        group = jnp.where(group == 2, 3, jnp.where(group == 3, 2, group))
        rank = (group * BLOCK + lax.rem(i, BLOCK)) * (n_lat * n_lon) + i * n_lon + j
        return jnp.where((i == 0) & (j == 0), 2 * BLOCK * n_lat * n_lon - 1, rank)

    peers = [(lax.rem(lat + n_lat + di, n_lat), lax.rem(lon + n_lon + dj, n_lon)) for di, dj in DIRS]
    here = start_rank(lat, lon)
    earlier = [start_rank(*peer) < here for peer in peers]
    first_row, last_row = lax.rem(lat, BLOCK) == 0, lax.rem(lat, BLOCK) == BLOCK - 1
    first_column, last_column = lax.rem(lon, BLOCK) == 0, lax.rem(lon, BLOCK) == BLOCK - 1
    inner_west, inner_east = jnp.logical_not(first_column), jnp.logical_not(last_column)
    relayed = lon // BLOCK >= RELAYED_FROM
    west_relayed = peers[WEST][1] // BLOCK >= RELAYED_FROM
    corner_a, corner_b, corner_hub = first_row & last_column, last_row & first_column, first_row & first_column
    later = [jnp.logical_not(flag) for flag in earlier]
    earlier[SE] = earlier[SE] & jnp.logical_not(corner_a)
    later[SE] = later[SE] & jnp.logical_not(corner_a)
    earlier[NW] = (earlier[NW] & jnp.logical_not(corner_b)) | (corner_b & jnp.logical_not(west_relayed))
    later[NW] = later[NW] & jnp.logical_not(corner_b)

    barrier = pltpu.get_barrier_semaphore()
    expected = 0
    for d in range(8):
        expected = expected + jnp.where(earlier[d], 1, 0)

        @pl.when(later[d])
        def _():
            pl.semaphore_signal(barrier, inc=1, device_id=peers[d], device_id_type=MESH)

    @pl.when(corner_a & jnp.logical_not(relayed))
    def _():
        pl.semaphore_signal(barrier, inc=1, device_id=peers[SE], device_id_type=MESH)

    for load in loads:
        load.wait()

    OWN = pl.ds(PAD, ROWS)

    def wetted(first, face):
        return [jnp.where(wet[face] > k, raw[first + k], 0.0) for k in range(LEVELS)]

    lane32 = lax.broadcasted_iota(jnp.int32, (ROWS, COLS), 1)
    half32 = lax.rem(lane32, 32) < 16
    ring_u, ring_v, ring_t, ring_s = ring(wetted(0, 1)), ring(wetted(4, 2)), ring(wetted(8, 0)), ring(wetted(12, 0))
    eta8 = lanes(raw2[...], 8)
    wet8 = lanes(ring([wet[0].astype(F32)] * LEVELS), 8)
    spot = lax.rem(lane32, 32)
    PE[0, OWN, :] = jnp.where(half32, ring_u, lanes(ring_v, 16))
    PW[0, OWN, :] = jnp.where(half32, lanes(ring_u, -16), ring_v)
    PE[1, OWN, :] = jnp.where(lane32 < 8, eta8, jnp.where(
        (spot >= 16) & (spot < 24), wet8, jnp.where(half32, ring_t, lanes(ring_s, 16))))
    PW[1, OWN, :] = jnp.where((lane32 >= 8) & (lane32 < 16), eta8, jnp.where(
        spot >= 24, wet8, jnp.where(half32, lanes(ring_t, -16), ring_s)))

    RINGS[0, pl.ds(0, ROWS), :] = ring_t
    RINGS[1, pl.ds(0, ROWS), :] = ring_s
    top, bottom = pl.ds(32, 16), pl.ds(16, 16)
    under, over = pl.ds(0, 16), pl.ds(48, 16)
    every = pl.ds(0, 8)
    parcels = {
        NORTH: [(UV.at[every, pl.ds(36, 12), :], UV.at[every, pl.ds(4, 12), :]),
                (WE.at[:, pl.ds(40, 8), :], WE.at[:, pl.ds(8, 8), :]),
                (TS.at[:, pl.ds(45, 3), :], TS.at[:, pl.ds(13, 3), :])],
        SOUTH: [(UV.at[every, pl.ds(16, 12), :], UV.at[every, pl.ds(48, 12), :]),
                (WE.at[:, pl.ds(16, 8), :], WE.at[:, pl.ds(48, 8), :]),
                (TS.at[:, pl.ds(16, 3), :], TS.at[:, pl.ds(48, 3), :])],
        EAST: [(PE.at[:, OWN, :], RW.at[:, OWN, :])],
        WEST: [(PW.at[:, OWN, :], RE.at[:, OWN, :])],
        NE: [(PE.at[:, pl.ds(36, 12), :], RW.at[:, pl.ds(4, 12), :])],
        SE: [(PE.at[:, pl.ds(16, 12), :], RW.at[:, pl.ds(48, 12), :])],
        NW: [(PW.at[:, pl.ds(36, 12), :], RE.at[:, pl.ds(4, 12), :])],
        SW: [(PW.at[:, pl.ds(16, 12), :], RE.at[:, pl.ds(48, 12), :])],
    }
    first_slot, slots = {}, 0
    for d in range(8):
        first_slot[d] = slots
        slots += len(parcels[d])

    def copies(d):
        return [
            pltpu.make_async_remote_copy(
                src_ref=src, dst_ref=dst, send_sem=send_sem.at[first_slot[d] + i], recv_sem=recv_sem.at[first_slot[d] + i],
                device_id=peers[d], device_id_type=MESH)
            for i, (src, dst) in enumerate(parcels[d])]

    def send_to_earlier(d, also=True):
        @pl.when(earlier[d] & also)
        def _():
            for copy in copies(d):
                copy.start()

    def send_to_later(d, also=True):
        @pl.when(later[d] & also)
        def _():
            pl.semaphore_wait(ready.at[d], 1)
            for copy in copies(d):
                copy.start()

    def wait_from(d):
        for copy in copies(d):
            copy.wait_recv()

    def extra(slot, src, dst, arrival, peer):
        return pltpu.make_async_remote_copy(
            src_ref=src, dst_ref=dst, send_sem=send_sem.at[slot], recv_sem=recv_sem.at[arrival],
            device_id=peer, device_id_type=MESH)

    to_hub = extra(slots, PW.at[:, pl.ds(36, 12), :], HUB.at[:, pl.ds(4, 12), :], slots, peers[NORTH])
    hub_west = extra(slots + 1, HUB.at[:, pl.ds(4, 12), :], RE.at[:, pl.ds(4, 12), :], first_slot[NW], peers[WEST])
    hub_south = extra(slots + 2, RW.at[:, pl.ds(16, 12), :], RW.at[:, pl.ds(48, 12), :], first_slot[SE], peers[SOUTH])

    @pl.when(expected > 0)
    def _():
        pl.semaphore_wait(barrier, expected)

    for d in range(8):
        @pl.when(earlier[d] & jnp.logical_not(corner_b) if d == NW else earlier[d])
        def _():
            pl.semaphore_signal(ready.at[DIRS.index((-DIRS[d][0], -DIRS[d][1]))], inc=1, device_id=peers[d], device_id_type=MESH)

    send_to_earlier(NW, corner_b)
    for d in (EAST, NE, SE, WEST, SW):
        send_to_earlier(d)
    send_to_earlier(NW, jnp.logical_not(corner_b))

    for first, face, planes in ((0, 1, UV), (4, 2, UV), (8, 0, TS), (12, 0, TS)):
        for k, plane in enumerate(wetted(first, face)):
            planes[first % 8 + k, OWN, :] = plane
    WE[0, OWN, :] = wet[0].astype(F32)
    WE[1, OWN, :] = raw2[...]

    for d in (NORTH, SOUTH):
        send_to_earlier(d)

    @pl.when(corner_b & west_relayed & earlier[NORTH])
    def _():
        to_hub.start()

    def flux_x(q_plane, u_plane, r0, n):
        flow = UV[u_plane, pl.ds(r0, n), :]
        flux = flow * upwind_value(flow, *x_parts(UV[q_plane, pl.ds(r0, n), :]))
        return flux - lanes(flux, 1)

    def flux_y(q_plane, v_plane, r0):
        flow = UV[v_plane, pl.ds(r0, 8), :]
        return flow * upwind_value(flow, *y_parts(UV, q_plane, r0, 8))

    def put_x(q_plane, u_plane, r0, n):
        TEND[q_plane, pl.ds(r0 - LO, n), :] = flux_x(q_plane, u_plane, r0, n)

    def put_y(q_plane, v_plane, r0):
        FY[q_plane, pl.ds(r0 - LO + 1, 8), :] = flux_y(q_plane, v_plane, r0)

    def combine(q_plane):
        for r0 in range(0, SPAN, 16):
            TEND[q_plane, pl.ds(r0, 16), :] = -(TEND[q_plane, pl.ds(r0, 16), :] + (
                FY[q_plane, pl.ds(r0 + 1, 16), :] - FY[q_plane, pl.ds(r0, 16), :]))

    def tracer_x(k, r0, n):
        q0, q1, gm2, gm1, g0, g1, g2 = x_parts(TS[k, pl.ds(PAD + r0, n), :])
        XU[k, pl.ds(r0, n), :] = q0 + correction(gm2, gm1, g0, g1)
        XD[k, pl.ds(r0, n), :] = q1 - correction(g2, g1, g0, gm1)

    def tracer_y(k, r0):
        q0, q1, gm2, gm1, g0, g1, g2 = y_parts(TS, k, PAD - 1 + r0, 8)
        YU[k, pl.ds(r0, 8), :] = q0 + correction(gm2, gm1, g0, g1)
        YD[k, pl.ds(r0, 8), :] = q1 - correction(g2, g1, g0, gm1)

    def local_part(k, carry):
        plane = lax.rem(k, LEVELS)
        for r0 in (16, 32):
            put_x(k, plane, r0, 16)
        for r0 in (23, 31):
            put_y(k, V_MAIN + plane, r0)
        for r0 in (0, 16):
            tracer_x(k, r0, 16)
        for r0 in (8, 16):
            tracer_y(k, r0)
        return carry

    lax.fori_loop(0, 8, local_part, 0)

    send_to_later(NORTH)

    @pl.when(corner_b & west_relayed & later[NORTH])
    def _():
        to_hub.start()

    send_to_later(EAST, inner_east)
    send_to_later(NE, inner_east)
    send_to_later(WEST, inner_west)
    send_to_later(NW, inner_west)
    send_to_later(SOUTH)
    send_to_later(SE, inner_east)
    send_to_later(SW, inner_west)
    for d in (EAST, NE, SE):
        send_to_later(d, last_column)

    for d in (NORTH, SOUTH):
        wait_from(d)

    zero16 = jnp.zeros((16, COLS), F32)

    @pl.when(lat == 0)
    def _():
        for k in range(8):
            UV[k, under, :] = zero16
            TS[k, under, :] = zero16
        WE[0, under, :] = zero16
        WE[1, under, :] = zero16

    @pl.when(lat == n_lat - 1)
    def _():
        for k in range(8):
            UV[k, over, :] = zero16
            TS[k, over, :] = zero16
        WE[0, over, :] = zero16
        WE[1, over, :] = zero16

    def edge_part(k, carry):
        plane = lax.rem(k, LEVELS)
        for r0 in (8, 48):
            put_x(k, plane, r0, 8)
        for r0 in (7, 15, 39, 47):
            put_y(k, V_MAIN + plane, r0)
        combine(k)
        for r0 in (0, 24, 32):
            tracer_y(k, r0)
        return carry

    lax.fori_loop(0, 8, edge_part, 0)

    lane64 = lax.broadcasted_iota(jnp.int32, (EXT, COLS), 1)
    half = lax.rem(lane64, 32) < 16
    lane = lax.broadcasted_iota(jnp.int32, (SPAN, COLS), 1)
    level = (lane // 32).astype(F32)
    BAND = pl.ds(LO, SPAN)
    LOWER = pl.ds(LO - 1, SPAN)
    ALL = pl.ds(0, SPAN)
    scale = STEP / SUB
    own = slice(PAD - LO, PAD - LO + ROWS)

    def band(x):
        return x[LO:LO + SPAN]

    def laid(main):
        return jnp.where(lane < 48, lanes(main, 16), lanes(main, -48))

    def faces(w):
        at = band(w)
        return jnp.minimum(at, lanes(at, -1)), jnp.minimum(at, band(rows(w, -1)))

    def main_sum(ref, first, where_rows, limit=None):
        total = None
        for k in range(LEVELS):
            term = ref[first + k, where_rows, :]
            if limit is not None:
                term = jnp.where(limit > k, term, 0.0)
            total = term if total is None else total + term
        return total

    def pair_sum(sw, se):
        low = lane < 64
        folded = jnp.where(low, sw, se) + lanes(jnp.where(low, se, sw), 64)
        return folded + lanes(folded, -32)

    def substeps(height, tx, ty, tym, fx, fy, cx, cy):
        for n in range(SUB):
            below = tym if n == 0 else rows(ty, 1)
            height = height - (tx - lanes(tx, 1) + (ty - below))
            tx = (tx + fx) - cx * (lanes(height, -1) - height)
            ty = (ty + fy) - cy * (rows(height, -1) - height)
        return height, tx, ty

    wx_main, wy_main = faces(WE[0])
    push_x = main_sum(TEND, U_MAIN, ALL, wx_main)
    push_y = main_sum(TEND, V_MAIN, ALL, wy_main)
    tx0 = main_sum(UV, U_MAIN, BAND)
    ty0 = main_sum(UV, V_MAIN, BAND)
    tym_main = main_sum(UV, V_MAIN, LOWER)
    h_main, tx_main, ty_main = substeps(
        WE[1, BAND, :], tx0, ty0, tym_main, scale * push_x, scale * push_y, WAVE * wx_main, WAVE * wy_main)
    gain_x = (tx_main - (tx0 + STEP * push_x)) / jnp.maximum(wx_main, 1.0)
    gain_y = (ty_main - (ty0 + STEP * push_y)) / jnp.maximum(wy_main, 1.0)
    for k in range(LEVELS):
        NU[k] = jnp.where(wx_main > k, UV[U_MAIN + k, BAND, :] + STEP * TEND[U_MAIN + k, ALL, :] + gain_x, 0.0)[own]
        NV[k] = jnp.where(wy_main > k, UV[V_MAIN + k, BAND, :] + STEP * TEND[V_MAIN + k, ALL, :] + gain_y, 0.0)
    KEPT[0] = h_main
    for slot, plane in enumerate((tx0, ty0, tym_main, push_x, push_y, wx_main, wy_main, WE[1, BAND, :])):
        KEPT[slot + 1] = laid(plane)
    RINGS[2] = ring([UV[U_MAIN + k] for k in range(LEVELS)])
    RINGS[3] = ring([UV[V_MAIN + k] for k in range(LEVELS)])
    RINGS[4] = ring([WE[0]] * LEVELS)

    def clear_poles(ref):
        @pl.when(lat == 0)
        def _():
            for i in range(2):
                ref[i, under, :] = zero16

        @pl.when(lat == n_lat - 1)
        def _():
            for i in range(2):
                ref[i, over, :] = zero16

    def strip(u_plane, v_plane):
        def one(i, carry):
            q_plane = u_plane + i * (v_plane - u_plane)
            for r0 in (8, 24, 40):
                put_x(q_plane, u_plane, r0, 16)
            for r0 in (7, 15, 23, 31, 39, 47):
                put_y(q_plane, v_plane, r0)
            combine(q_plane)
            return carry

        lax.fori_loop(0, 2, one, 0)

    def western_strip():
        for d in (NE, SE):
            wait_from(d)
        clear_poles(RW)
        UV[U_SW] = jnp.where(half, RW[0], RINGS[2])
        UV[V_SW] = jnp.where(half, lanes(RW[0], -16), RINGS[3])
        strip(U_SW, V_SW)

    def eastern_strip():
        for d in (WEST, NW, SW):
            wait_from(d)
        clear_poles(RE)
        UV[U_SE] = jnp.where(half, RINGS[2], lanes(RE[0], 16))
        UV[V_SE] = jnp.where(half, RINGS[3], RE[0])
        strip(U_SE, V_SE)

    for d in (NORTH, SOUTH):
        for copy in copies(d):
            copy.wait_send()

    @pl.when(first_column)
    def _():
        eastern_strip()

    for d in (WEST, NW, SW):
        send_to_later(d, first_column)

    @pl.when(corner_hub & west_relayed)
    def _():
        to_hub.wait_recv()
        hub_west.start()

    wait_from(EAST)

    @pl.when(corner_hub)
    def _():
        hub_south.start()

    western_strip()

    @pl.when(inner_west)
    def _():
        eastern_strip()

    in_sw, in_se = lane < 24, (lane >= 72) & (lane < 96)

    def kept(slot, sides):
        return jnp.where(in_sw | in_se, sides, KEPT[slot])

    wx_sw, wy_sw = faces(jnp.where(half, lanes(RW[1], -8), RINGS[4]))
    wx_se, wy_se = faces(jnp.where(half, RINGS[4], lanes(RE[1], -8)))
    wx_side = kept(6, jnp.where(lane < 64, wx_sw, wx_se))
    wy_side = kept(7, jnp.where(lane < 64, wy_sw, wy_se))
    eta_side = jnp.where(lane < 16, lanes(RW[1, BAND, :], 8), jnp.where(
        (lane >= 80) & (lane < 88), lanes(RE[1, BAND, :], 72), KEPT[8]))

    def masked(plane, limit):
        return jnp.where(limit > level, TEND[plane, ALL, :], 0.0)

    push_x_side = kept(4, pair_sum(masked(U_SW, wx_sw), masked(U_SE, wx_se)))
    push_y_side = kept(5, pair_sum(masked(V_SW, wy_sw), masked(V_SE, wy_se)))
    tx0_side = kept(1, pair_sum(UV[U_SW, BAND, :], UV[U_SE, BAND, :]))
    ty0_side = kept(2, pair_sum(UV[V_SW, BAND, :], UV[V_SE, BAND, :]))
    tym_side = kept(3, pair_sum(UV[V_SW, LOWER, :], UV[V_SE, LOWER, :]))

    h_side, tx_side, ty_side = substeps(
        eta_side, tx0_side, ty0_side, tym_side, scale * push_x_side, scale * push_y_side, WAVE * wx_side, WAVE * wy_side)

    result[16] = jnp.where(lane < 16, lanes(h_side, -16), jnp.where(lane >= 112, lanes(h_side, 48), KEPT[0]))[own]

    gain_x = (tx_side - (tx0_side + STEP * push_x_side)) / jnp.maximum(wx_side, 1.0)
    gain_y = (ty_side - (ty0_side + STEP * push_y_side)) / jnp.maximum(wy_side, 1.0)

    def fresh_side(plane, depth, gain):
        return jnp.where(depth > level, UV[plane, BAND, :] + STEP * TEND[plane, ALL, :] + gain, 0.0)

    u_sw = fresh_side(U_SW, wx_sw, spread(gain_x, 0))[own]
    u_se = fresh_side(U_SE, wx_se, spread(gain_x, 64))[own]
    v_sw = fresh_side(V_SW, wy_sw, spread(gain_y, 0))
    v_se = fresh_side(V_SE, wy_se, spread(gain_y, 64))

    for k in range(LEVELS):
        fresh = jnp.where(lane32 < 12, lanes(u_sw, -(32 * k + 16)), jnp.where(lane32 >= 116, lanes(u_se, 112 - 32 * k), NU[k]))
        NU[k] = fresh
        result[k] = fresh
        fresh = jnp.where(lane < 12, lanes(v_sw, -(32 * k + 16)), jnp.where(lane >= 116, lanes(v_se, 112 - 32 * k), NV[k]))
        NV[k] = fresh
        result[4 + k] = fresh[own]

    ring_t, ring_s = RINGS[0, pl.ds(0, ROWS), :], RINGS[1, pl.ds(0, ROWS), :]

    def side_flux(cells, flow):
        flux = flow * upwind_value(flow, *x_parts(cells))
        return flux - lanes(flux, 1)

    XS[0] = side_flux(jnp.where(half32, RW[1, OWN, :], ring_t), u_sw)
    XS[1] = side_flux(jnp.where(half32, ring_t, lanes(RE[1, OWN, :], 16)), u_se)
    XS[2] = side_flux(jnp.where(half32, lanes(RW[1, OWN, :], -16), ring_s), u_sw)
    XS[3] = side_flux(jnp.where(half32, ring_s, RE[1, OWN, :]), u_se)

    for field in range(2):
        for k in range(LEVELS):
            p = 4 * field + k
            flow = NU[k]
            flux = flow * jnp.where(flow >= 0.0, XU[p], XD[p])
            div_x = flux - lanes(flux, 1)
            div_x = jnp.where(lane32 < 8, lanes(XS[2 * field], -(32 * k + 16)),
                              jnp.where(lane32 >= 120, lanes(XS[2 * field + 1], 112 - 32 * k), div_x))
            up = NV[k, pl.ds(8, ROWS), :]
            down = NV[k, pl.ds(7, ROWS), :]
            flux_up = up * jnp.where(up >= 0.0, YU[p, pl.ds(1, ROWS), :], YD[p, pl.ds(1, ROWS), :])
            flux_down = down * jnp.where(down >= 0.0, YU[p, pl.ds(0, ROWS), :], YD[p, pl.ds(0, ROWS), :])
            cells = TS[p, OWN, :]
            fresh = cells - STEP * (div_x + (flux_up - flux_down))
            result[8 + p] = jnp.where(wet[0] > k, fresh, 0.0)

    for d in (EAST, WEST, NE, SE, NW, SW):
        if d in (SE, NW):
            @pl.when(earlier[d] | later[d])
            def _():
                for copy in copies(d):
                    copy.wait_send()
        else:
            for copy in copies(d):
                copy.wait_send()

    @pl.when(corner_hub)
    def _():
        hub_south.wait_send()

    @pl.when(corner_hub & west_relayed)
    def _():
        hub_west.wait_send()

    @pl.when(corner_b & west_relayed)
    def _():
        to_hub.wait_send()


def deal(result, u_out, v_out, t_out, s_out, e_out, sem):
    copies = [pltpu.make_async_copy(result.at[pl.ds(LEVELS * i, LEVELS)], out, sem.at[i])
              for i, out in enumerate((u_out, v_out, t_out, s_out))]
    copies.append(pltpu.make_async_copy(result.at[16], e_out, sem.at[4]))
    for copy in copies:
        copy.start()
    for copy in copies:
        copy.wait()


def solution(mesh):
    n_lat, n_lon = mesh.shape["lat"], mesh.shape["lon"]

    def step(u_vel, v_vel, temp, salt, eta, wet_levels):
        levels = jax.ShapeDtypeStruct((LEVELS, ROWS, COLS), F32)
        plane = jax.ShapeDtypeStruct((ROWS, COLS), F32)
        hbm = pl.BlockSpec(memory_space=pl.ANY)
        vmem = pl.BlockSpec(memory_space=pltpu.VMEM)

        def body(*refs):
            kernel(n_lat, n_lon, *refs)

        def buffer(*shape):
            return pltpu.VMEM(shape, F32)

        result = pl.pallas_call(
            body,
            out_shape=pltpu.VMEM((17, ROWS, COLS), F32),
            in_specs=[hbm] * 6,
            out_specs=vmem,
            scratch_shapes=[
                buffer(16, ROWS, COLS),
                buffer(ROWS, COLS),
                pltpu.VMEM((3, ROWS, COLS), jnp.int32),
                buffer(12, EXT, COLS),
                buffer(8, EXT, COLS),
                buffer(2, EXT, COLS),
                buffer(2, EXT, COLS),
                buffer(2, EXT, COLS),
                buffer(2, EXT, COLS),
                buffer(2, EXT, COLS),
                buffer(2, PAD, COLS),
                buffer(9, SPAN, COLS),
                buffer(5, EXT, COLS),
                buffer(12, SPAN, COLS),
                buffer(12, SPAN + 8, COLS),
                buffer(8, ROWS, COLS),
                buffer(8, ROWS, COLS),
                buffer(8, 40, COLS),
                buffer(8, 40, COLS),
                buffer(4, SPAN, COLS),
                buffer(4, ROWS, COLS),
                buffer(4, ROWS, COLS),
                pltpu.SemaphoreType.DMA((6,)),
                pltpu.SemaphoreType.REGULAR((8,)),
                pltpu.SemaphoreType.DMA((15,)),
                pltpu.SemaphoreType.DMA((15,)),
            ],
            compiler_params=pltpu.CompilerParams(collective_id=0, has_side_effects=True),
        )(u_vel, v_vel, temp, salt, eta, wet_levels)
        return pl.pallas_call(
            deal,
            out_shape=(levels, levels, levels, levels, plane),
            in_specs=[vmem],
            out_specs=(hbm,) * 5,
            scratch_shapes=[pltpu.SemaphoreType.DMA((5,))],
            compiler_params=pltpu.CompilerParams(vmem_limit_bytes=1 << 20),
        )(result)

    tile, flat = P(None, "lat", "lon"), P("lat", "lon")
    return jax.shard_map(
        step, mesh=mesh, in_specs=(tile, tile, tile, tile, flat, tile),
        out_specs=(tile, tile, tile, tile, flat), check_vma=False)
```
